128 devices in a mesh: grp: 8 (over y, x_lo), bal: 16 (over x_hi, z, core).
Axes of the slice: x: 4 (x_hi: 2, x_lo: 2; x = x_hi * 2 + x_lo), y: 4, z: 4, core: 2. Of those that a mesh axis runs over, the one named last changes fastest.
Arguments:
- events: bfloat16 [8, 8192, 512], P('grp', 'bal'), may hold values from -6 to 6
- cotangent: bfloat16 [8, 8192, 512], P('grp', 'bal'), may hold values from -6 to 6
- lengths: int32 [8, 16], P('grp'), may hold values from 1 to 16, as said below
- gain_in: float32 [512], replicated, may hold values from 0.1 to 1.9
- w_proj: bfloat16 [512, 2048], replicated, may hold values from -0.25 to 0.25
- gain_attn: float32 [512], replicated, may hold values from 0.1 to 1.9
- w_out: bfloat16 [512, 512], replicated, may hold values from -0.25 to 0.25
Outputs:
- d_x: bfloat16 [8, 8192, 512], P('grp', 'bal')
- grad_proj: float32 [512, 2048], replicated
- grad_out: float32 [512, 512], replicated
- grad_gain_in: float32 [512], replicated
- grad_gain_attn: float32 [512], replicated
The draws below stay inside these ranges and needn't reach their ends.
Inputs may be any that keep to these rules, and one draw needn't show every extreme that they name: A group's 16 lengths count blocks of 64 events and sum to 128; in every group one length equals 16.
All inputs are finite; a program needn't handle non-finite values.
Results may differ from the reference program's by a relative error of at most 0.013.
Values may be sent and summed in bfloat16 or wider, within the bound.
No kernel may reach another device: no remote copies, remote signals or barrier semaphores. Data moves between devices by JAX's collectives and lax.ppermute only.
A program may use at most 256 MiB of HBM per device.

```python
import jax
import jax.numpy as jnp
from jax import lax

D = 512
HEADS = 8
FF = 2048
BLOCK = 64
LEN_BLK = 16
PEERS = 16
GROUPS = 8
SEQ_GRP = 16
BLK_GRP = 128
ROWS_GRP = 8192
N_GRP = 8
N_BAL = 16


def group_lengths(key):
    others = SEQ_GRP - 1
    spare = BLK_GRP - SEQ_GRP - (LEN_BLK - 1)
    key_order, key_moves, key_long = jax.random.split(key, 3)
    base_extra = spare // others
    leftover = spare - base_extra * others
    shuffled = jax.random.permutation(key_order, others)
    extras = (base_extra + (shuffled < leftover).astype(jnp.int32)).astype(jnp.int32)
    rounds = 4 * others
    key_from, key_to, key_size = jax.random.split(key_moves, 3)
    givers = jax.random.randint(key_from, (rounds,), 0, others)
    takers = jax.random.randint(key_to, (rounds,), 0, others)
    amounts = jax.random.randint(key_size, (rounds,), 1, LEN_BLK)

    def transfer(turn, current):
        giver = givers[turn]
        taker = takers[turn]
        room_left = LEN_BLK - 1 - current[taker]
        moved = jnp.minimum(jnp.minimum(amounts[turn], current[giver]), room_left)
        moved = jnp.where(giver == taker, 0, moved)
        return current.at[giver].add(-moved).at[taker].add(moved)
    extras = lax.fori_loop(0, rounds, transfer, extras)
    long_place = jax.random.randint(key_long, (), 0, SEQ_GRP)
    positions = jnp.arange(SEQ_GRP, dtype=jnp.int32)
    shifted = jnp.clip(positions - (positions > long_place).astype(jnp.int32), 0, others - 1)
    picked = 1 + jnp.take(extras, shifted)
    return jnp.where(positions == long_place, LEN_BLK, picked).astype(jnp.int32)


def draw_lengths(key, part):
    group_keys = jax.random.split(jax.random.fold_in(key, 11), GROUPS)
    return jax.vmap(group_lengths)(group_keys)


def steps_of(rng, shape, shards, smallest, high):
    gain = 1.0
    for dim, parts in shards:
        draws = jax.random.uniform(jax.random.fold_in(jax.random.fold_in(rng, 6), dim), (parts,), jnp.float32, smallest / len(shards), high / len(shards))
        gain = gain * jnp.repeat(jnp.exp(draws), shape[dim] // parts).reshape((-1,) + (1,) * (len(shape) - 1 - dim))
    return gain


def gaussian(key, extent, scale, bound, cuts=(), kind=jnp.bfloat16):
    factor_of = steps_of(key, extent, cuts, -0.22, 0.18) if cuts else 1.0
    values = jax.random.normal(key, extent, jnp.float32) * scale * factor_of
    return jnp.minimum(jnp.maximum(values, -bound), bound).astype(kind)


def setup_inputs(seed: int = 0) -> dict:
    key_of = jax.random.split(jax.random.key(seed), 8)
    events = gaussian(key_of[0], (GROUPS, ROWS_GRP, D), 1.0, 6.0, ((0, 8), (1, 16)))
    cotangent = gaussian(key_of[1], (GROUPS, ROWS_GRP, D), 1.0, 6.0, ((0, 8), (1, 16)))
    lengths = draw_lengths(jax.random.fold_in(key_of[7], 71), 0)
    gain_in = jnp.clip(1.0 + 0.18 * jax.random.normal(key_of[3], (D,), jnp.float32), 0.1, 1.9)
    w_proj = gaussian(key_of[4], (D, FF), D ** -0.5, 0.25)
    gain_attn = jnp.clip(1.0 + 0.18 * jax.random.normal(key_of[5], (D,), jnp.float32), 0.1, 1.9)
    w_out = gaussian(key_of[6], (D, D), D ** -0.5, 0.25)
    return dict(events=events, cotangent=cotangent, lengths=lengths, gain_in=gain_in, w_proj=w_proj, gain_attn=gain_attn, w_out=w_out)


epsilon = 1e-06
query_rows = 256

def norm_rows(values):
    mean_value = lax.optimization_barrier(jnp.mean(values, axis=-1, keepdims=True))
    centred = values - mean_value
    rstd = lax.rsqrt(lax.optimization_barrier(jnp.mean(centred * centred, axis=-1, keepdims=True)) + epsilon)
    return (centred * rstd, rstd)

def silu_slope(values):
    sigma = jax.nn.sigmoid(values)
    return sigma * (1.0 + values * (1.0 - sigma))

def norm_back(grad, normed, rstd):
    return rstd * (grad - lax.optimization_barrier(jnp.mean(grad, axis=-1, keepdims=True)) - normed * lax.optimization_barrier(jnp.mean(grad * normed, axis=-1, keepdims=True)))

def contract_rows(left, right):
    return lax.dot_general(left, right, (((0,), (0,)), ((), ())), preferred_element_type=jnp.float32)

def contract_cols(left, right):
    return lax.dot_general(left, right, (((1,), (1,)), ((), ())), preferred_element_type=jnp.float32)

def project_rows(rows, gain_in, w_proj):
    normed, rstd_in = norm_rows(rows.astype(jnp.float32))
    scaled = (normed * gain_in).astype(jnp.bfloat16)
    hidden = jnp.dot(scaled, w_proj, preferred_element_type=jnp.float32)
    active = jax.nn.silu(hidden).astype(jnp.bfloat16)
    return (normed, rstd_in, scaled, hidden, active)

def output_rows(attn, upper, grads_out, gain_attn, w_out):
    normed, rstd = norm_rows(attn.astype(jnp.float32))
    upper_wide = upper.astype(jnp.float32)
    mixed = (normed * gain_attn * upper_wide).astype(jnp.bfloat16)
    d_mixed = contract_cols(grads_out, w_out)
    d_upper = d_mixed * normed * gain_attn
    d_attn = norm_back(d_mixed * gain_attn * upper_wide, normed, rstd).astype(jnp.bfloat16)
    out_term = contract_rows(mixed, grads_out)
    gain_term = lax.optimization_barrier(jnp.sum(d_mixed * normed * upper_wide, axis=0))
    return (d_upper, d_attn, out_term, gain_term)

def input_rows(grads_out, d_act, hidden, normed, rstd_in, scaled, gain_in, w_proj):
    d_hidden = (d_act * silu_slope(hidden)).astype(jnp.bfloat16)
    proj_term = contract_rows(scaled, d_hidden)
    d_scaled = contract_cols(d_hidden, w_proj)
    d_rows = (grads_out.astype(jnp.float32) + norm_back(d_scaled * gain_in, normed, rstd_in)).astype(jnp.bfloat16)
    gain_term = lax.optimization_barrier(jnp.sum(d_scaled * normed, axis=0))
    return (d_rows, proj_term, gain_term)

def event_order(array):
    blocks = array.reshape(PEERS, -1, BLOCK, array.shape[-1])
    return jnp.transpose(blocks, (1, 0, 2, 3)).reshape(-1, array.shape[-1])

def device_order(array):
    blocks = array.reshape(-1, PEERS, BLOCK, array.shape[-1])
    return jnp.transpose(blocks, (1, 0, 2, 3)).reshape(-1, array.shape[-1])

def add_window(total, part, start):
    current = lax.dynamic_slice_in_dim(total, start, part.shape[0], 0)
    return lax.dynamic_update_slice_in_dim(total, current + part, start, 0)

def group_grads(rows, grads_out, seq_lengths, gain_in, w_proj, gain_attn, w_out):
    total_rows = rows.shape[0]
    width = rows.shape[1]
    head_width = width // HEADS
    scale = head_width ** (-0.5)
    span = LEN_BLK * BLOCK
    window = span + query_rows
    ends = (jnp.cumsum(seq_lengths) * BLOCK).astype(jnp.int32)
    positions = jnp.arange(total_rows, dtype=jnp.int32)
    row_seq = lax.optimization_barrier(jnp.sum((ends[None, :] <= positions[:, None]).astype(jnp.int32), axis=1)).astype(jnp.int32)
    normed, rstd_in, scaled, hidden, active = project_rows(rows, gain_in, w_proj)
    upper = active[:, :width]
    values = active[:, width:2 * width]
    query = active[:, 2 * width:3 * width]
    keys = active[:, 3 * width:]
    front = jnp.zeros((span, width), jnp.bfloat16)
    keys_pad = jnp.concatenate([front, keys], axis=0)
    values_pad = jnp.concatenate([front, values], axis=0)
    seq_pad = jnp.concatenate([jnp.full((span,), -1, jnp.int32), row_seq], axis=0)

    def block_step(carry, start):
        grad_keys, grad_values, out_sum, gain_sum = carry
        query_block = lax.dynamic_slice_in_dim(query, start, query_rows, 0)
        upper_block = lax.dynamic_slice_in_dim(upper, start, query_rows, 0)
        grads_block = lax.dynamic_slice_in_dim(grads_out, start, query_rows, 0)
        seq_query = lax.dynamic_slice_in_dim(row_seq, start, query_rows, 0)
        key_window = lax.dynamic_slice_in_dim(keys_pad, start, window, 0)
        value_window = lax.dynamic_slice_in_dim(values_pad, start, window, 0)
        seq_key = lax.dynamic_slice_in_dim(seq_pad, start, window, 0)
        place_query = start + jnp.arange(query_rows, dtype=jnp.int32)
        place_key = start - span + jnp.arange(window, dtype=jnp.int32)
        allowed = ((seq_query[:, None] == seq_key[None, :]) & (place_key[None, :] <= place_query[:, None])).astype(jnp.float32)
        query_heads = query_block.astype(jnp.float32).reshape(query_rows, HEADS, head_width)
        key_heads = key_window.astype(jnp.float32).reshape(window, HEADS, head_width)
        value_heads = value_window.astype(jnp.float32).reshape(window, HEADS, head_width)
        scores = jnp.einsum('qhd,khd->hqk', query_heads, key_heads) * scale
        weights = (jax.nn.silu(scores) * allowed[None]).astype(jnp.bfloat16)
        attn = jnp.einsum('hqk,khd->qhd', weights.astype(jnp.float32), value_heads).reshape(query_rows, width).astype(jnp.bfloat16)
        d_upper, d_attn, out_term, gain_term = output_rows(attn, upper_block, grads_block, gain_attn, w_out)
        grad_heads = d_attn.astype(jnp.float32).reshape(query_rows, HEADS, head_width)
        grad_weights = jnp.einsum('qhd,khd->hqk', grad_heads, value_heads)
        grad_scores = (grad_weights * silu_slope(scores) * allowed[None]).astype(jnp.bfloat16)
        grad_query = (jnp.einsum('hqk,khd->qhd', grad_scores.astype(jnp.float32), key_heads).reshape(query_rows, width) * scale).astype(jnp.bfloat16)
        part_values = jnp.einsum('hqk,qhd->khd', weights.astype(jnp.float32), grad_heads).reshape(window, width)
        part_keys = jnp.einsum('hqk,qhd->khd', grad_scores.astype(jnp.float32), query_heads).reshape(window, width) * scale
        grad_values = add_window(grad_values, part_values, start)
        grad_keys = add_window(grad_keys, part_keys, start)
        return ((grad_keys, grad_values, out_sum + out_term, gain_sum + gain_term), (d_upper, grad_query))
    starts = jnp.arange(0, total_rows, query_rows, dtype=jnp.int32)
    empty_rows = jnp.zeros((span + total_rows, width), jnp.float32)
    initial = (empty_rows, empty_rows, jnp.zeros((width, width), jnp.float32), jnp.zeros((width,), jnp.float32))
    carry, stacked = lax.scan(block_step, initial, starts)
    grad_keys, grad_values, out_sum, gain_attn_sum = carry
    d_keys = grad_keys[span:].astype(jnp.bfloat16)
    d_values = grad_values[span:].astype(jnp.bfloat16)
    d_upper = stacked[0].reshape(total_rows, width)
    d_query = stacked[1].reshape(total_rows, width)
    d_act = jnp.concatenate([d_upper, d_values.astype(jnp.float32), d_query.astype(jnp.float32), d_keys.astype(jnp.float32)], axis=1)
    d_rows, proj_term, gain_in_term = input_rows(grads_out, d_act, hidden, normed, rstd_in, scaled, gain_in, w_proj)
    return (d_rows, (proj_term, out_sum, gain_in_term, gain_attn_sum))

def reference(events, cotangent, lengths, gain_in, w_proj, gain_attn, w_out):

    def one_group(item):
        rows, grads, seq_lengths = item
        d_rows, terms = group_grads(event_order(rows), event_order(grads), seq_lengths, gain_in, w_proj, gain_attn, w_out)
        return (device_order(d_rows), terms)
    d_x, terms = lax.map(one_group, (events, cotangent, lengths))
    divisor = N_GRP * N_BAL
    grad_proj = lax.optimization_barrier(jnp.sum(terms[0], axis=0)) / divisor
    grad_out = lax.optimization_barrier(jnp.sum(terms[1], axis=0)) / divisor
    grad_gain_in = lax.optimization_barrier(jnp.sum(terms[2], axis=0)) / divisor
    grad_gain_attn = lax.optimization_barrier(jnp.sum(terms[3], axis=0)) / divisor
    return (d_x, grad_proj, grad_out, grad_gain_in, grad_gain_attn)
```

```python
import jax
import jax.numpy as jnp
from jax import lax
from jax.experimental import pallas as pl
from jax.experimental.pallas import tpu as pltpu
from jax.sharding import Mesh, PartitionSpec as P

D = 512
HEADS = 8
BLOCK = 64
LEN_BLK = 16
SEQ = 16
PEERS = 16
LOCAL = 8
TILE = 256
TILES = 4
ROWS = 1024
LANES = 128
PAIRS = 4
PART = 88
HALF = 64 * PART
EPS = 1e-06
DEVICES = 128
BF = jnp.bfloat16
F32 = jnp.float32
VMEM_LIMIT = 56 * 1024 * 1024

SMEM_SPEC = pl.BlockSpec(memory_space=pltpu.SMEM)
ANY_SPEC = pl.BlockSpec(memory_space=pl.ANY)
VMEM_SPEC = pl.BlockSpec(memory_space=pltpu.VMEM)


def dot(left, right):
    return lax.dot_general(left, right, (((1,), (0,)), ((), ())), preferred_element_type=F32)


def dot_cols(left, right):
    return lax.dot_general(left, right, (((1,), (1,)), ((), ())), preferred_element_type=F32)


def dot_rows(left, right):
    return lax.dot_general(left, right, (((0,), (0,)), ((), ())), preferred_element_type=F32)


def packing(len_ref):
    starts, sizes, ranks = [], [], []
    start = jnp.int32(0)
    rank = jnp.int32(0)
    held = jnp.int32(0)
    for i in range(SEQ):
        size = len_ref[i]
        fresh = held + size > LEN_BLK
        rank = jnp.where(fresh, rank + 1, rank)
        held = jnp.where(fresh, size, held + size)
        starts.append(start)
        sizes.append(size)
        ranks.append(rank)
        start = start + size
    return starts, sizes, ranks


def owners(len_ref, own):
    starts, _, ranks = packing(len_ref)
    found = []
    for k in range(LOCAL):
        block = own + PEERS * k
        owner = ranks[0]
        for i in range(1, SEQ):
            owner = jnp.where(starts[i] <= block, ranks[i], owner)
        found.append(owner)
    return found


def holdings(len_ref, own):
    starts, sizes, ranks = packing(len_ref)
    first = jnp.int32(LEN_BLK * LOCAL)
    count = jnp.int32(0)
    for i in range(SEQ):
        mine = ranks[i] == own
        first = jnp.where(mine, jnp.minimum(first, starts[i]), first)
        count = jnp.where(mine, count + sizes[i], count)
    return starts, sizes, ranks, first, count


def history_starts(hist_ref, own, starts, sizes, ranks, first):
    for j in range(LEN_BLK):
        hist_ref[j] = j
    for i in range(SEQ):

        @pl.when(ranks[i] == own)
        def _(i=i):
            begin = starts[i] - first

            def put(j, carry):
                hist_ref[j] = begin
                return carry

            lax.fori_loop(begin, begin + sizes[i], put, 0)


def send_kernel(len_ref, own_ref, rows_ref, grads_ref, rows_out, grads_out, sems):
    owner = owners(len_ref, own_ref[0])
    copies = []
    for n, (src, dst) in enumerate(((rows_ref, rows_out), (grads_ref, grads_out))):
        for k in range(LOCAL):
            copies.append(pltpu.make_async_copy(src.at[k], dst.at[owner[k]], sems.at[n, k]))
    for copy in copies:
        copy.start()
    for copy in copies:
        copy.wait()


def home_kernel(len_ref, own_ref, back_ref, out_ref, sems):
    owner = owners(len_ref, own_ref[0])
    copies = [
        pltpu.make_async_copy(back_ref.at[owner[k]], out_ref.at[k], sems.at[k])
        for k in range(LOCAL)
    ]
    for copy in copies:
        copy.start()
    for copy in copies:
        copy.wait()


def fetch(src_ref, dst_ref, sems, first, count):
    for j in range(LEN_BLK):

        @pl.when(j < count)
        def _(j=j):
            slot = (first + j) & (PEERS - 1)
            pltpu.make_async_copy(src_ref.at[slot], dst_ref.at[j], sems.at[j]).start()


def arrive(src_ref, dst_ref, sems, count):
    for j in range(LEN_BLK):

        @pl.when(j < count)
        def _(j=j):
            pltpu.make_async_copy(src_ref.at[0], dst_ref.at[j], sems.at[j]).wait()


def tile_rows(ref, t, count):
    tile = ref[pl.ds(t * 4, 4)].reshape(TILE, D).astype(F32)
    place = lax.broadcasted_iota(jnp.int32, (TILE, D), 0) + t * TILE
    return jnp.where(place < count * BLOCK, tile, 0.0)


def normed_rows(values):
    centred = values - jnp.mean(values, axis=-1, keepdims=True)
    rstd = lax.rsqrt(jnp.mean(centred * centred, axis=-1, keepdims=True) + EPS)
    return centred * rstd, rstd


def head_masks():
    lane = lax.broadcasted_iota(jnp.int32, (1, LANES), 1)
    low = (lane < 64).astype(F32).astype(BF)
    high = (lane >= 64).astype(F32).astype(BF)
    return low, high


def rows_at(t):
    return pl.ds(pl.multiple_of(t * TILE, TILE), TILE)


def block_starts(hist_ref, t, shape, dim):
    place = lax.broadcasted_iota(jnp.int32, shape, dim)
    begin = jnp.full(shape, hist_ref[4 * t], jnp.int32)
    for b in range(1, 4):
        begin = jnp.where(place >= b * BLOCK, hist_ref[4 * t + b], begin)
    return begin * BLOCK


def key_tiles(hist_ref, i):
    low = hist_ref[4 * i] // 4
    clear = jnp.minimum((hist_ref[4 * i + 3] + 3) // 4, i)
    return low, jnp.maximum(clear, low)


def forward_kernel(
    len_ref,
    own_ref,
    got_ref,
    w_ref,
    gain_ref,
    upper_ref,
    values_ref,
    query_ref,
    keys_ref,
    slope_ref,
    attn_ref,
    scaled_ref,
    rows_ref,
    acc_ref,
    hist_ref,
    sems,
):
    own = own_ref[0]
    starts, sizes, ranks, first, count = holdings(len_ref, own)
    fetch(got_ref, rows_ref, sems, first, count)
    history_starts(hist_ref, own, starts, sizes, ranks, first)
    live = (count + 3) // 4
    arrive(got_ref, rows_ref, sems, count)

    def project(t, carry):
        normed, _ = normed_rows(tile_rows(rows_ref, t, count))
        scaled = (normed * gain_ref[...]).astype(BF)
        rows = rows_at(t)
        scaled_ref[rows, :] = scaled
        for quarter in range(4):
            half = 0.5 * dot(scaled, w_ref[:, quarter * D : (quarter + 1) * D])
            swing = jnp.tanh(half)
            active = half + half * swing
            slope = ((0.5 + 0.5 * swing) * (1.0 + (half - half * swing))).astype(BF)
            if quarter == 0:
                upper_ref[rows, :] = active.astype(BF)
            if quarter == 2:
                active = active * 0.0625
            active = active.astype(BF)
            for p in range(PAIRS):
                lanes = slice(p * LANES, (p + 1) * LANES)
                slope_ref[quarter * PAIRS + p, rows, :] = slope[:, lanes]
                if quarter:
                    ref = (None, values_ref, query_ref, keys_ref)[quarter]
                    ref[p, rows, :] = active[:, lanes]
        return carry

    lax.fori_loop(0, live, project, 0)

    def clear(t, carry):
        scaled_ref[rows_at(t), :] = jnp.zeros((TILE, D), BF)
        return carry

    lax.fori_loop(live, TILES, clear, 0)

    masks = head_masks()

    def pair(p, carry):
        def query_tile(i, carry):
            query = query_ref[p, rows_at(i), :]
            acc_ref[...] = jnp.zeros((TILE, LANES), F32)

            def step(j, masked):
                keys = keys_ref[p, rows_at(j), :]
                values = values_ref[p, rows_at(j), :]
                if masked:
                    shape = (TILE, TILE)
                    col = lax.broadcasted_iota(jnp.int32, shape, 1) + j * TILE
                    row = lax.broadcasted_iota(jnp.int32, shape, 0) + i * TILE
                    allowed = (col <= row) & (col >= block_starts(hist_ref, i, shape, 0))
                total = acc_ref[...]
                for mask in masks:
                    half = dot_cols(query, keys * mask)
                    weights = half + half * jnp.tanh(half)
                    if masked:
                        weights = jnp.where(allowed, weights, 0.0)
                    total += dot(weights.astype(BF), values * mask)
                acc_ref[...] = total

            low, clear_from = key_tiles(hist_ref, i)

            def masked_step(j, carry):
                step(j, True)
                return carry

            def clear_step(j, carry):
                step(j, False)
                return carry

            lax.fori_loop(low, clear_from, masked_step, 0)
            lax.fori_loop(clear_from, i, clear_step, 0)
            step(i, True)
            attn_ref[p, rows_at(i), :] = acc_ref[...].astype(BF)
            return carry

        return lax.fori_loop(0, live, query_tile, carry)

    lax.fori_loop(0, PAIRS, pair, 0)


def backward_kernel(
    len_ref,
    own_ref,
    got_ref,
    grads_ref,
    upper_ref,
    values_ref,
    query_ref,
    keys_ref,
    slope_ref,
    attn_ref,
    scaled_ref,
    w_ref,
    w_out_ref,
    gain_in_ref,
    gain_attn_ref,
    back_ref,
    terms_ref,
    rows_ref,
    cot_ref,
    d_attn_ref,
    d_hidden_ref,
    out_ref,
    gains_ref,
    d_query_ref,
    d_keys_ref,
    d_values_ref,
    hist_ref,
    row_sems,
    cot_sems,
):
    own = own_ref[0]
    core = own & 1
    starts, sizes, ranks, first, count = holdings(len_ref, own)
    fetch(grads_ref, cot_ref, cot_sems, first, count)
    fetch(got_ref, rows_ref, row_sems, first, count)
    history_starts(hist_ref, own, starts, sizes, ranks, first)
    live = (count + 3) // 4
    out_ref[...] = jnp.zeros((D, D), F32)
    gains_ref[...] = jnp.zeros((2, D), F32)
    arrive(grads_ref, cot_ref, cot_sems, count)

    def middle(t, carry):
        rows = rows_at(t)
        attn = jnp.concatenate([attn_ref[p, rows, :] for p in range(PAIRS)], axis=1)
        normed, rstd = normed_rows(attn.astype(F32))
        upper = upper_ref[rows, :].astype(F32)
        cot = tile_rows(cot_ref, t, count).astype(BF)
        d_mixed = dot_cols(cot, w_out_ref[...])
        gained = normed * gain_attn_ref[...]
        out_ref[...] += dot_rows((gained * upper).astype(BF), cot)
        d_upper = d_mixed * gained
        pull = d_mixed * upper
        gains_ref[1:2, :] += jnp.sum(pull * normed, axis=0, keepdims=True)
        pull = pull * gain_attn_ref[...]
        d_attn = rstd * (
            pull
            - jnp.mean(pull, axis=-1, keepdims=True)
            - normed * jnp.mean(pull * normed, axis=-1, keepdims=True)
        )
        for p in range(PAIRS):
            lanes = slice(p * LANES, (p + 1) * LANES)
            d_attn_ref[p, rows, :] = d_attn[:, lanes].astype(BF)
            slope = slope_ref[p, rows, :].astype(F32)
            d_hidden_ref[p, rows, :] = (d_upper[:, lanes] * slope).astype(BF)
        return carry

    lax.fori_loop(0, live, middle, 0)

    def clear(t, carry):
        d_hidden_ref[:, rows_at(t), :] = jnp.zeros((4 * PAIRS, TILE, LANES), BF)
        return carry

    lax.fori_loop(live, TILES, clear, 0)

    masks = head_masks()

    def pair(p, carry):
        d_keys_ref[...] = jnp.zeros((ROWS, LANES), F32)
        d_values_ref[...] = jnp.zeros((ROWS, LANES), F32)

        def query_tile(i, carry):
            query = query_ref[p, rows_at(i), :]
            d_attn = d_attn_ref[p, rows_at(i), :]
            d_query_ref[...] = jnp.zeros((TILE, LANES), F32)

            def step(j, masked):
                rows = rows_at(j)
                keys = keys_ref[p, rows, :]
                values = values_ref[p, rows, :]
                if masked:
                    shape = (TILE, TILE)
                    key_row = lax.broadcasted_iota(jnp.int32, shape, 0) + j * TILE
                    query_row = lax.broadcasted_iota(jnp.int32, shape, 1) + i * TILE
                    allowed = (key_row <= query_row) & (
                        key_row >= block_starts(hist_ref, i, shape, 1)
                    )
                d_query = d_query_ref[...]
                d_keys = d_keys_ref[rows, :]
                d_values = d_values_ref[rows, :]
                for mask in masks:
                    masked_keys = keys * mask
                    half = dot_cols(masked_keys, query)
                    swing = jnp.tanh(half)
                    bend = half * swing
                    weights = half + bend
                    slope = (1.0 + swing) * ((1.0 + half) - bend)
                    grad = dot_cols(values * mask, d_attn) * slope
                    if masked:
                        weights = jnp.where(allowed, weights, 0.0)
                        grad = jnp.where(allowed, grad, 0.0)
                    grad = grad.astype(BF)
                    d_values += dot(weights.astype(BF), d_attn * mask)
                    d_keys += dot(grad, query * mask)
                    d_query += dot_rows(grad, masked_keys)
                d_query_ref[...] = d_query
                d_keys_ref[rows, :] = d_keys
                d_values_ref[rows, :] = d_values

            low, clear_from = key_tiles(hist_ref, i)

            def masked_step(j, carry):
                step(j, True)
                return carry

            def clear_step(j, carry):
                step(j, False)
                return carry

            lax.fori_loop(low, clear_from, masked_step, 0)
            lax.fori_loop(clear_from, i, clear_step, 0)
            step(i, True)
            slope = slope_ref[2 * PAIRS + p, rows_at(i), :].astype(F32)
            d_hidden_ref[2 * PAIRS + p, rows_at(i), :] = (
                d_query_ref[...] * 0.0625 * slope
            ).astype(BF)
            return carry

        lax.fori_loop(0, live, query_tile, 0)

        def finish(t, carry):
            rows = rows_at(t)
            for place, ref in ((1, d_values_ref), (3, d_keys_ref)):
                slope = slope_ref[place * PAIRS + p, rows, :].astype(F32)
                d_hidden_ref[place * PAIRS + p, rows, :] = (ref[rows, :] * slope).astype(BF)
            return carry

        lax.fori_loop(0, live, finish, 0)
        return carry

    lax.fori_loop(0, PAIRS, pair, 0)

    arrive(got_ref, rows_ref, row_sems, count)

    def final(t, carry):
        rows = rows_at(t)
        normed, rstd = normed_rows(tile_rows(rows_ref, t, count))
        d_scaled = jnp.zeros((TILE, D), F32)
        for c in range(8):
            part = jnp.concatenate(
                [d_hidden_ref[2 * c, rows, :], d_hidden_ref[2 * c + 1, rows, :]], axis=1
            )
            d_scaled += dot_cols(part, w_ref[:, c * 256 : (c + 1) * 256])
        gains_ref[0:1, :] += jnp.sum(d_scaled * normed, axis=0, keepdims=True)
        pull = d_scaled * gain_in_ref[...]
        d_rows = rstd * (
            pull
            - jnp.mean(pull, axis=-1, keepdims=True)
            - normed * jnp.mean(pull * normed, axis=-1, keepdims=True)
        )
        d_rows = (d_rows + tile_rows(cot_ref, t, count)).astype(BF)
        for b in range(4):
            slot = (first + t * 4 + b) & (PEERS - 1)
            back_ref[slot] = d_rows[b * BLOCK : (b + 1) * BLOCK, :]
        return carry

    lax.fori_loop(0, live, final, 0)

    def put(piece, values):
        half, place = divmod(piece, 10)
        terms_ref[half ^ core, place * D : (place + 1) * D, :] = values.astype(BF)

    for c in range(8):
        part = jnp.concatenate([d_hidden_ref[2 * c], d_hidden_ref[2 * c + 1]], axis=1)
        term = dot_rows(scaled_ref[...], part)
        put(2 * c, term[:, :LANES])
        put(2 * c + 1, term[:, LANES:])
    for p in range(PAIRS):
        put(16 + p, out_ref[:, p * LANES : (p + 1) * LANES])
    for half in range(2):
        terms_ref[half ^ core, 10 * D :, :] = jnp.concatenate(
            [gains_ref[half : half + 1, p * LANES : (p + 1) * LANES] for p in range(PAIRS)]
            + [jnp.zeros((HALF - 10 * D - PAIRS, LANES), F32)],
            axis=0,
        ).astype(BF)


def spread_kernel(own_ref, mine_ref, other_ref, proj_ref, out_ref, gain_in_ref, gain_attn_ref):
    core = own_ref[0] & 1

    def write(low_ref, high_ref):
        for piece in range(20):
            half, place = divmod(piece, 10)
            part = (low_ref, high_ref)[half][place * D : (place + 1) * D, :].astype(F32)
            if piece < 16:
                proj_ref[:, piece * LANES : (piece + 1) * LANES] = part
            else:
                out_ref[:, (piece - 16) * LANES : (piece - 15) * LANES] = part
        gain_in_ref[...] = low_ref[10 * D : 10 * D + 16, :].astype(F32)[:PAIRS]
        gain_attn_ref[...] = high_ref[10 * D : 10 * D + 16, :].astype(F32)[:PAIRS]

    @pl.when(core == 0)
    def _():
        write(mine_ref, other_ref)

    @pl.when(core == 1)
    def _():
        write(other_ref, mine_ref)


def struct(shape, dtype):
    return jax.ShapeDtypeStruct(shape, dtype)


def params():
    return pltpu.CompilerParams(vmem_limit_bytes=VMEM_LIMIT)


def per_device(events, cotangent, lengths, gain_in, w_proj, gain_attn, w_out):
    own = lax.axis_index(("chip", "core")).astype(jnp.int32).reshape(1)
    lens = lengths[0]
    blocks = struct((PEERS, BLOCK, D), BF)
    send_rows, send_grads = pl.pallas_call(
        send_kernel,
        out_shape=(blocks, blocks),
        in_specs=[SMEM_SPEC, SMEM_SPEC, ANY_SPEC, ANY_SPEC],
        out_specs=(ANY_SPEC, ANY_SPEC),
        scratch_shapes=[pltpu.SemaphoreType.DMA((2, LOCAL))],
        name="send_blocks",
    )(lens, own, events.reshape(LOCAL, BLOCK, D), cotangent.reshape(LOCAL, BLOCK, D))
    got_rows = lax.all_to_all(send_rows, ("chip", "core"), 0, 0, tiled=True)
    got_grads = lax.all_to_all(send_grads, ("chip", "core"), 0, 0, tiled=True)
    pairs = struct((PAIRS, ROWS, LANES), BF)
    wide = struct((ROWS, D), BF)
    saved = pl.pallas_call(
        forward_kernel,
        out_shape=(
            wide,
            pairs,
            pairs,
            pairs,
            struct((4 * PAIRS, ROWS, LANES), BF),
            pairs,
            wide,
        ),
        in_specs=[SMEM_SPEC, SMEM_SPEC, ANY_SPEC, VMEM_SPEC, VMEM_SPEC],
        out_specs=(VMEM_SPEC,) * 7,
        scratch_shapes=[
            pltpu.VMEM((LEN_BLK, BLOCK, D), BF),
            pltpu.VMEM((TILE, LANES), F32),
            pltpu.SMEM((LEN_BLK,), jnp.int32),
            pltpu.SemaphoreType.DMA((LEN_BLK,)),
        ],
        compiler_params=params(),
        name="forward_layer",
    )(lens, own, got_rows, w_proj, gain_in.reshape(1, D))
    send_back, terms = pl.pallas_call(
        backward_kernel,
        out_shape=(blocks, struct((2, HALF, LANES), BF)),
        in_specs=[SMEM_SPEC, SMEM_SPEC, ANY_SPEC, ANY_SPEC] + [VMEM_SPEC] * 11,
        out_specs=(VMEM_SPEC, VMEM_SPEC),
        scratch_shapes=[
            pltpu.VMEM((LEN_BLK, BLOCK, D), BF),
            pltpu.VMEM((LEN_BLK, BLOCK, D), BF),
            pltpu.VMEM((PAIRS, ROWS, LANES), BF),
            pltpu.VMEM((4 * PAIRS, ROWS, LANES), BF),
            pltpu.VMEM((D, D), F32),
            pltpu.VMEM((2, D), F32),
            pltpu.VMEM((TILE, LANES), F32),
            pltpu.VMEM((ROWS, LANES), F32),
            pltpu.VMEM((ROWS, LANES), F32),
            pltpu.SMEM((LEN_BLK,), jnp.int32),
            pltpu.SemaphoreType.DMA((LEN_BLK,)),
            pltpu.SemaphoreType.DMA((LEN_BLK,)),
        ],
        compiler_params=params(),
        name="backward_layer",
    )(
        lens,
        own,
        got_rows,
        got_grads,
        *saved,
        w_proj,
        w_out,
        gain_in.reshape(1, D),
        gain_attn.reshape(1, D),
    )
    swap = [(0, 1), (1, 0)]
    other = lax.ppermute(terms[1], "core", swap)
    chip_sum = (terms[0].astype(F32) + other.astype(F32)).astype(BF)
    parts = lax.all_to_all(chip_sum.reshape(64, PART, LANES), ("grp", "chip"), 0, 0, tiled=True)
    total = (jnp.sum(parts.astype(F32), axis=0) * (1.0 / DEVICES)).astype(BF)
    copies = jnp.broadcast_to(total[None], (64, PART, LANES))
    mine = lax.all_to_all(copies, ("grp", "chip"), 0, 0, tiled=True).reshape(HALF, LANES)
    others = lax.ppermute(mine, "core", swap)
    came_back = lax.all_to_all(send_back, ("chip", "core"), 0, 0, tiled=True)
    d_rows = pl.pallas_call(
        home_kernel,
        out_shape=struct((LOCAL, BLOCK, D), BF),
        in_specs=[SMEM_SPEC, SMEM_SPEC, ANY_SPEC],
        out_specs=ANY_SPEC,
        scratch_shapes=[pltpu.SemaphoreType.DMA((LOCAL,))],
        name="take_home",
    )(lens, own, came_back)
    gain = struct((PAIRS, LANES), F32)
    grad_proj, grad_out, grad_in, grad_attn = pl.pallas_call(
        spread_kernel,
        out_shape=(struct((D, 4 * D), F32), struct((D, D), F32), gain, gain),
        in_specs=[SMEM_SPEC, VMEM_SPEC, VMEM_SPEC],
        out_specs=(VMEM_SPEC,) * 4,
        compiler_params=params(),
        name="spread_grads",
    )(own, mine, others)
    return (
        d_rows.reshape(1, LOCAL * BLOCK, D),
        grad_proj,
        grad_out,
        grad_in.reshape(D),
        grad_attn.reshape(D),
    )


def solution(mesh):
    fine = Mesh(mesh.devices.reshape(8, 8, 2), ("grp", "chip", "core"))
    rows = P("grp", ("chip", "core"), None)
    return jax.shard_map(
        per_device,
        mesh=fine,
        in_specs=(rows, rows, P("grp", None), P(), P(), P(), P()),
        out_specs=(rows, P(), P(), P(), P()),
        check_vma=False,
    )
```

```python
import jax
import jax.numpy as jnp
from jax import lax
from jax.experimental import pallas as pl
from jax.experimental.pallas import tpu as pltpu
from jax.sharding import Mesh, PartitionSpec as P

D = 512
HEADS = 8
BLOCK = 64
LEN_BLK = 16
SEQ = 16
PEERS = 16
LOCAL = 8
TILE = 256
TILES = 4
ROWS = 1024
LANES = 128
PAIRS = 4
PART = 88
HALF = 64 * PART
EPS = 1e-06
DEVICES = 128
BF = jnp.bfloat16
F32 = jnp.float32
VMEM_LIMIT = 56 * 1024 * 1024

SMEM_SPEC = pl.BlockSpec(memory_space=pltpu.SMEM)
ANY_SPEC = pl.BlockSpec(memory_space=pl.ANY)
VMEM_SPEC = pl.BlockSpec(memory_space=pltpu.VMEM)


def dot(left, right):
    return lax.dot_general(left, right, (((1,), (0,)), ((), ())), preferred_element_type=F32)


def dot_cols(left, right):
    return lax.dot_general(left, right, (((1,), (1,)), ((), ())), preferred_element_type=F32)


def dot_rows(left, right):
    return lax.dot_general(left, right, (((0,), (0,)), ((), ())), preferred_element_type=F32)


def packing(len_ref):
    starts, sizes, ranks = [], [], []
    start = jnp.int32(0)
    rank = jnp.int32(0)
    held = jnp.int32(0)
    for i in range(SEQ):
        size = len_ref[i]
        fresh = held + size > LEN_BLK
        rank = jnp.where(fresh, rank + 1, rank)
        held = jnp.where(fresh, size, held + size)
        starts.append(start)
        sizes.append(size)
        ranks.append(rank)
        start = start + size
    return starts, sizes, ranks


def owners(len_ref, own):
    starts, _, ranks = packing(len_ref)
    found = []
    for k in range(LOCAL):
        block = own + PEERS * k
        owner = ranks[0]
        for i in range(1, SEQ):
            owner = jnp.where(starts[i] <= block, ranks[i], owner)
        found.append(owner)
    return found


def holdings(len_ref, own):
    starts, sizes, ranks = packing(len_ref)
    first = jnp.int32(LEN_BLK * LOCAL)
    count = jnp.int32(0)
    for i in range(SEQ):
        mine = ranks[i] == own
        first = jnp.where(mine, jnp.minimum(first, starts[i]), first)
        count = jnp.where(mine, count + sizes[i], count)
    return starts, sizes, ranks, first, count


def history_starts(hist_ref, own, starts, sizes, ranks, first):
    for j in range(LEN_BLK):
        hist_ref[j] = j
    for i in range(SEQ):

        @pl.when(ranks[i] == own)
        def _(i=i):
            begin = starts[i] - first

            def put(j, carry):
                hist_ref[j] = begin
                return carry

            lax.fori_loop(begin, begin + sizes[i], put, 0)


def send_kernel(len_ref, own_ref, rows_ref, out_ref):
    owner = owners(len_ref, own_ref[0])
    for k in range(LOCAL):
        out_ref[owner[k]] = rows_ref[k]


def home_kernel(len_ref, own_ref, back_ref, out_ref):
    owner = owners(len_ref, own_ref[0])
    for k in range(LOCAL):
        out_ref[k] = back_ref[owner[k]]


def fetch(src_ref, dst_ref, sems, first, count):
    for j in range(LEN_BLK):

        @pl.when(j < count)
        def _(j=j):
            slot = (first + j) & (PEERS - 1)
            pltpu.make_async_copy(src_ref.at[slot], dst_ref.at[j], sems.at[j]).start()


def arrive(src_ref, dst_ref, sems, count):
    for j in range(LEN_BLK):

        @pl.when(j < count)
        def _(j=j):
            pltpu.make_async_copy(src_ref.at[0], dst_ref.at[j], sems.at[j]).wait()


def tile_rows(ref, t, count):
    tile = ref[pl.ds(t * 4, 4)].reshape(TILE, D).astype(F32)
    place = lax.broadcasted_iota(jnp.int32, (TILE, D), 0) + t * TILE
    return jnp.where(place < count * BLOCK, tile, 0.0)


def normed_rows(values):
    centred = values - jnp.mean(values, axis=-1, keepdims=True)
    rstd = lax.rsqrt(jnp.mean(centred * centred, axis=-1, keepdims=True) + EPS)
    return centred * rstd, rstd


def head_masks():
    lane = lax.broadcasted_iota(jnp.int32, (1, LANES), 1)
    low = (lane < 64).astype(F32).astype(BF)
    high = (lane >= 64).astype(F32).astype(BF)
    return low, high


def rows_at(t):
    return pl.ds(pl.multiple_of(t * TILE, TILE), TILE)


def block_starts(hist_ref, t, shape, dim):
    place = lax.broadcasted_iota(jnp.int32, shape, dim)
    begin = jnp.full(shape, hist_ref[4 * t], jnp.int32)
    for b in range(1, 4):
        begin = jnp.where(place >= b * BLOCK, hist_ref[4 * t + b], begin)
    return begin * BLOCK


def key_tiles(hist_ref, i):
    low = hist_ref[4 * i] // 4
    clear = jnp.minimum((hist_ref[4 * i + 3] + 3) // 4, i)
    return low, jnp.maximum(clear, low)


def forward_kernel(
    len_ref,
    own_ref,
    got_ref,
    w_ref,
    gain_ref,
    upper_ref,
    values_ref,
    query_ref,
    keys_ref,
    slope_ref,
    attn_ref,
    scaled_ref,
    rows_ref,
    acc_ref,
    hist_ref,
    sems,
):
    own = own_ref[0]
    starts, sizes, ranks, first, count = holdings(len_ref, own)
    fetch(got_ref, rows_ref, sems, first, count)
    history_starts(hist_ref, own, starts, sizes, ranks, first)
    live = (count + 3) // 4
    arrive(got_ref, rows_ref, sems, count)

    def project(t, carry):
        normed, _ = normed_rows(tile_rows(rows_ref, t, count))
        scaled = (normed * gain_ref[...]).astype(BF)
        rows = rows_at(t)
        scaled_ref[rows, :] = scaled
        for quarter in range(4):
            half = 0.5 * dot(scaled, w_ref[:, quarter * D : (quarter + 1) * D])
            swing = jnp.tanh(half)
            active = half + half * swing
            slope = ((0.5 + 0.5 * swing) * (1.0 + (half - half * swing))).astype(BF)
            if quarter == 0:
                upper_ref[rows, :] = active.astype(BF)
            if quarter == 2:
                active = active * 0.0625
            active = active.astype(BF)
            for p in range(PAIRS):
                lanes = slice(p * LANES, (p + 1) * LANES)
                slope_ref[quarter * PAIRS + p, rows, :] = slope[:, lanes]
                if quarter:
                    ref = (None, values_ref, query_ref, keys_ref)[quarter]
                    ref[p, rows, :] = active[:, lanes]
        return carry

    lax.fori_loop(0, live, project, 0)

    def clear(t, carry):
        scaled_ref[rows_at(t), :] = jnp.zeros((TILE, D), BF)
        return carry

    lax.fori_loop(live, TILES, clear, 0)

    masks = head_masks()

    def pair(p, carry):
        def query_tile(i, carry):
            query = query_ref[p, rows_at(i), :]
            acc_ref[...] = jnp.zeros((TILE, LANES), F32)

            def step(j, masked):
                keys = keys_ref[p, rows_at(j), :]
                values = values_ref[p, rows_at(j), :]
                if masked:
                    shape = (TILE, TILE)
                    col = lax.broadcasted_iota(jnp.int32, shape, 1) + j * TILE
                    row = lax.broadcasted_iota(jnp.int32, shape, 0) + i * TILE
                    allowed = (col <= row) & (col >= block_starts(hist_ref, i, shape, 0))
                total = acc_ref[...]
                for mask in masks:
                    half = dot_cols(query, keys * mask)
                    weights = half + half * jnp.tanh(half)
                    if masked:
                        weights = jnp.where(allowed, weights, 0.0)
                    total += dot(weights.astype(BF), values * mask)
                acc_ref[...] = total

            low, clear_from = key_tiles(hist_ref, i)

            def masked_step(j, carry):
                step(j, True)
                return carry

            def clear_step(j, carry):
                step(j, False)
                return carry

            lax.fori_loop(low, clear_from, masked_step, 0)
            lax.fori_loop(clear_from, i, clear_step, 0)
            step(i, True)
            attn_ref[p, rows_at(i), :] = acc_ref[...].astype(BF)
            return carry

        return lax.fori_loop(0, live, query_tile, carry)

    lax.fori_loop(0, PAIRS, pair, 0)


def backward_kernel(
    len_ref,
    own_ref,
    got_ref,
    grads_ref,
    upper_ref,
    values_ref,
    query_ref,
    keys_ref,
    slope_ref,
    attn_ref,
    scaled_ref,
    w_ref,
    w_out_ref,
    gain_in_ref,
    gain_attn_ref,
    back_ref,
    terms_ref,
    rows_ref,
    cot_ref,
    d_attn_ref,
    d_hidden_ref,
    out_ref,
    gains_ref,
    d_query_ref,
    d_keys_ref,
    d_values_ref,
    hist_ref,
    row_sems,
    cot_sems,
):
    own = own_ref[0]
    core = own & 1
    starts, sizes, ranks, first, count = holdings(len_ref, own)
    fetch(grads_ref, cot_ref, cot_sems, first, count)
    fetch(got_ref, rows_ref, row_sems, first, count)
    history_starts(hist_ref, own, starts, sizes, ranks, first)
    live = (count + 3) // 4
    out_ref[...] = jnp.zeros((D, D), F32)
    gains_ref[...] = jnp.zeros((2, D), F32)
    arrive(grads_ref, cot_ref, cot_sems, count)

    def middle(t, carry):
        rows = rows_at(t)
        attn = jnp.concatenate([attn_ref[p, rows, :] for p in range(PAIRS)], axis=1)
        normed, rstd = normed_rows(attn.astype(F32))
        upper = upper_ref[rows, :].astype(F32)
        cot = tile_rows(cot_ref, t, count).astype(BF)
        d_mixed = dot_cols(cot, w_out_ref[...])
        gained = normed * gain_attn_ref[...]
        out_ref[...] += dot_rows((gained * upper).astype(BF), cot)
        d_upper = d_mixed * gained
        pull = d_mixed * upper
        gains_ref[1:2, :] += jnp.sum(pull * normed, axis=0, keepdims=True)
        pull = pull * gain_attn_ref[...]
        d_attn = rstd * (
            pull
            - jnp.mean(pull, axis=-1, keepdims=True)
            - normed * jnp.mean(pull * normed, axis=-1, keepdims=True)
        )
        for p in range(PAIRS):
            lanes = slice(p * LANES, (p + 1) * LANES)
            d_attn_ref[p, rows, :] = d_attn[:, lanes].astype(BF)
            slope = slope_ref[p, rows, :].astype(F32)
            d_hidden_ref[p, rows, :] = (d_upper[:, lanes] * slope).astype(BF)
        return carry

    lax.fori_loop(0, live, middle, 0)

    def clear(t, carry):
        d_hidden_ref[:, rows_at(t), :] = jnp.zeros((4 * PAIRS, TILE, LANES), BF)
        return carry

    lax.fori_loop(live, TILES, clear, 0)

    masks = head_masks()

    def pair(p, carry):
        d_keys_ref[...] = jnp.zeros((ROWS, LANES), F32)
        d_values_ref[...] = jnp.zeros((ROWS, LANES), F32)

        def query_tile(i, carry):
            query = query_ref[p, rows_at(i), :]
            d_attn = d_attn_ref[p, rows_at(i), :]
            d_query_ref[...] = jnp.zeros((TILE, LANES), F32)

            def step(j, masked):
                rows = rows_at(j)
                keys = keys_ref[p, rows, :]
                values = values_ref[p, rows, :]
                if masked:
                    shape = (TILE, TILE)
                    key_row = lax.broadcasted_iota(jnp.int32, shape, 0) + j * TILE
                    query_row = lax.broadcasted_iota(jnp.int32, shape, 1) + i * TILE
                    allowed = (key_row <= query_row) & (
                        key_row >= block_starts(hist_ref, i, shape, 1)
                    )
                d_query = d_query_ref[...]
                d_keys = d_keys_ref[rows, :]
                d_values = d_values_ref[rows, :]
                for mask in masks:
                    masked_keys = keys * mask
                    half = dot_cols(masked_keys, query)
                    swing = jnp.tanh(half)
                    bend = half * swing
                    weights = half + bend
                    slope = (1.0 + swing) * ((1.0 + half) - bend)
                    grad = dot_cols(values * mask, d_attn) * slope
                    if masked:
                        weights = jnp.where(allowed, weights, 0.0)
                        grad = jnp.where(allowed, grad, 0.0)
                    grad = grad.astype(BF)
                    d_values += dot(weights.astype(BF), d_attn * mask)
                    d_keys += dot(grad, query * mask)
                    d_query += dot_rows(grad, masked_keys)
                d_query_ref[...] = d_query
                d_keys_ref[rows, :] = d_keys
                d_values_ref[rows, :] = d_values

            low, clear_from = key_tiles(hist_ref, i)

            def masked_step(j, carry):
                step(j, True)
                return carry

            def clear_step(j, carry):
                step(j, False)
                return carry

            lax.fori_loop(low, clear_from, masked_step, 0)
            lax.fori_loop(clear_from, i, clear_step, 0)
            step(i, True)
            slope = slope_ref[2 * PAIRS + p, rows_at(i), :].astype(F32)
            d_hidden_ref[2 * PAIRS + p, rows_at(i), :] = (
                d_query_ref[...] * 0.0625 * slope
            ).astype(BF)
            return carry

        lax.fori_loop(0, live, query_tile, 0)

        def finish(t, carry):
            rows = rows_at(t)
            for place, ref in ((1, d_values_ref), (3, d_keys_ref)):
                slope = slope_ref[place * PAIRS + p, rows, :].astype(F32)
                d_hidden_ref[place * PAIRS + p, rows, :] = (ref[rows, :] * slope).astype(BF)
            return carry

        lax.fori_loop(0, live, finish, 0)
        return carry

    lax.fori_loop(0, PAIRS, pair, 0)

    arrive(got_ref, rows_ref, row_sems, count)

    def final(t, carry):
        rows = rows_at(t)
        normed, rstd = normed_rows(tile_rows(rows_ref, t, count))
        d_scaled = jnp.zeros((TILE, D), F32)
        for c in range(8):
            part = jnp.concatenate(
                [d_hidden_ref[2 * c, rows, :], d_hidden_ref[2 * c + 1, rows, :]], axis=1
            )
            d_scaled += dot_cols(part, w_ref[:, c * 256 : (c + 1) * 256])
        gains_ref[0:1, :] += jnp.sum(d_scaled * normed, axis=0, keepdims=True)
        pull = d_scaled * gain_in_ref[...]
        d_rows = rstd * (
            pull
            - jnp.mean(pull, axis=-1, keepdims=True)
            - normed * jnp.mean(pull * normed, axis=-1, keepdims=True)
        )
        d_rows = (d_rows + tile_rows(cot_ref, t, count)).astype(BF)
        for b in range(4):
            slot = (first + t * 4 + b) & (PEERS - 1)
            back_ref[slot] = d_rows[b * BLOCK : (b + 1) * BLOCK, :]
        return carry

    lax.fori_loop(0, live, final, 0)

    def put(piece, values):
        half, place = divmod(piece, 10)
        terms_ref[half ^ core, place * D : (place + 1) * D, :] = values.astype(BF)

    for c in range(8):
        part = jnp.concatenate([d_hidden_ref[2 * c], d_hidden_ref[2 * c + 1]], axis=1)
        term = dot_rows(scaled_ref[...], part)
        put(2 * c, term[:, :LANES])
        put(2 * c + 1, term[:, LANES:])
    for p in range(PAIRS):
        put(16 + p, out_ref[:, p * LANES : (p + 1) * LANES])
    for half in range(2):
        terms_ref[half ^ core, 10 * D :, :] = jnp.concatenate(
            [gains_ref[half : half + 1, p * LANES : (p + 1) * LANES] for p in range(PAIRS)]
            + [jnp.zeros((HALF - 10 * D - PAIRS, LANES), F32)],
            axis=0,
        ).astype(BF)


def spread_kernel(own_ref, mine_ref, other_ref, proj_ref, out_ref, gain_in_ref, gain_attn_ref):
    core = own_ref[0] & 1

    def write(low_ref, high_ref):
        for piece in range(20):
            half, place = divmod(piece, 10)
            part = (low_ref, high_ref)[half][place * D : (place + 1) * D, :].astype(F32)
            if piece < 16:
                proj_ref[:, piece * LANES : (piece + 1) * LANES] = part
            else:
                out_ref[:, (piece - 16) * LANES : (piece - 15) * LANES] = part
        gain_in_ref[...] = low_ref[10 * D : 10 * D + 16, :].astype(F32)[:PAIRS]
        gain_attn_ref[...] = high_ref[10 * D : 10 * D + 16, :].astype(F32)[:PAIRS]

    @pl.when(core == 0)
    def _():
        write(mine_ref, other_ref)

    @pl.when(core == 1)
    def _():
        write(other_ref, mine_ref)


def struct(shape, dtype):
    return jax.ShapeDtypeStruct(shape, dtype)


def params():
    return pltpu.CompilerParams(vmem_limit_bytes=VMEM_LIMIT)


def send_blocks(lens, own, rows):
    return pl.pallas_call(
        send_kernel,
        out_shape=struct((PEERS, BLOCK, D), BF),
        in_specs=[SMEM_SPEC, SMEM_SPEC, VMEM_SPEC],
        out_specs=VMEM_SPEC,
        name="send_blocks",
    )(lens, own, rows.reshape(LOCAL, BLOCK, D))


def forward_layer(lens, own, got_rows, w_proj, gain_in):
    pairs = struct((PAIRS, ROWS, LANES), BF)
    wide = struct((ROWS, D), BF)
    return pl.pallas_call(
        forward_kernel,
        out_shape=(
            wide,
            pairs,
            pairs,
            pairs,
            struct((4 * PAIRS, ROWS, LANES), BF),
            pairs,
            wide,
        ),
        in_specs=[SMEM_SPEC, SMEM_SPEC, ANY_SPEC, VMEM_SPEC, VMEM_SPEC],
        out_specs=(VMEM_SPEC,) * 7,
        scratch_shapes=[
            pltpu.VMEM((LEN_BLK, BLOCK, D), BF),
            pltpu.VMEM((TILE, LANES), F32),
            pltpu.SMEM((LEN_BLK,), jnp.int32),
            pltpu.SemaphoreType.DMA((LEN_BLK,)),
        ],
        compiler_params=params(),
        name="forward_layer",
    )(lens, own, got_rows, w_proj, gain_in)


def backward_layer(lens, own, got_rows, got_grads, saved, w_proj, w_out, gain_in, gain_attn):
    return pl.pallas_call(
        backward_kernel,
        out_shape=(struct((PEERS, BLOCK, D), BF), struct((2, HALF, LANES), BF)),
        in_specs=[SMEM_SPEC, SMEM_SPEC, ANY_SPEC, ANY_SPEC] + [VMEM_SPEC] * 11,
        out_specs=(VMEM_SPEC, VMEM_SPEC),
        scratch_shapes=[
            pltpu.VMEM((LEN_BLK, BLOCK, D), BF),
            pltpu.VMEM((LEN_BLK, BLOCK, D), BF),
            pltpu.VMEM((PAIRS, ROWS, LANES), BF),
            pltpu.VMEM((4 * PAIRS, ROWS, LANES), BF),
            pltpu.VMEM((D, D), F32),
            pltpu.VMEM((2, D), F32),
            pltpu.VMEM((TILE, LANES), F32),
            pltpu.VMEM((ROWS, LANES), F32),
            pltpu.VMEM((ROWS, LANES), F32),
            pltpu.SMEM((LEN_BLK,), jnp.int32),
            pltpu.SemaphoreType.DMA((LEN_BLK,)),
            pltpu.SemaphoreType.DMA((LEN_BLK,)),
        ],
        compiler_params=params(),
        name="backward_layer",
    )(
        lens, own, got_rows, got_grads, *saved, w_proj, w_out, gain_in, gain_attn
    )


def per_device(events, cotangent, lengths, gain_in, w_proj, gain_attn, w_out):
    own = lax.axis_index(("chip", "core")).astype(jnp.int32).reshape(1)
    lens = lengths[0]
    got_rows = lax.all_to_all(send_blocks(lens, own, events), ("chip", "core"), 0, 0, tiled=True)
    got_grads = lax.all_to_all(send_blocks(lens, own, cotangent), ("chip", "core"), 0, 0, tiled=True)
    gain_in = gain_in.reshape(1, D)
    saved = forward_layer(lens, own, got_rows, w_proj, gain_in)
    send_back, terms = backward_layer(
        lens, own, got_rows, got_grads, saved, w_proj, w_out, gain_in, gain_attn.reshape(1, D)
    )
    swap = [(0, 1), (1, 0)]
    other = lax.ppermute(terms[1], "core", swap)
    chip_sum = (terms[0].astype(F32) + other.astype(F32)).astype(BF)
    parts = lax.all_to_all(chip_sum.reshape(64, PART, LANES), ("grp", "chip"), 0, 0, tiled=True)
    total = (jnp.sum(parts.astype(F32), axis=0) * (1.0 / DEVICES)).astype(BF)
    copies = jnp.broadcast_to(total[None], (64, PART, LANES))
    mine = lax.all_to_all(copies, ("grp", "chip"), 0, 0, tiled=True).reshape(HALF, LANES)
    others = lax.ppermute(mine, "core", swap)
    came_back = lax.all_to_all(send_back, ("chip", "core"), 0, 0, tiled=True)
    d_rows = pl.pallas_call(
        home_kernel,
        out_shape=struct((LOCAL, BLOCK, D), BF),
        in_specs=[SMEM_SPEC, SMEM_SPEC, VMEM_SPEC],
        out_specs=VMEM_SPEC,
        name="take_home",
    )(lens, own, came_back)
    gain = struct((PAIRS, LANES), F32)
    grad_proj, grad_out, grad_in, grad_attn = pl.pallas_call(
        spread_kernel,
        out_shape=(struct((D, 4 * D), F32), struct((D, D), F32), gain, gain),
        in_specs=[SMEM_SPEC, VMEM_SPEC, VMEM_SPEC],
        out_specs=(VMEM_SPEC,) * 4,
        compiler_params=params(),
        name="spread_grads",
    )(own, mine, others)
    return (
        d_rows.reshape(1, LOCAL * BLOCK, D),
        grad_proj,
        grad_out,
        grad_in.reshape(D),
        grad_attn.reshape(D),
    )


def solution(mesh):
    fine = Mesh(mesh.devices.reshape(8, 8, 2), ("grp", "chip", "core"))
    rows = P("grp", ("chip", "core"), None)
    return jax.shard_map(
        per_device,
        mesh=fine,
        in_specs=(rows, rows, P("grp", None), P(), P(), P(), P()),
        out_specs=(rows, P(), P(), P(), P()),
        check_vma=False,
    )
```

```python
import jax
import jax.numpy as jnp
from jax import lax
from jax.experimental import pallas as pl
from jax.experimental.pallas import tpu as pltpu
from jax.sharding import Mesh, PartitionSpec as P

D = 512
HEADS = 8
BLOCK = 64
LEN_BLK = 16
SEQ = 16
PEERS = 16
LOCAL = 8
TILE = 256
TILES = 4
ROWS = 1024
LANES = 128
PAIRS = 4
PART = 88
HALF = 64 * PART
EPS = 1e-06
DEVICES = 128
BF = jnp.bfloat16
F32 = jnp.float32
VMEM_LIMIT = 52 * 1024 * 1024

SMEM_SPEC = pl.BlockSpec(memory_space=pltpu.SMEM)
ANY_SPEC = pl.BlockSpec(memory_space=pl.ANY)
VMEM_SPEC = pl.BlockSpec(memory_space=pltpu.VMEM)


def dot(left, right):
    return lax.dot_general(left, right, (((1,), (0,)), ((), ())), preferred_element_type=F32)


def dot_cols(left, right):
    return lax.dot_general(left, right, (((1,), (1,)), ((), ())), preferred_element_type=F32)


def dot_rows(left, right):
    return lax.dot_general(left, right, (((0,), (0,)), ((), ())), preferred_element_type=F32)


def packing(len_ref):
    starts, sizes, ranks = [], [], []
    start = jnp.int32(0)
    rank = jnp.int32(0)
    held = jnp.int32(0)
    for i in range(SEQ):
        size = len_ref[i]
        fresh = held + size > LEN_BLK
        rank = jnp.where(fresh, rank + 1, rank)
        held = jnp.where(fresh, size, held + size)
        starts.append(start)
        sizes.append(size)
        ranks.append(rank)
        start = start + size
    return starts, sizes, ranks


def owners(len_ref, own):
    starts, _, ranks = packing(len_ref)
    found = []
    for k in range(LOCAL):
        block = own + PEERS * k
        owner = ranks[0]
        for i in range(1, SEQ):
            owner = jnp.where(starts[i] <= block, ranks[i], owner)
        found.append(owner)
    return found


def holdings(len_ref, own):
    starts, sizes, ranks = packing(len_ref)
    first = jnp.int32(LEN_BLK * LOCAL)
    count = jnp.int32(0)
    for i in range(SEQ):
        mine = ranks[i] == own
        first = jnp.where(mine, jnp.minimum(first, starts[i]), first)
        count = jnp.where(mine, count + sizes[i], count)
    return starts, sizes, ranks, first, count


def history_starts(hist_ref, own, starts, sizes, ranks, first):
    for j in range(LEN_BLK):
        hist_ref[j] = j
    for i in range(SEQ):

        @pl.when(ranks[i] == own)
        def _(i=i):
            begin = starts[i] - first

            def put(j, carry):
                hist_ref[j] = begin
                return carry

            lax.fori_loop(begin, begin + sizes[i], put, 0)


def send_kernel(len_ref, own_ref, rows_ref, out_ref):
    owner = owners(len_ref, own_ref[0])
    for k in range(LOCAL):
        out_ref[owner[k]] = rows_ref[k]


def home_kernel(len_ref, own_ref, back_ref, out_ref):
    owner = owners(len_ref, own_ref[0])
    for k in range(LOCAL):
        out_ref[k] = back_ref[owner[k]]


def fetch(src_ref, dst_ref, sems, first, count):
    for j in range(LEN_BLK):

        @pl.when(j < count)
        def _(j=j):
            slot = (first + j) & (PEERS - 1)
            pltpu.make_async_copy(src_ref.at[slot], dst_ref.at[j], sems.at[j]).start()


def arrive(src_ref, dst_ref, sems, count):
    for j in range(LEN_BLK):

        @pl.when(j < count)
        def _(j=j):
            pltpu.make_async_copy(src_ref.at[0], dst_ref.at[j], sems.at[j]).wait()


def tile_rows(ref, t, count):
    tile = ref[pl.ds(t * 4, 4)].reshape(TILE, D).astype(F32)
    place = lax.broadcasted_iota(jnp.int32, (TILE, D), 0) + t * TILE
    return jnp.where(place < count * BLOCK, tile, 0.0)


def normed_rows(values):
    centred = values - jnp.mean(values, axis=-1, keepdims=True)
    rstd = lax.rsqrt(jnp.mean(centred * centred, axis=-1, keepdims=True) + EPS)
    return centred * rstd, rstd


def head_masks():
    lane = lax.broadcasted_iota(jnp.int32, (1, LANES), 1)
    low = (lane < 64).astype(F32).astype(BF)
    high = (lane >= 64).astype(F32).astype(BF)
    return low, high


GROUP = 4


def rows_at(t):
    return pl.ds(pl.multiple_of(t * TILE, TILE), TILE)


def block_starts(hist_ref, t, shape, dim):
    place = lax.broadcasted_iota(jnp.int32, shape, dim)
    begin = jnp.full(shape, hist_ref[4 * t], jnp.int32)
    for b in range(1, 4):
        begin = jnp.where(place >= b * BLOCK, hist_ref[4 * t + b], begin)
    return begin * BLOCK


def key_tiles(hist_ref, i):
    low = hist_ref[4 * i] // 4
    clear = jnp.minimum((hist_ref[4 * i + 3] + 3) // 4, i)
    return low, jnp.maximum(clear, low)


def forward_kernel(
    len_ref,
    own_ref,
    got_ref,
    w_ref,
    gain_ref,
    attn_ref,
    upper_out,
    values_out,
    query_out,
    keys_out,
    slope_out,
    scaled_out,
    upper_ref,
    values_ref,
    query_ref,
    keys_ref,
    slope_ref,
    scaled_ref,
    rows_ref,
    acc_ref,
    hist_ref,
    sems,
    save_sems,
):
    own = own_ref[0]
    starts, sizes, ranks, first, count = holdings(len_ref, own)
    fetch(got_ref, rows_ref, sems, first, count)
    history_starts(hist_ref, own, starts, sizes, ranks, first)
    live = (count + 3) // 4
    arrive(got_ref, rows_ref, sems, count)

    def project(t, carry):
        normed, _ = normed_rows(tile_rows(rows_ref, t, count))
        scaled = (normed * gain_ref[...]).astype(BF)
        rows = rows_at(t)
        scaled_ref[rows, :] = scaled
        for quarter in range(4):
            half = 0.5 * dot(scaled, w_ref[:, quarter * D : (quarter + 1) * D])
            swing = jnp.tanh(half)
            active = half + half * swing
            slope = ((0.5 + 0.5 * swing) * (1.0 + (half - half * swing))).astype(BF)
            if quarter == 0:
                upper_ref[rows, :] = active.astype(BF)
            if quarter == 2:
                active = active * 0.0625
            active = active.astype(BF)
            for p in range(PAIRS):
                lanes = slice(p * LANES, (p + 1) * LANES)
                slope_ref[quarter * PAIRS + p, rows, :] = slope[:, lanes]
                if quarter:
                    ref = (None, values_ref, query_ref, keys_ref)[quarter]
                    ref[p, rows, :] = active[:, lanes]
        return carry

    lax.fori_loop(0, live, project, 0)

    def clear(t, carry):
        scaled_ref[rows_at(t), :] = jnp.zeros((TILE, D), BF)
        return carry

    lax.fori_loop(live, TILES, clear, 0)

    saves = [
        pltpu.make_async_copy(src, dst, save_sems.at[n])
        for n, (src, dst) in enumerate(
            (
                (upper_ref, upper_out),
                (values_ref, values_out),
                (query_ref, query_out),
                (keys_ref, keys_out),
                (slope_ref, slope_out),
                (scaled_ref, scaled_out),
            )
        )
    ]
    for save in saves:
        save.start()

    masks = head_masks()

    def group(g, carry):
        def query_tile(i, carry):
            acc_ref[...] = jnp.zeros((GROUP, TILE, LANES), F32)

            def step(j, masked):
                if masked:
                    shape = (TILE, TILE)
                    col = lax.broadcasted_iota(jnp.int32, shape, 1) + j * TILE
                    row = lax.broadcasted_iota(jnp.int32, shape, 0) + i * TILE
                    allowed = (col <= row) & (col >= block_starts(hist_ref, i, shape, 0))
                for n in range(GROUP):
                    p = g * GROUP + n
                    query = query_ref[p, rows_at(i), :]
                    keys = keys_ref[p, rows_at(j), :]
                    values = values_ref[p, rows_at(j), :]
                    total = acc_ref[n]
                    for mask in masks:
                        half = dot_cols(query, keys * mask)
                        weights = half + half * jnp.tanh(half)
                        if masked:
                            weights = jnp.where(allowed, weights, 0.0)
                        total += dot(weights.astype(BF), values * mask)
                    acc_ref[n] = total

            low, clear_from = key_tiles(hist_ref, i)

            def masked_step(j, carry):
                step(j, True)
                return carry

            def clear_step(j, carry):
                step(j, False)
                return carry

            lax.fori_loop(low, clear_from, masked_step, 0)
            lax.fori_loop(clear_from, i, clear_step, 0)
            step(i, True)
            for n in range(GROUP):
                attn_ref[g * GROUP + n, rows_at(i), :] = acc_ref[n].astype(BF)
            return carry

        return lax.fori_loop(0, live, query_tile, carry)

    lax.fori_loop(0, PAIRS // GROUP, group, 0)
    for save in saves:
        save.wait()


def backward_kernel(
    len_ref,
    own_ref,
    got_ref,
    grads_ref,
    attn_in,
    upper_in,
    values_in,
    query_in,
    keys_in,
    slope_in,
    scaled_in,
    w_in,
    w_out_ref,
    gain_in_ref,
    gain_attn_ref,
    back_ref,
    terms_ref,
    rows_ref,
    cot_ref,
    d_attn_ref,
    d_hidden_ref,
    out_ref,
    gains_ref,
    d_query_ref,
    keys_t_ref,
    d_keys_ref,
    d_values_ref,
    hist_ref,
    row_sems,
    cot_sems,
    load_sems,
    attn_ref,
    upper_ref,
    values_ref,
    query_ref,
    keys_ref,
    slope_ref,
    scaled_ref,
    w_ref,
):
    own = own_ref[0]
    core = own & 1
    starts, sizes, ranks, first, count = holdings(len_ref, own)
    fetch(grads_ref, cot_ref, cot_sems, first, count)
    early = pl.ds(0, PAIRS)
    late = pl.ds(PAIRS, 3 * PAIRS)
    loads = [
        pltpu.make_async_copy(src, dst, load_sems.at[n])
        for n, (src, dst) in enumerate(
            (
                (attn_in, attn_ref),
                (upper_in, upper_ref),
                (slope_in.at[early], slope_ref.at[early]),
                (keys_in, keys_ref),
                (query_in, query_ref),
                (values_in, values_ref),
                (slope_in.at[late], slope_ref.at[late]),
                (w_in, w_ref),
                (scaled_in, scaled_ref),
            )
        )
    ]
    for load in loads:
        load.start()
    fetch(got_ref, rows_ref, row_sems, first, count)
    history_starts(hist_ref, own, starts, sizes, ranks, first)
    live = (count + 3) // 4
    out_ref[...] = jnp.zeros((D, D), F32)
    gains_ref[...] = jnp.zeros((2, D), F32)
    arrive(grads_ref, cot_ref, cot_sems, count)
    for load in loads[:3]:
        load.wait()

    def middle(t, carry):
        rows = rows_at(t)
        attn = jnp.concatenate([attn_ref[p, rows, :] for p in range(PAIRS)], axis=1)
        normed, rstd = normed_rows(attn.astype(F32))
        upper = upper_ref[rows, :].astype(F32)
        cot = tile_rows(cot_ref, t, count).astype(BF)
        d_mixed = dot_cols(cot, w_out_ref[...])
        gained = normed * gain_attn_ref[...]
        out_ref[...] += dot_rows((gained * upper).astype(BF), cot)
        d_upper = d_mixed * gained
        pull = d_mixed * upper
        gains_ref[1:2, :] += jnp.sum(pull * normed, axis=0, keepdims=True)
        pull = pull * gain_attn_ref[...]
        d_attn = rstd * (
            pull
            - jnp.mean(pull, axis=-1, keepdims=True)
            - normed * jnp.mean(pull * normed, axis=-1, keepdims=True)
        )
        for p in range(PAIRS):
            lanes = slice(p * LANES, (p + 1) * LANES)
            d_attn_ref[p, rows, :] = d_attn[:, lanes].astype(BF)
            slope = slope_ref[p, rows, :].astype(F32)
            d_hidden_ref[p, rows, :] = (d_upper[:, lanes] * slope).astype(BF)
        return carry

    lax.fori_loop(0, live, middle, 0)

    def clear(t, carry):
        d_hidden_ref[:, rows_at(t), :] = jnp.zeros((4 * PAIRS, TILE, LANES), BF)
        return carry

    lax.fori_loop(live, TILES, clear, 0)

    masks = head_masks()
    for load in loads[3:7]:
        load.wait()

    def turn(t, carry):
        for p in range(PAIRS):
            keys_t_ref[p, :, rows_at(t)] = keys_ref[p, rows_at(t), :].T
        return carry

    lax.fori_loop(0, live, turn, 0)

    def group(g, carry):
        d_keys_ref[...] = jnp.zeros((GROUP, ROWS, LANES), F32)
        d_values_ref[...] = jnp.zeros((GROUP, ROWS, LANES), F32)

        def query_tile(i, carry):
            d_query_ref[...] = jnp.zeros((GROUP, LANES, TILE), F32)

            def step(j, masked):
                rows = rows_at(j)
                if masked:
                    shape = (TILE, TILE)
                    key_row = lax.broadcasted_iota(jnp.int32, shape, 0) + j * TILE
                    query_row = lax.broadcasted_iota(jnp.int32, shape, 1) + i * TILE
                    allowed = (key_row <= query_row) & (
                        key_row >= block_starts(hist_ref, i, shape, 1)
                    )
                for n in range(GROUP):
                    p = g * GROUP + n
                    query = query_ref[p, rows_at(i), :]
                    d_attn = d_attn_ref[p, rows_at(i), :]
                    keys = keys_ref[p, rows, :]
                    values = values_ref[p, rows, :]
                    d_keys = d_keys_ref[n, rows, :]
                    d_values = d_values_ref[n, rows, :]
                    for h, mask in enumerate(masks):
                        masked_keys = keys * mask
                        half = dot_cols(masked_keys, query)
                        swing = jnp.tanh(half)
                        bend = half * swing
                        weights = half + bend
                        slope = (1.0 + swing) * ((1.0 + half) - bend)
                        grad = dot_cols(values * mask, d_attn) * slope
                        if masked:
                            weights = jnp.where(allowed, weights, 0.0)
                            grad = jnp.where(allowed, grad, 0.0)
                        grad = grad.astype(BF)
                        d_values += dot(weights.astype(BF), d_attn * mask)
                        d_keys += dot(grad, query * mask)
                        head_rows = slice(h * 64, h * 64 + 64)
                        d_query_ref[n, head_rows, :] += dot(keys_t_ref[p, head_rows, rows], grad)
                    d_keys_ref[n, rows, :] = d_keys
                    d_values_ref[n, rows, :] = d_values

            low, clear_from = key_tiles(hist_ref, i)

            def masked_step(j, carry):
                step(j, True)
                return carry

            def clear_step(j, carry):
                step(j, False)
                return carry

            lax.fori_loop(low, clear_from, masked_step, 0)
            lax.fori_loop(clear_from, i, clear_step, 0)
            step(i, True)
            for n in range(GROUP):
                place = 2 * PAIRS + g * GROUP + n
                slope = slope_ref[place, rows_at(i), :].astype(F32)
                d_hidden_ref[place, rows_at(i), :] = (d_query_ref[n].T * 0.0625 * slope).astype(BF)
            return carry

        lax.fori_loop(0, live, query_tile, 0)

        def finish(t, carry):
            rows = rows_at(t)
            for n in range(GROUP):
                for quarter, ref in ((1, d_values_ref), (3, d_keys_ref)):
                    place = quarter * PAIRS + g * GROUP + n
                    slope = slope_ref[place, rows, :].astype(F32)
                    d_hidden_ref[place, rows, :] = (ref[n, rows, :] * slope).astype(BF)
            return carry

        lax.fori_loop(0, live, finish, 0)
        return carry

    lax.fori_loop(0, PAIRS // GROUP, group, 0)

    arrive(got_ref, rows_ref, row_sems, count)
    for load in loads[7:]:
        load.wait()

    def final(t, carry):
        rows = rows_at(t)
        normed, rstd = normed_rows(tile_rows(rows_ref, t, count))
        d_scaled = jnp.zeros((TILE, D), F32)
        for c in range(8):
            part = jnp.concatenate(
                [d_hidden_ref[2 * c, rows, :], d_hidden_ref[2 * c + 1, rows, :]], axis=1
            )
            d_scaled += dot_cols(part, w_ref[:, c * 256 : (c + 1) * 256])
        gains_ref[0:1, :] += jnp.sum(d_scaled * normed, axis=0, keepdims=True)
        pull = d_scaled * gain_in_ref[...]
        d_rows = rstd * (
            pull
            - jnp.mean(pull, axis=-1, keepdims=True)
            - normed * jnp.mean(pull * normed, axis=-1, keepdims=True)
        )
        d_rows = (d_rows + tile_rows(cot_ref, t, count)).astype(BF)
        for b in range(4):
            slot = (first + t * 4 + b) & (PEERS - 1)
            back_ref[slot] = d_rows[b * BLOCK : (b + 1) * BLOCK, :]
        return carry

    lax.fori_loop(0, live, final, 0)

    def put(piece, values):
        half, place = divmod(piece, 10)
        terms_ref[half ^ core, place * D : (place + 1) * D, :] = values.astype(BF)

    for c in range(8):
        part = jnp.concatenate([d_hidden_ref[2 * c], d_hidden_ref[2 * c + 1]], axis=1)
        term = dot_rows(scaled_ref[...], part)
        put(2 * c, term[:, :LANES])
        put(2 * c + 1, term[:, LANES:])
    for p in range(PAIRS):
        put(16 + p, out_ref[:, p * LANES : (p + 1) * LANES])
    for half in range(2):
        terms_ref[half ^ core, 10 * D :, :] = jnp.concatenate(
            [gains_ref[half : half + 1, p * LANES : (p + 1) * LANES] for p in range(PAIRS)]
            + [jnp.zeros((HALF - 10 * D - PAIRS, LANES), F32)],
            axis=0,
        ).astype(BF)


def spread_kernel(own_ref, mine_ref, other_ref, proj_ref, out_ref, gain_in_ref, gain_attn_ref):
    core = own_ref[0] & 1

    def write(low_ref, high_ref):
        for piece in range(20):
            half, place = divmod(piece, 10)
            part = (low_ref, high_ref)[half][place * D : (place + 1) * D, :].astype(F32)
            if piece < 16:
                proj_ref[:, piece * LANES : (piece + 1) * LANES] = part
            else:
                out_ref[:, (piece - 16) * LANES : (piece - 15) * LANES] = part
        gain_in_ref[...] = low_ref[10 * D : 10 * D + 16, :].astype(F32)[:PAIRS]
        gain_attn_ref[...] = high_ref[10 * D : 10 * D + 16, :].astype(F32)[:PAIRS]

    @pl.when(core == 0)
    def _():
        write(mine_ref, other_ref)

    @pl.when(core == 1)
    def _():
        write(other_ref, mine_ref)


def struct(shape, dtype):
    return jax.ShapeDtypeStruct(shape, dtype)


def params():
    return pltpu.CompilerParams(vmem_limit_bytes=VMEM_LIMIT)


def send_blocks(lens, own, rows):
    return pl.pallas_call(
        send_kernel,
        out_shape=struct((PEERS, BLOCK, D), BF),
        in_specs=[SMEM_SPEC, SMEM_SPEC, VMEM_SPEC],
        out_specs=VMEM_SPEC,
        name="send_blocks",
    )(lens, own, rows.reshape(LOCAL, BLOCK, D))


def saved_shapes(make):
    pairs = make((PAIRS, ROWS, LANES), BF)
    wide = make((ROWS, D), BF)
    return [wide, pairs, pairs, pairs, make((4 * PAIRS, ROWS, LANES), BF), wide]


def forward_layer(lens, own, got_rows, w_proj, gain_in):
    return pl.pallas_call(
        forward_kernel,
        out_shape=[struct((PAIRS, ROWS, LANES), BF)] + saved_shapes(struct),
        in_specs=[SMEM_SPEC, SMEM_SPEC, ANY_SPEC, VMEM_SPEC, VMEM_SPEC],
        out_specs=[VMEM_SPEC] + [ANY_SPEC] * 6,
        scratch_shapes=saved_shapes(pltpu.VMEM)
        + [
            pltpu.VMEM((LEN_BLK, BLOCK, D), BF),
            pltpu.VMEM((GROUP, TILE, LANES), F32),
            pltpu.SMEM((LEN_BLK,), jnp.int32),
            pltpu.SemaphoreType.DMA((LEN_BLK,)),
            pltpu.SemaphoreType.DMA((6,)),
        ],
        compiler_params=params(),
        name="forward_layer",
    )(lens, own, got_rows, w_proj, gain_in)


def backward_layer(lens, own, got_rows, got_grads, saved, w_proj, w_out, gain_in, gain_attn):
    return pl.pallas_call(
        backward_kernel,
        out_shape=(struct((PEERS, BLOCK, D), BF), struct((2, HALF, LANES), BF)),
        in_specs=[SMEM_SPEC, SMEM_SPEC] + [ANY_SPEC] * 10 + [VMEM_SPEC] * 3,
        out_specs=(VMEM_SPEC, VMEM_SPEC),
        scratch_shapes=[
            pltpu.VMEM((LEN_BLK, BLOCK, D), BF),
            pltpu.VMEM((LEN_BLK, BLOCK, D), BF),
            pltpu.VMEM((PAIRS, ROWS, LANES), BF),
            pltpu.VMEM((4 * PAIRS, ROWS, LANES), BF),
            pltpu.VMEM((D, D), F32),
            pltpu.VMEM((2, D), F32),
            pltpu.VMEM((GROUP, LANES, TILE), F32),
            pltpu.VMEM((PAIRS, LANES, ROWS), BF),
            pltpu.VMEM((GROUP, ROWS, LANES), F32),
            pltpu.VMEM((GROUP, ROWS, LANES), F32),
            pltpu.SMEM((LEN_BLK,), jnp.int32),
            pltpu.SemaphoreType.DMA((LEN_BLK,)),
            pltpu.SemaphoreType.DMA((LEN_BLK,)),
            pltpu.SemaphoreType.DMA((9,)),
            pltpu.VMEM((PAIRS, ROWS, LANES), BF),
        ]
        + saved_shapes(pltpu.VMEM)
        + [pltpu.VMEM((D, 4 * D), BF)],
        compiler_params=params(),
        name="backward_layer",
    )(lens, own, got_rows, got_grads, *saved, w_proj, w_out, gain_in, gain_attn)


def per_device(events, cotangent, lengths, gain_in, w_proj, gain_attn, w_out):
    own = lax.axis_index(("chip", "core")).astype(jnp.int32).reshape(1)
    lens = lengths[0]
    got_rows = lax.all_to_all(send_blocks(lens, own, events), ("chip", "core"), 0, 0, tiled=True)
    got_grads = lax.all_to_all(send_blocks(lens, own, cotangent), ("chip", "core"), 0, 0, tiled=True)
    gain_in = gain_in.reshape(1, D)
    saved = forward_layer(lens, own, got_rows, w_proj, gain_in)
    send_back, terms = backward_layer(
        lens, own, got_rows, got_grads, saved, w_proj, w_out, gain_in, gain_attn.reshape(1, D)
    )
    swap = [(0, 1), (1, 0)]
    other = lax.ppermute(terms[1], "core", swap)
    chip_sum = (terms[0].astype(F32) + other.astype(F32)).astype(BF)
    parts = lax.all_to_all(chip_sum.reshape(64, PART, LANES), ("grp", "chip"), 0, 0, tiled=True)
    total = (jnp.sum(parts.astype(F32), axis=0) * (1.0 / DEVICES)).astype(BF)
    copies = jnp.broadcast_to(total[None], (64, PART, LANES))
    mine = lax.all_to_all(copies, ("grp", "chip"), 0, 0, tiled=True).reshape(HALF, LANES)
    others = lax.ppermute(mine, "core", swap)
    came_back = lax.all_to_all(send_back, ("chip", "core"), 0, 0, tiled=True)
    d_rows = pl.pallas_call(
        home_kernel,
        out_shape=struct((LOCAL, BLOCK, D), BF),
        in_specs=[SMEM_SPEC, SMEM_SPEC, VMEM_SPEC],
        out_specs=VMEM_SPEC,
        name="take_home",
    )(lens, own, came_back)
    gain = struct((PAIRS, LANES), F32)
    grad_proj, grad_out, grad_in, grad_attn = pl.pallas_call(
        spread_kernel,
        out_shape=(struct((D, 4 * D), F32), struct((D, D), F32), gain, gain),
        in_specs=[SMEM_SPEC, VMEM_SPEC, VMEM_SPEC],
        out_specs=(VMEM_SPEC,) * 4,
        compiler_params=params(),
        name="spread_grads",
    )(own, mine, others)
    return (
        d_rows.reshape(1, LOCAL * BLOCK, D),
        grad_proj,
        grad_out,
        grad_in.reshape(D),
        grad_attn.reshape(D),
    )


def solution(mesh):
    fine = Mesh(mesh.devices.reshape(8, 8, 2), ("grp", "chip", "core"))
    rows = P("grp", ("chip", "core"), None)
    return jax.shard_map(
        per_device,
        mesh=fine,
        in_specs=(rows, rows, P("grp", None), P(), P(), P(), P()),
        out_specs=(rows, P(), P(), P(), P()),
        check_vma=False,
    )
```

```python
import jax
import jax.numpy as jnp
from jax import lax
from jax.experimental import pallas as pl
from jax.experimental.pallas import tpu as pltpu
from jax.sharding import Mesh, PartitionSpec as P

D = 512
HEADS = 8
BLOCK = 64
LEN_BLK = 16
SEQ = 16
PEERS = 16
LOCAL = 8
TILE = 256
TILES = 4
ROWS = 1024
LANES = 128
PAIRS = 4
PART = 88
HALF = 64 * PART
EPS = 1e-06
DEVICES = 128
BF = jnp.bfloat16
F32 = jnp.float32
MIB = 1024 * 1024

SMEM_SPEC = pl.BlockSpec(memory_space=pltpu.SMEM)
ANY_SPEC = pl.BlockSpec(memory_space=pl.ANY)
VMEM_SPEC = pl.BlockSpec(memory_space=pltpu.VMEM)
HBM_SPEC = pl.BlockSpec(memory_space=pltpu.HBM)


def dot(left, right):
    return lax.dot_general(left, right, (((1,), (0,)), ((), ())), preferred_element_type=F32)


def dot_cols(left, right):
    return lax.dot_general(left, right, (((1,), (1,)), ((), ())), preferred_element_type=F32)


def dot_rows(left, right):
    return lax.dot_general(left, right, (((0,), (0,)), ((), ())), preferred_element_type=F32)


def packing(len_ref):
    starts, sizes, ranks = [], [], []
    start = jnp.int32(0)
    rank = jnp.int32(0)
    held = jnp.int32(0)
    for i in range(SEQ):
        size = len_ref[i]
        fresh = held + size > LEN_BLK
        rank = jnp.where(fresh, rank + 1, rank)
        held = jnp.where(fresh, size, held + size)
        starts.append(start)
        sizes.append(size)
        ranks.append(rank)
        start = start + size
    return starts, sizes, ranks


def owners(len_ref, own):
    starts, _, ranks = packing(len_ref)
    found = []
    for k in range(LOCAL):
        block = own + PEERS * k
        owner = ranks[0]
        for i in range(1, SEQ):
            owner = jnp.where(starts[i] <= block, ranks[i], owner)
        found.append(owner)
    return found


def holdings(len_ref, own):
    starts, sizes, ranks = packing(len_ref)
    first = jnp.int32(LEN_BLK * LOCAL)
    count = jnp.int32(0)
    for i in range(SEQ):
        mine = ranks[i] == own
        first = jnp.where(mine, jnp.minimum(first, starts[i]), first)
        count = jnp.where(mine, count + sizes[i], count)
    return starts, sizes, ranks, first, count


def history_starts(hist_ref, own, starts, sizes, ranks, first):
    for j in range(LEN_BLK):
        hist_ref[j] = j
    for i in range(SEQ):

        @pl.when(ranks[i] == own)
        def _(i=i):
            begin = starts[i] - first

            def put(j, carry):
                hist_ref[j] = begin
                return carry

            lax.fori_loop(begin, begin + sizes[i], put, 0)


def send_kernel(len_ref, own_ref, rows_ref, out_ref):
    owner = owners(len_ref, own_ref[0])
    for k in range(LOCAL):
        out_ref[owner[k]] = rows_ref[k]


def home_kernel(len_ref, own_ref, back_ref, out_ref):
    owner = owners(len_ref, own_ref[0])
    for k in range(LOCAL):
        out_ref[k] = back_ref[owner[k]]


def fetch(src_ref, dst_ref, sems, first, count):
    for j in range(LEN_BLK):

        @pl.when(j < count)
        def _(j=j):
            slot = (first + j) & (PEERS - 1)
            pltpu.make_async_copy(src_ref.at[slot], dst_ref.at[j], sems.at[j]).start()


def arrive(src_ref, dst_ref, sems, count):
    for j in range(LEN_BLK):

        @pl.when(j < count)
        def _(j=j):
            pltpu.make_async_copy(src_ref.at[0], dst_ref.at[j], sems.at[j]).wait()


def tile_rows(ref, t, count):
    tile = ref[pl.ds(t * 4, 4)].reshape(TILE, D).astype(F32)
    place = lax.broadcasted_iota(jnp.int32, (TILE, D), 0) + t * TILE
    return jnp.where(place < count * BLOCK, tile, 0.0)


def normed_rows(values):
    centred = values - jnp.mean(values, axis=-1, keepdims=True)
    rstd = lax.rsqrt(jnp.mean(centred * centred, axis=-1, keepdims=True) + EPS)
    return centred * rstd, rstd


def head_masks():
    lane = lax.broadcasted_iota(jnp.int32, (1, LANES), 1)
    low = (lane < 64).astype(F32).astype(BF)
    high = (lane >= 64).astype(F32).astype(BF)
    return low, high


GROUP = 4


def rows_at(t):
    return pl.ds(pl.multiple_of(t * TILE, TILE), TILE)


def block_starts(hist_ref, t, shape, dim):
    place = lax.broadcasted_iota(jnp.int32, shape, dim)
    begin = jnp.full(shape, hist_ref[4 * t], jnp.int32)
    for b in range(1, 4):
        begin = jnp.where(place >= b * BLOCK, hist_ref[4 * t + b], begin)
    return begin * BLOCK


def key_tiles(hist_ref, i):
    low = hist_ref[4 * i] // 4
    clear = jnp.minimum((hist_ref[4 * i + 3] + 3) // 4, i)
    return low, jnp.maximum(clear, low)


def forward_kernel(
    len_ref,
    own_ref,
    got_ref,
    w_ref,
    gain_ref,
    attn_ref,
    upper_out,
    values_out,
    query_out,
    keys_out,
    slope_out,
    scaled_out,
    upper_ref,
    values_ref,
    query_ref,
    keys_ref,
    slope_ref,
    scaled_ref,
    rows_ref,
    acc_ref,
    hist_ref,
    sems,
    save_sems,
):
    own = own_ref[0]
    starts, sizes, ranks, first, count = holdings(len_ref, own)
    fetch(got_ref, rows_ref, sems, first, count)
    history_starts(hist_ref, own, starts, sizes, ranks, first)
    live = (count + 3) // 4
    arrive(got_ref, rows_ref, sems, count)

    def project(t, carry):
        normed, _ = normed_rows(tile_rows(rows_ref, t, count))
        scaled = (normed * gain_ref[...]).astype(BF)
        rows = rows_at(t)
        scaled_ref[:, rows] = scaled.T
        for quarter in range(4):
            half = 0.5 * dot(scaled, w_ref[:, quarter * D : (quarter + 1) * D])
            swing = jnp.tanh(half)
            active = half + half * swing
            slope = ((0.5 + 0.5 * swing) * (1.0 + (half - half * swing))).astype(BF)
            if quarter == 0:
                upper_ref[rows, :] = active.astype(BF)
            if quarter == 2:
                active = active * 0.0625
            active = active.astype(BF)
            for p in range(PAIRS):
                lanes = slice(p * LANES, (p + 1) * LANES)
                slope_ref[quarter * PAIRS + p, rows, :] = slope[:, lanes]
                if quarter:
                    ref = (None, values_ref, query_ref, keys_ref)[quarter]
                    ref[p, rows, :] = active[:, lanes]
        return carry

    lax.fori_loop(0, live, project, 0)

    def clear(t, carry):
        scaled_ref[:, rows_at(t)] = jnp.zeros((D, TILE), BF)
        return carry

    lax.fori_loop(live, TILES, clear, 0)

    saves = [
        pltpu.make_async_copy(src, dst, save_sems.at[n])
        for n, (src, dst) in enumerate(
            (
                (upper_ref, upper_out),
                (values_ref, values_out),
                (query_ref, query_out),
                (keys_ref, keys_out),
                (slope_ref, slope_out),
                (scaled_ref, scaled_out),
            )
        )
    ]
    for save in saves:
        save.start()

    masks = head_masks()

    def group(g, carry):
        def query_tile(i, carry):
            acc_ref[...] = jnp.zeros((GROUP, TILE, LANES), F32)

            def step(j, masked):
                if masked:
                    shape = (TILE, TILE)
                    col = lax.broadcasted_iota(jnp.int32, shape, 1) + j * TILE
                    row = lax.broadcasted_iota(jnp.int32, shape, 0) + i * TILE
                    allowed = (col <= row) & (col >= block_starts(hist_ref, i, shape, 0))
                for n in range(GROUP):
                    p = g * GROUP + n
                    query = query_ref[p, rows_at(i), :]
                    keys = keys_ref[p, rows_at(j), :]
                    values = values_ref[p, rows_at(j), :]
                    total = acc_ref[n]
                    for mask in masks:
                        half = dot_cols(query, keys * mask)
                        weights = half + half * jnp.tanh(half)
                        if masked:
                            weights = jnp.where(allowed, weights, 0.0)
                        total += dot(weights.astype(BF), values * mask)
                    acc_ref[n] = total

            low, clear_from = key_tiles(hist_ref, i)

            def masked_step(j, carry):
                step(j, True)
                return carry

            def clear_step(j, carry):
                step(j, False)
                return carry

            lax.fori_loop(low, clear_from, masked_step, 0)
            lax.fori_loop(clear_from, i, clear_step, 0)
            step(i, True)
            for n in range(GROUP):
                attn_ref[g * GROUP + n, rows_at(i), :] = acc_ref[n].astype(BF)
            return carry

        return lax.fori_loop(0, live, query_tile, carry)

    lax.fori_loop(0, PAIRS // GROUP, group, 0)
    for save in saves:
        save.wait()


def backward_kernel(
    len_ref,
    own_ref,
    got_ref,
    grads_ref,
    attn_in,
    upper_in,
    values_in,
    query_in,
    keys_in,
    slope_in,
    w_in,
    w_out_ref,
    gain_in_ref,
    gain_attn_ref,
    back_ref,
    d_hidden_out,
    out_terms_ref,
    gains_ref,
    rows_ref,
    cot_ref,
    d_attn_ref,
    d_hidden_ref,
    out_ref,
    d_query_ref,
    keys_t_ref,
    d_keys_ref,
    d_values_ref,
    hist_ref,
    row_sems,
    cot_sems,
    load_sems,
    attn_ref,
    upper_ref,
    values_ref,
    query_ref,
    keys_ref,
    slope_ref,
    w_ref,
):
    own = own_ref[0]
    starts, sizes, ranks, first, count = holdings(len_ref, own)
    fetch(grads_ref, cot_ref, cot_sems, first, count)
    early = pl.ds(0, PAIRS)
    late = pl.ds(PAIRS, 3 * PAIRS)
    loads = [
        pltpu.make_async_copy(src, dst, load_sems.at[n])
        for n, (src, dst) in enumerate(
            (
                (attn_in, attn_ref),
                (upper_in, upper_ref),
                (slope_in.at[early], slope_ref.at[early]),
                (keys_in, keys_ref),
                (query_in, query_ref),
                (values_in, values_ref),
                (slope_in.at[late], slope_ref.at[late]),
                (w_in, w_ref),
            )
        )
    ]
    for load in loads:
        load.start()
    fetch(got_ref, rows_ref, row_sems, first, count)
    history_starts(hist_ref, own, starts, sizes, ranks, first)
    live = (count + 3) // 4
    out_ref[...] = jnp.zeros((D, D), F32)
    gains_ref[...] = jnp.zeros((2, D), F32)
    arrive(grads_ref, cot_ref, cot_sems, count)
    for load in loads[:3]:
        load.wait()

    def middle(t, carry):
        rows = rows_at(t)
        attn = jnp.concatenate([attn_ref[p, rows, :] for p in range(PAIRS)], axis=1)
        normed, rstd = normed_rows(attn.astype(F32))
        upper = upper_ref[rows, :].astype(F32)
        cot = tile_rows(cot_ref, t, count).astype(BF)
        d_mixed = dot_cols(cot, w_out_ref[...])
        gained = normed * gain_attn_ref[...]
        out_ref[...] += dot_rows((gained * upper).astype(BF), cot)
        d_upper = d_mixed * gained
        pull = d_mixed * upper
        gains_ref[1:2, :] += jnp.sum(pull * normed, axis=0, keepdims=True)
        pull = pull * gain_attn_ref[...]
        d_attn = rstd * (
            pull
            - jnp.mean(pull, axis=-1, keepdims=True)
            - normed * jnp.mean(pull * normed, axis=-1, keepdims=True)
        )
        for p in range(PAIRS):
            lanes = slice(p * LANES, (p + 1) * LANES)
            d_attn_ref[p, rows, :] = d_attn[:, lanes].astype(BF)
            slope = slope_ref[p, rows, :].astype(F32)
            d_hidden_ref[p, rows, :] = (d_upper[:, lanes] * slope).astype(BF)
        return carry

    lax.fori_loop(0, live, middle, 0)

    def clear(t, carry):
        d_hidden_ref[:, rows_at(t), :] = jnp.zeros((4 * PAIRS, TILE, LANES), BF)
        return carry

    lax.fori_loop(live, TILES, clear, 0)

    masks = head_masks()
    for load in loads[3:7]:
        load.wait()

    def turn(t, carry):
        for p in range(PAIRS):
            keys_t_ref[p, :, rows_at(t)] = keys_ref[p, rows_at(t), :].T
        return carry

    lax.fori_loop(0, live, turn, 0)

    def group(g, carry):
        d_keys_ref[...] = jnp.zeros((GROUP, ROWS, LANES), F32)
        d_values_ref[...] = jnp.zeros((GROUP, ROWS, LANES), F32)

        def query_tile(i, carry):
            d_query_ref[...] = jnp.zeros((GROUP, LANES, TILE), F32)

            def step(j, masked):
                rows = rows_at(j)
                if masked:
                    shape = (TILE, TILE)
                    key_row = lax.broadcasted_iota(jnp.int32, shape, 0) + j * TILE
                    query_row = lax.broadcasted_iota(jnp.int32, shape, 1) + i * TILE
                    allowed = (key_row <= query_row) & (
                        key_row >= block_starts(hist_ref, i, shape, 1)
                    )
                for n in range(GROUP):
                    p = g * GROUP + n
                    query = query_ref[p, rows_at(i), :]
                    d_attn = d_attn_ref[p, rows_at(i), :]
                    keys = keys_ref[p, rows, :]
                    values = values_ref[p, rows, :]
                    d_keys = d_keys_ref[n, rows, :]
                    d_values = d_values_ref[n, rows, :]
                    for h, mask in enumerate(masks):
                        masked_keys = keys * mask
                        half = dot_cols(masked_keys, query)
                        swing = jnp.tanh(half)
                        bend = half * swing
                        weights = half + bend
                        slope = (1.0 + swing) * ((1.0 + half) - bend)
                        grad = dot_cols(values * mask, d_attn) * slope
                        if masked:
                            weights = jnp.where(allowed, weights, 0.0)
                            grad = jnp.where(allowed, grad, 0.0)
                        grad = grad.astype(BF)
                        d_values += dot(weights.astype(BF), d_attn * mask)
                        d_keys += dot(grad, query * mask)
                        head_rows = slice(h * 64, h * 64 + 64)
                        d_query_ref[n, head_rows, :] += dot(keys_t_ref[p, head_rows, rows], grad)
                    d_keys_ref[n, rows, :] = d_keys
                    d_values_ref[n, rows, :] = d_values

            low, clear_from = key_tiles(hist_ref, i)

            def masked_step(j, carry):
                step(j, True)
                return carry

            def clear_step(j, carry):
                step(j, False)
                return carry

            lax.fori_loop(low, clear_from, masked_step, 0)
            lax.fori_loop(clear_from, i, clear_step, 0)
            step(i, True)
            for n in range(GROUP):
                place = 2 * PAIRS + g * GROUP + n
                slope = slope_ref[place, rows_at(i), :].astype(F32)
                d_hidden_ref[place, rows_at(i), :] = (d_query_ref[n].T * 0.0625 * slope).astype(BF)
            return carry

        lax.fori_loop(0, live, query_tile, 0)

        def finish(t, carry):
            rows = rows_at(t)
            for n in range(GROUP):
                for quarter, ref in ((1, d_values_ref), (3, d_keys_ref)):
                    place = quarter * PAIRS + g * GROUP + n
                    slope = slope_ref[place, rows, :].astype(F32)
                    d_hidden_ref[place, rows, :] = (ref[n, rows, :] * slope).astype(BF)
            return carry

        lax.fori_loop(0, live, finish, 0)
        return carry

    lax.fori_loop(0, PAIRS // GROUP, group, 0)

    save = pltpu.make_async_copy(d_hidden_ref, d_hidden_out, load_sems.at[8])
    save.start()
    arrive(got_ref, rows_ref, row_sems, count)
    for load in loads[7:]:
        load.wait()

    def final(t, carry):
        rows = rows_at(t)
        normed, rstd = normed_rows(tile_rows(rows_ref, t, count))
        d_scaled = jnp.zeros((TILE, D), F32)
        for c in range(8):
            part = jnp.concatenate(
                [d_hidden_ref[2 * c, rows, :], d_hidden_ref[2 * c + 1, rows, :]], axis=1
            )
            d_scaled += dot_cols(part, w_ref[:, c * 256 : (c + 1) * 256])
        gains_ref[0:1, :] += jnp.sum(d_scaled * normed, axis=0, keepdims=True)
        pull = d_scaled * gain_in_ref[...]
        d_rows = rstd * (
            pull
            - jnp.mean(pull, axis=-1, keepdims=True)
            - normed * jnp.mean(pull * normed, axis=-1, keepdims=True)
        )
        d_rows = (d_rows + tile_rows(cot_ref, t, count)).astype(BF)
        for b in range(4):
            slot = (first + t * 4 + b) & (PEERS - 1)
            back_ref[slot] = d_rows[b * BLOCK : (b + 1) * BLOCK, :]
        return carry

    lax.fori_loop(0, live, final, 0)

    for p in range(PAIRS):
        out_terms_ref[p] = out_ref[:, p * LANES : (p + 1) * LANES].astype(BF)
    save.wait()


def terms_kernel(
    own_ref,
    d_hidden_in,
    scaled_in,
    out_terms_ref,
    gains_ref,
    keep_ref,
    send_ref,
    d_hidden_ref,
    scaled_ref,
    sems,
):
    core = own_ref[0] & 1
    loads = [pltpu.make_async_copy(scaled_in, scaled_ref, sems.at[8])]
    for c in range(8):
        part = pl.ds(2 * c, 2)
        loads.append(
            pltpu.make_async_copy(d_hidden_in.at[part], d_hidden_ref.at[part], sems.at[c])
        )
    for load in loads:
        load.start()

    def put(half, rows, values):
        values = values.astype(BF)

        @pl.when(core == half)
        def _():
            keep_ref[rows, :] = values

        @pl.when(core != half)
        def _():
            send_ref[rows, :] = values

    def put_piece(piece, values):
        half, place = divmod(piece, 10)
        put(half, pl.ds(place * D, D), values)

    for p in range(PAIRS):
        put_piece(16 + p, out_terms_ref[p])
    for half in range(2):
        tail = jnp.concatenate(
            [gains_ref[half : half + 1, p * LANES : (p + 1) * LANES] for p in range(PAIRS)]
            + [jnp.zeros((HALF - 10 * D - PAIRS, LANES), F32)],
            axis=0,
        )
        put(half, pl.ds(10 * D, HALF - 10 * D), tail)
    loads[0].wait()
    for c in range(8):
        loads[1 + c].wait()
        part = jnp.concatenate([d_hidden_ref[2 * c], d_hidden_ref[2 * c + 1]], axis=1)
        term = dot(scaled_ref[...], part)
        put_piece(2 * c, term[:, :LANES])
        put_piece(2 * c + 1, term[:, LANES:])


def spread_kernel(own_ref, mine_ref, other_ref, proj_ref, out_ref, gain_in_ref, gain_attn_ref):
    core = own_ref[0] & 1

    def write(low_ref, high_ref):
        for piece in range(20):
            half, place = divmod(piece, 10)
            part = (low_ref, high_ref)[half][place * D : (place + 1) * D, :].astype(F32)
            if piece < 16:
                proj_ref[:, piece * LANES : (piece + 1) * LANES] = part
            else:
                out_ref[:, (piece - 16) * LANES : (piece - 15) * LANES] = part
        gain_in_ref[...] = low_ref[10 * D : 10 * D + 16, :].astype(F32)[:PAIRS]
        gain_attn_ref[...] = high_ref[10 * D : 10 * D + 16, :].astype(F32)[:PAIRS]

    @pl.when(core == 0)
    def _():
        write(mine_ref, other_ref)

    @pl.when(core == 1)
    def _():
        write(other_ref, mine_ref)


def struct(shape, dtype):
    return jax.ShapeDtypeStruct(shape, dtype)


def params(mebibytes):
    return pltpu.CompilerParams(vmem_limit_bytes=mebibytes * MIB)


def send_blocks(lens, own, rows):
    return pl.pallas_call(
        send_kernel,
        out_shape=struct((PEERS, BLOCK, D), BF),
        in_specs=[SMEM_SPEC, SMEM_SPEC, VMEM_SPEC],
        out_specs=VMEM_SPEC,
        name="send_blocks",
    )(lens, own, rows.reshape(LOCAL, BLOCK, D))


def saved_shapes(make):
    pairs = make((PAIRS, ROWS, LANES), BF)
    wide = make((ROWS, D), BF)
    tall = make((D, ROWS), BF)
    return [wide, pairs, pairs, pairs, make((4 * PAIRS, ROWS, LANES), BF), tall]


def forward_layer(lens, own, got_rows, w_proj, gain_in):
    return pl.pallas_call(
        forward_kernel,
        out_shape=[struct((PAIRS, ROWS, LANES), BF)] + saved_shapes(struct),
        in_specs=[SMEM_SPEC, SMEM_SPEC, ANY_SPEC, VMEM_SPEC, VMEM_SPEC],
        out_specs=[VMEM_SPEC] + [HBM_SPEC] * 6,
        scratch_shapes=saved_shapes(pltpu.VMEM)
        + [
            pltpu.VMEM((LEN_BLK, BLOCK, D), BF),
            pltpu.VMEM((GROUP, TILE, LANES), F32),
            pltpu.SMEM((LEN_BLK,), jnp.int32),
            pltpu.SemaphoreType.DMA((LEN_BLK,)),
            pltpu.SemaphoreType.DMA((6,)),
        ],
        compiler_params=params(52),
        name="forward_layer",
    )(lens, own, got_rows, w_proj, gain_in)


def backward_layer(lens, own, got_rows, got_grads, saved, w_proj, w_out, gain_in, gain_attn):
    return pl.pallas_call(
        backward_kernel,
        out_shape=(
            struct((PEERS, BLOCK, D), BF),
            struct((4 * PAIRS, ROWS, LANES), BF),
            struct((PAIRS, D, LANES), BF),
            struct((2, D), F32),
        ),
        in_specs=[SMEM_SPEC, SMEM_SPEC] + [ANY_SPEC] * 3 + [HBM_SPEC] * 6 + [VMEM_SPEC] * 3,
        out_specs=(VMEM_SPEC, HBM_SPEC, VMEM_SPEC, VMEM_SPEC),
        scratch_shapes=[
            pltpu.VMEM((LEN_BLK, BLOCK, D), BF),
            pltpu.VMEM((LEN_BLK, BLOCK, D), BF),
            pltpu.VMEM((PAIRS, ROWS, LANES), BF),
            pltpu.VMEM((4 * PAIRS, ROWS, LANES), BF),
            pltpu.VMEM((D, D), F32),
            pltpu.VMEM((GROUP, LANES, TILE), F32),
            pltpu.VMEM((PAIRS, LANES, ROWS), BF),
            pltpu.VMEM((GROUP, ROWS, LANES), F32),
            pltpu.VMEM((GROUP, ROWS, LANES), F32),
            pltpu.SMEM((LEN_BLK,), jnp.int32),
            pltpu.SemaphoreType.DMA((LEN_BLK,)),
            pltpu.SemaphoreType.DMA((LEN_BLK,)),
            pltpu.SemaphoreType.DMA((9,)),
            pltpu.VMEM((PAIRS, ROWS, LANES), BF),
        ]
        + saved_shapes(pltpu.VMEM)[:5]
        + [pltpu.VMEM((D, 4 * D), BF)],
        compiler_params=params(52),
        name="backward_layer",
    )(lens, own, got_rows, got_grads, *saved[:6], w_proj, w_out, gain_in, gain_attn)


def gradient_terms(own, d_hidden, scaled, out_terms, gains):
    half = struct((HALF, LANES), BF)
    return pl.pallas_call(
        terms_kernel,
        out_shape=(half, half),
        in_specs=[SMEM_SPEC, HBM_SPEC, HBM_SPEC, VMEM_SPEC, VMEM_SPEC],
        out_specs=(VMEM_SPEC, VMEM_SPEC),
        scratch_shapes=[
            pltpu.VMEM((4 * PAIRS, ROWS, LANES), BF),
            pltpu.VMEM((D, ROWS), BF),
            pltpu.SemaphoreType.DMA((9,)),
        ],
        compiler_params=params(52),
        cost_estimate=pl.CostEstimate(
            flops=8 * ROWS * D * D, transcendentals=0, bytes_accessed=8 * MIB
        ),
        name="gradient_terms",
    )(own, d_hidden, scaled, out_terms, gains)


def per_device(events, cotangent, lengths, gain_in, w_proj, gain_attn, w_out):
    own = lax.axis_index(("chip", "core")).astype(jnp.int32).reshape(1)
    lens = lengths[0]
    got_rows = lax.all_to_all(send_blocks(lens, own, events), ("chip", "core"), 0, 0, tiled=True)
    got_grads = lax.all_to_all(send_blocks(lens, own, cotangent), ("chip", "core"), 0, 0, tiled=True)
    gain_in = gain_in.reshape(1, D)
    saved = forward_layer(lens, own, got_rows, w_proj, gain_in)
    send_back, d_hidden, out_terms, gains = backward_layer(
        lens, own, got_rows, got_grads, saved, w_proj, w_out, gain_in, gain_attn.reshape(1, D)
    )
    came_back = lax.all_to_all(send_back, ("chip", "core"), 0, 0, tiled=True)
    keep, send = gradient_terms(own, d_hidden, saved[6], out_terms, gains)
    send, came_back = lax.optimization_barrier((send, came_back))
    swap = [(0, 1), (1, 0)]
    other = lax.ppermute(send, "core", swap)
    chip_sum = (keep.astype(F32) + other.astype(F32)).astype(BF)
    parts = lax.all_to_all(chip_sum.reshape(64, PART, LANES), ("grp", "chip"), 0, 0, tiled=True)
    total = (jnp.sum(parts.astype(F32), axis=0) * (1.0 / DEVICES)).astype(BF)
    copies = jnp.broadcast_to(total[None], (64, PART, LANES))
    mine = lax.all_to_all(copies, ("grp", "chip"), 0, 0, tiled=True).reshape(HALF, LANES)
    others = lax.ppermute(mine, "core", swap)
    d_rows = pl.pallas_call(
        home_kernel,
        out_shape=struct((LOCAL, BLOCK, D), BF),
        in_specs=[SMEM_SPEC, SMEM_SPEC, VMEM_SPEC],
        out_specs=VMEM_SPEC,
        name="take_home",
    )(lens, own, came_back)
    gain = struct((PAIRS, LANES), F32)
    grad_proj, grad_out, grad_in, grad_attn = pl.pallas_call(
        spread_kernel,
        out_shape=(struct((D, 4 * D), F32), struct((D, D), F32), gain, gain),
        in_specs=[SMEM_SPEC, VMEM_SPEC, VMEM_SPEC],
        out_specs=(VMEM_SPEC,) * 4,
        compiler_params=params(16),
        name="spread_grads",
    )(own, mine, others)
    return (
        d_rows.reshape(1, LOCAL * BLOCK, D),
        grad_proj,
        grad_out,
        grad_in.reshape(D),
        grad_attn.reshape(D),
    )


def solution(mesh):
    fine = Mesh(mesh.devices.reshape(8, 8, 2), ("grp", "chip", "core"))
    rows = P("grp", ("chip", "core"), None)
    return jax.shard_map(
        per_device,
        mesh=fine,
        in_specs=(rows, rows, P("grp", None), P(), P(), P(), P()),
        out_specs=(rows, P(), P(), P(), P()),
        check_vma=False,
    )
```

```python
import jax
import jax.numpy as jnp
from jax import lax
from jax.experimental import pallas as pl
from jax.experimental.pallas import tpu as pltpu
from jax.sharding import Mesh, PartitionSpec as P

D = 512
HEADS = 8
BLOCK = 64
LEN_BLK = 16
SEQ = 16
PEERS = 16
LOCAL = 8
TILE = 256
TILES = 4
ROWS = 1024
LANES = 128
PAIRS = 4
PART = 88
HALF = 64 * PART
EPS = 1e-06
DEVICES = 128
BF = jnp.bfloat16
F32 = jnp.float32
MIB = 1024 * 1024

SMEM_SPEC = pl.BlockSpec(memory_space=pltpu.SMEM)
ANY_SPEC = pl.BlockSpec(memory_space=pl.ANY)
VMEM_SPEC = pl.BlockSpec(memory_space=pltpu.VMEM)
HBM_SPEC = pl.BlockSpec(memory_space=pltpu.HBM)


def dot(left, right):
    return lax.dot_general(left, right, (((1,), (0,)), ((), ())), preferred_element_type=F32)


def dot_cols(left, right):
    return lax.dot_general(left, right, (((1,), (1,)), ((), ())), preferred_element_type=F32)


def dot_rows(left, right):
    return lax.dot_general(left, right, (((0,), (0,)), ((), ())), preferred_element_type=F32)


def packing(len_ref):
    starts, sizes, ranks = [], [], []
    start = jnp.int32(0)
    rank = jnp.int32(0)
    held = jnp.int32(0)
    for i in range(SEQ):
        size = len_ref[i]
        fresh = held + size > LEN_BLK
        rank = jnp.where(fresh, rank + 1, rank)
        held = jnp.where(fresh, size, held + size)
        starts.append(start)
        sizes.append(size)
        ranks.append(rank)
        start = start + size
    return starts, sizes, ranks


def owners(len_ref, own):
    starts, _, ranks = packing(len_ref)
    found = []
    for k in range(LOCAL):
        block = own + PEERS * k
        owner = ranks[0]
        for i in range(1, SEQ):
            owner = jnp.where(starts[i] <= block, ranks[i], owner)
        found.append(owner)
    return found


def holdings(len_ref, own):
    starts, sizes, ranks = packing(len_ref)
    first = jnp.int32(LEN_BLK * LOCAL)
    count = jnp.int32(0)
    for i in range(SEQ):
        mine = ranks[i] == own
        first = jnp.where(mine, jnp.minimum(first, starts[i]), first)
        count = jnp.where(mine, count + sizes[i], count)
    return starts, sizes, ranks, first, count


def history_starts(hist_ref, own, starts, sizes, ranks, first):
    for j in range(LEN_BLK):
        hist_ref[j] = j
    for i in range(SEQ):

        @pl.when(ranks[i] == own)
        def _(i=i):
            begin = starts[i] - first

            def put(j, carry):
                hist_ref[j] = begin
                return carry

            lax.fori_loop(begin, begin + sizes[i], put, 0)


def send_kernel(len_ref, own_ref, rows_ref, out_ref, held_ref, sems):
    load = pltpu.make_async_copy(rows_ref, held_ref, sems.at[LOCAL])
    load.start()
    owner = owners(len_ref, own_ref[0])
    copies = [
        pltpu.make_async_copy(held_ref.at[k], out_ref.at[owner[k]], sems.at[k])
        for k in range(LOCAL)
    ]
    load.wait()
    for copy in copies:
        copy.start()
    for copy in copies:
        copy.wait()


def home_kernel(len_ref, own_ref, back_ref, out_ref):
    owner = owners(len_ref, own_ref[0])
    for k in range(LOCAL):
        out_ref[k] = back_ref[owner[k]]


def fetch(src_ref, dst_ref, sems, first, count):
    for j in range(LEN_BLK):

        @pl.when(j < count)
        def _(j=j):
            slot = (first + j) & (PEERS - 1)
            pltpu.make_async_copy(src_ref.at[slot], dst_ref.at[j], sems.at[j]).start()


def arrive(src_ref, dst_ref, sems, count):
    for j in range(LEN_BLK):

        @pl.when(j < count)
        def _(j=j):
            pltpu.make_async_copy(src_ref.at[0], dst_ref.at[j], sems.at[j]).wait()


def tile_rows(ref, t, count):
    tile = ref[pl.ds(t * 4, 4)].reshape(TILE, D).astype(F32)
    place = lax.broadcasted_iota(jnp.int32, (TILE, D), 0) + t * TILE
    return jnp.where(place < count * BLOCK, tile, 0.0)


def normed_rows(values):
    centred = values - jnp.mean(values, axis=-1, keepdims=True)
    rstd = lax.rsqrt(jnp.mean(centred * centred, axis=-1, keepdims=True) + EPS)
    return centred * rstd, rstd


def head_masks():
    lane = lax.broadcasted_iota(jnp.int32, (1, LANES), 1)
    low = (lane < 64).astype(F32).astype(BF)
    high = (lane >= 64).astype(F32).astype(BF)
    return low, high


GROUP = 4


def rows_at(t):
    return pl.ds(pl.multiple_of(t * TILE, TILE), TILE)


def block_starts(hist_ref, t, shape, dim):
    place = lax.broadcasted_iota(jnp.int32, shape, dim)
    begin = jnp.full(shape, hist_ref[4 * t], jnp.int32)
    for b in range(1, 4):
        begin = jnp.where(place >= b * BLOCK, hist_ref[4 * t + b], begin)
    return begin * BLOCK


def key_tiles(hist_ref, i):
    low = hist_ref[4 * i] // 4
    clear = jnp.minimum((hist_ref[4 * i + 3] + 3) // 4, i)
    return low, jnp.maximum(clear, low)


def forward_kernel(
    len_ref,
    own_ref,
    got_ref,
    w_ref,
    gain_ref,
    attn_ref,
    upper_out,
    values_out,
    query_out,
    keys_out,
    slope_out,
    scaled_out,
    upper_ref,
    values_ref,
    query_ref,
    keys_ref,
    slope_ref,
    scaled_ref,
    rows_ref,
    acc_ref,
    hist_ref,
    sems,
    save_sems,
):
    own = own_ref[0]
    starts, sizes, ranks, first, count = holdings(len_ref, own)
    fetch(got_ref, rows_ref, sems, first, count)
    history_starts(hist_ref, own, starts, sizes, ranks, first)
    live = (count + 3) // 4
    arrive(got_ref, rows_ref, sems, count)

    def project(t, carry):
        normed, _ = normed_rows(tile_rows(rows_ref, t, count))
        scaled = (normed * gain_ref[...]).astype(BF)
        rows = rows_at(t)
        scaled_ref[:, rows] = scaled.T
        for quarter in range(4):
            half = 0.5 * dot(scaled, w_ref[:, quarter * D : (quarter + 1) * D])
            swing = jnp.tanh(half)
            active = half + half * swing
            slope = ((0.5 + 0.5 * swing) * (1.0 + (half - half * swing))).astype(BF)
            if quarter == 0:
                upper_ref[rows, :] = active.astype(BF)
            if quarter == 2:
                active = active * 0.0625
            active = active.astype(BF)
            for p in range(PAIRS):
                lanes = slice(p * LANES, (p + 1) * LANES)
                slope_ref[quarter * PAIRS + p, rows, :] = slope[:, lanes]
                if quarter:
                    ref = (None, values_ref, query_ref, keys_ref)[quarter]
                    ref[p, rows, :] = active[:, lanes]
        return carry

    lax.fori_loop(0, live, project, 0)

    def clear(t, carry):
        scaled_ref[:, rows_at(t)] = jnp.zeros((D, TILE), BF)
        return carry

    lax.fori_loop(live, TILES, clear, 0)

    saves = [
        pltpu.make_async_copy(src, dst, save_sems.at[n])
        for n, (src, dst) in enumerate(
            (
                (upper_ref, upper_out),
                (values_ref, values_out),
                (query_ref, query_out),
                (keys_ref, keys_out),
                (slope_ref, slope_out),
                (scaled_ref, scaled_out),
            )
        )
    ]
    for save in saves:
        save.start()

    masks = head_masks()

    def group(g, carry):
        def query_tile(i, carry):
            acc_ref[...] = jnp.zeros((GROUP, TILE, LANES), F32)

            def step(j, masked):
                if masked:
                    shape = (TILE, TILE)
                    col = lax.broadcasted_iota(jnp.int32, shape, 1) + j * TILE
                    row = lax.broadcasted_iota(jnp.int32, shape, 0) + i * TILE
                    allowed = (col <= row) & (col >= block_starts(hist_ref, i, shape, 0))
                for n in range(GROUP):
                    p = g * GROUP + n
                    query = query_ref[p, rows_at(i), :]
                    keys = keys_ref[p, rows_at(j), :]
                    values = values_ref[p, rows_at(j), :]
                    total = acc_ref[n]
                    for mask in masks:
                        half = dot_cols(query, keys * mask)
                        weights = half + half * jnp.tanh(half)
                        if masked:
                            weights = jnp.where(allowed, weights, 0.0)
                        total += dot(weights.astype(BF), values * mask)
                    acc_ref[n] = total

            low, clear_from = key_tiles(hist_ref, i)

            def masked_step(j, carry):
                step(j, True)
                return carry

            def clear_step(j, carry):
                step(j, False)
                return carry

            lax.fori_loop(low, clear_from, masked_step, 0)
            lax.fori_loop(clear_from, i, clear_step, 0)
            step(i, True)
            for n in range(GROUP):
                attn_ref[g * GROUP + n, rows_at(i), :] = acc_ref[n].astype(BF)
            return carry

        return lax.fori_loop(0, live, query_tile, carry)

    lax.fori_loop(0, PAIRS // GROUP, group, 0)
    for save in saves:
        save.wait()


def backward_kernel(
    len_ref,
    own_ref,
    got_ref,
    grads_ref,
    attn_in,
    upper_in,
    values_in,
    query_in,
    keys_in,
    slope_in,
    w_in,
    w_out_ref,
    gain_in_ref,
    gain_attn_ref,
    back_ref,
    d_hidden_out,
    mixed_out,
    cot_out,
    gains_ref,
    rows_ref,
    cot_ref,
    d_attn_ref,
    d_hidden_ref,
    mixed_ref,
    cot_rows_ref,
    d_query_ref,
    keys_t_ref,
    d_keys_ref,
    d_values_ref,
    hist_ref,
    row_sems,
    cot_sems,
    load_sems,
    attn_ref,
    upper_ref,
    values_ref,
    query_ref,
    keys_ref,
    slope_ref,
    w_ref,
):
    own = own_ref[0]
    starts, sizes, ranks, first, count = holdings(len_ref, own)
    fetch(grads_ref, cot_ref, cot_sems, first, count)
    early = pl.ds(0, PAIRS)
    late = pl.ds(PAIRS, 3 * PAIRS)
    loads = [
        pltpu.make_async_copy(src, dst, load_sems.at[n])
        for n, (src, dst) in enumerate(
            (
                (attn_in, attn_ref),
                (upper_in, upper_ref),
                (slope_in.at[early], slope_ref.at[early]),
                (keys_in, keys_ref),
                (query_in, query_ref),
                (values_in, values_ref),
                (slope_in.at[late], slope_ref.at[late]),
                (w_in, w_ref),
            )
        )
    ]
    for load in loads:
        load.start()
    fetch(got_ref, rows_ref, row_sems, first, count)
    history_starts(hist_ref, own, starts, sizes, ranks, first)
    live = (count + 3) // 4
    gains_ref[...] = jnp.zeros((2, D), F32)
    arrive(grads_ref, cot_ref, cot_sems, count)
    for load in loads[:3]:
        load.wait()

    def middle(t, carry):
        rows = rows_at(t)
        attn = jnp.concatenate([attn_ref[p, rows, :] for p in range(PAIRS)], axis=1)
        normed, rstd = normed_rows(attn.astype(F32))
        upper = upper_ref[rows, :].astype(F32)
        cot = tile_rows(cot_ref, t, count).astype(BF)
        d_mixed = dot_cols(cot, w_out_ref[...])
        gained = normed * gain_attn_ref[...]
        mixed_ref[:, rows] = (gained * upper).astype(BF).T
        cot_rows_ref[rows, :] = cot
        d_upper = d_mixed * gained
        pull = d_mixed * upper
        gains_ref[1:2, :] += jnp.sum(pull * normed, axis=0, keepdims=True)
        pull = pull * gain_attn_ref[...]
        d_attn = rstd * (
            pull
            - jnp.mean(pull, axis=-1, keepdims=True)
            - normed * jnp.mean(pull * normed, axis=-1, keepdims=True)
        )
        for p in range(PAIRS):
            lanes = slice(p * LANES, (p + 1) * LANES)
            d_attn_ref[p, rows, :] = d_attn[:, lanes].astype(BF)
            slope = slope_ref[p, rows, :].astype(F32)
            d_hidden_ref[p, rows, :] = (d_upper[:, lanes] * slope).astype(BF)
        return carry

    lax.fori_loop(0, live, middle, 0)

    def clear(t, carry):
        d_hidden_ref[:, rows_at(t), :] = jnp.zeros((4 * PAIRS, TILE, LANES), BF)
        mixed_ref[:, rows_at(t)] = jnp.zeros((D, TILE), BF)
        cot_rows_ref[rows_at(t), :] = jnp.zeros((TILE, D), BF)
        return carry

    lax.fori_loop(live, TILES, clear, 0)
    saves = [
        pltpu.make_async_copy(mixed_ref, mixed_out, load_sems.at[9]),
        pltpu.make_async_copy(cot_rows_ref, cot_out, load_sems.at[10]),
    ]
    for save in saves:
        save.start()

    masks = head_masks()
    for load in loads[3:7]:
        load.wait()

    def turn(t, carry):
        for p in range(PAIRS):
            keys_t_ref[p, :, rows_at(t)] = keys_ref[p, rows_at(t), :].T
        return carry

    lax.fori_loop(0, live, turn, 0)

    def group(g, carry):
        d_keys_ref[...] = jnp.zeros((GROUP, ROWS, LANES), F32)
        d_values_ref[...] = jnp.zeros((GROUP, ROWS, LANES), F32)

        def query_tile(i, carry):
            d_query_ref[...] = jnp.zeros((GROUP, LANES, TILE), F32)

            def step(j, masked):
                rows = rows_at(j)
                if masked:
                    shape = (TILE, TILE)
                    key_row = lax.broadcasted_iota(jnp.int32, shape, 0) + j * TILE
                    query_row = lax.broadcasted_iota(jnp.int32, shape, 1) + i * TILE
                    allowed = (key_row <= query_row) & (
                        key_row >= block_starts(hist_ref, i, shape, 1)
                    )
                for n in range(GROUP):
                    p = g * GROUP + n
                    query = query_ref[p, rows_at(i), :]
                    d_attn = d_attn_ref[p, rows_at(i), :]
                    keys = keys_ref[p, rows, :]
                    values = values_ref[p, rows, :]
                    d_keys = d_keys_ref[n, rows, :]
                    d_values = d_values_ref[n, rows, :]
                    for h, mask in enumerate(masks):
                        masked_keys = keys * mask
                        half = dot_cols(masked_keys, query)
                        swing = jnp.tanh(half)
                        bend = half * swing
                        weights = half + bend
                        slope = (1.0 + swing) * ((1.0 + half) - bend)
                        grad = dot_cols(values * mask, d_attn) * slope
                        if masked:
                            weights = jnp.where(allowed, weights, 0.0)
                            grad = jnp.where(allowed, grad, 0.0)
                        grad = grad.astype(BF)
                        d_values += dot(weights.astype(BF), d_attn * mask)
                        d_keys += dot(grad, query * mask)
                        head_rows = slice(h * 64, h * 64 + 64)
                        d_query_ref[n, head_rows, :] += dot(keys_t_ref[p, head_rows, rows], grad)
                    d_keys_ref[n, rows, :] = d_keys
                    d_values_ref[n, rows, :] = d_values

            low, clear_from = key_tiles(hist_ref, i)

            def masked_step(j, carry):
                step(j, True)
                return carry

            def clear_step(j, carry):
                step(j, False)
                return carry

            lax.fori_loop(low, clear_from, masked_step, 0)
            lax.fori_loop(clear_from, i, clear_step, 0)
            step(i, True)
            for n in range(GROUP):
                place = 2 * PAIRS + g * GROUP + n
                slope = slope_ref[place, rows_at(i), :].astype(F32)
                d_hidden_ref[place, rows_at(i), :] = (d_query_ref[n].T * 0.0625 * slope).astype(BF)
            return carry

        lax.fori_loop(0, live, query_tile, 0)

        def finish(t, carry):
            rows = rows_at(t)
            for n in range(GROUP):
                for quarter, ref in ((1, d_values_ref), (3, d_keys_ref)):
                    place = quarter * PAIRS + g * GROUP + n
                    slope = slope_ref[place, rows, :].astype(F32)
                    d_hidden_ref[place, rows, :] = (ref[n, rows, :] * slope).astype(BF)
            return carry

        lax.fori_loop(0, live, finish, 0)
        return carry

    lax.fori_loop(0, PAIRS // GROUP, group, 0)

    saves.append(pltpu.make_async_copy(d_hidden_ref, d_hidden_out, load_sems.at[8]))
    saves[-1].start()
    arrive(got_ref, rows_ref, row_sems, count)
    for load in loads[7:]:
        load.wait()

    def final(t, carry):
        rows = rows_at(t)
        normed, rstd = normed_rows(tile_rows(rows_ref, t, count))
        d_scaled = jnp.zeros((TILE, D), F32)
        for c in range(8):
            part = jnp.concatenate(
                [d_hidden_ref[2 * c, rows, :], d_hidden_ref[2 * c + 1, rows, :]], axis=1
            )
            d_scaled += dot_cols(part, w_ref[:, c * 256 : (c + 1) * 256])
        gains_ref[0:1, :] += jnp.sum(d_scaled * normed, axis=0, keepdims=True)
        pull = d_scaled * gain_in_ref[...]
        d_rows = rstd * (
            pull
            - jnp.mean(pull, axis=-1, keepdims=True)
            - normed * jnp.mean(pull * normed, axis=-1, keepdims=True)
        )
        d_rows = (d_rows + cot_rows_ref[rows, :].astype(F32)).astype(BF)
        for b in range(4):
            slot = (first + t * 4 + b) & (PEERS - 1)
            back_ref[slot] = d_rows[b * BLOCK : (b + 1) * BLOCK, :]
        return carry

    lax.fori_loop(0, live, final, 0)

    for save in saves:
        save.wait()


def terms_kernel(
    own_ref,
    d_hidden_in,
    scaled_in,
    mixed_in,
    cot_in,
    gains_ref,
    keep_ref,
    send_ref,
    d_hidden_ref,
    scaled_ref,
    mixed_ref,
    cot_ref,
    sems,
):
    core = own_ref[0] & 1
    loads = [
        pltpu.make_async_copy(mixed_in, mixed_ref, sems.at[9]),
        pltpu.make_async_copy(cot_in, cot_ref, sems.at[10]),
        pltpu.make_async_copy(scaled_in, scaled_ref, sems.at[8]),
    ]
    for c in range(8):
        part = pl.ds(2 * c, 2)
        loads.append(
            pltpu.make_async_copy(d_hidden_in.at[part], d_hidden_ref.at[part], sems.at[c])
        )
    for load in loads:
        load.start()

    def put(half, rows, values):
        values = values.astype(BF)

        @pl.when(core == half)
        def _():
            keep_ref[rows, :] = values

        @pl.when(core != half)
        def _():
            send_ref[rows, :] = values

    def put_piece(piece, values):
        half, place = divmod(piece, 10)
        put(half, pl.ds(place * D, D), values)

    for half in range(2):
        tail = jnp.concatenate(
            [gains_ref[half : half + 1, p * LANES : (p + 1) * LANES] for p in range(PAIRS)]
            + [jnp.zeros((HALF - 10 * D - PAIRS, LANES), F32)],
            axis=0,
        )
        put(half, pl.ds(10 * D, HALF - 10 * D), tail)
    loads[0].wait()
    loads[1].wait()
    for c in range(2):
        term = dot(mixed_ref[...], cot_ref[:, c * 256 : (c + 1) * 256])
        put_piece(16 + 2 * c, term[:, :LANES])
        put_piece(17 + 2 * c, term[:, LANES:])
    loads[2].wait()
    for c in range(8):
        loads[3 + c].wait()
        part = jnp.concatenate([d_hidden_ref[2 * c], d_hidden_ref[2 * c + 1]], axis=1)
        term = dot(scaled_ref[...], part)
        put_piece(2 * c, term[:, :LANES])
        put_piece(2 * c + 1, term[:, LANES:])


def spread_kernel(
    own_ref,
    mine_ref,
    other_ref,
    proj_ref,
    out_ref,
    gain_in_ref,
    gain_attn_ref,
    wide_ref,
    sems,
):
    core = own_ref[0] & 1

    def copy(piece):
        if piece < 16:
            target = proj_ref.at[:, pl.ds(piece * LANES, LANES)]
        else:
            target = out_ref.at[:, pl.ds((piece - 16) * LANES, LANES)]
        return pltpu.make_async_copy(wide_ref.at[piece], target, sems.at[piece])

    def write(low_ref, high_ref):
        for piece in range(20):
            half, place = divmod(piece, 10)
            wide_ref[piece] = (low_ref, high_ref)[half][place * D : (place + 1) * D, :].astype(F32)
            copy(piece).start()
        gain_in_ref[...] = low_ref[10 * D : 10 * D + 16, :].astype(F32)[:PAIRS]
        gain_attn_ref[...] = high_ref[10 * D : 10 * D + 16, :].astype(F32)[:PAIRS]

    @pl.when(core == 0)
    def _():
        write(mine_ref, other_ref)

    @pl.when(core == 1)
    def _():
        write(other_ref, mine_ref)

    for piece in range(20):
        copy(piece).wait()


def struct(shape, dtype):
    return jax.ShapeDtypeStruct(shape, dtype)


def params(mebibytes):
    return pltpu.CompilerParams(vmem_limit_bytes=mebibytes * MIB)


def send_blocks(lens, own, rows):
    return pl.pallas_call(
        send_kernel,
        out_shape=struct((PEERS, BLOCK, D), BF),
        in_specs=[SMEM_SPEC, SMEM_SPEC, ANY_SPEC],
        out_specs=ANY_SPEC,
        scratch_shapes=[
            pltpu.VMEM((LOCAL, BLOCK, D), BF),
            pltpu.SemaphoreType.DMA((LOCAL + 1,)),
        ],
        name="send_blocks",
    )(lens, own, rows.reshape(LOCAL, BLOCK, D))


def saved_shapes(make):
    pairs = make((PAIRS, ROWS, LANES), BF)
    wide = make((ROWS, D), BF)
    tall = make((D, ROWS), BF)
    return [wide, pairs, pairs, pairs, make((4 * PAIRS, ROWS, LANES), BF), tall]


def forward_layer(lens, own, got_rows, w_proj, gain_in):
    return pl.pallas_call(
        forward_kernel,
        out_shape=[pltpu.HBM((PAIRS, ROWS, LANES), BF)] + saved_shapes(pltpu.HBM),
        in_specs=[SMEM_SPEC, SMEM_SPEC, ANY_SPEC, VMEM_SPEC, VMEM_SPEC],
        out_specs=[VMEM_SPEC] + [HBM_SPEC] * 6,
        scratch_shapes=saved_shapes(pltpu.VMEM)
        + [
            pltpu.VMEM((LEN_BLK, BLOCK, D), BF),
            pltpu.VMEM((GROUP, TILE, LANES), F32),
            pltpu.SMEM((LEN_BLK,), jnp.int32),
            pltpu.SemaphoreType.DMA((LEN_BLK,)),
            pltpu.SemaphoreType.DMA((6,)),
        ],
        compiler_params=params(32),
        name="forward_layer",
    )(lens, own, got_rows, w_proj, gain_in)


def backward_layer(lens, own, got_rows, got_grads, saved, w_proj, w_out, gain_in, gain_attn):
    return pl.pallas_call(
        backward_kernel,
        out_shape=(
            pltpu.HBM((PEERS, BLOCK, D), BF),
            pltpu.HBM((4 * PAIRS, ROWS, LANES), BF),
            pltpu.HBM((D, ROWS), BF),
            pltpu.HBM((ROWS, D), BF),
            struct((2, D), F32),
        ),
        in_specs=[SMEM_SPEC, SMEM_SPEC] + [ANY_SPEC] * 3 + [HBM_SPEC] * 6 + [VMEM_SPEC] * 3,
        out_specs=(VMEM_SPEC, HBM_SPEC, HBM_SPEC, HBM_SPEC, VMEM_SPEC),
        scratch_shapes=[
            pltpu.VMEM((LEN_BLK, BLOCK, D), BF),
            pltpu.VMEM((LEN_BLK, BLOCK, D), BF),
            pltpu.VMEM((PAIRS, ROWS, LANES), BF),
            pltpu.VMEM((4 * PAIRS, ROWS, LANES), BF),
            pltpu.VMEM((D, ROWS), BF),
            pltpu.VMEM((ROWS, D), BF),
            pltpu.VMEM((GROUP, LANES, TILE), F32),
            pltpu.VMEM((PAIRS, LANES, ROWS), BF),
            pltpu.VMEM((GROUP, ROWS, LANES), F32),
            pltpu.VMEM((GROUP, ROWS, LANES), F32),
            pltpu.SMEM((LEN_BLK,), jnp.int32),
            pltpu.SemaphoreType.DMA((LEN_BLK,)),
            pltpu.SemaphoreType.DMA((LEN_BLK,)),
            pltpu.SemaphoreType.DMA((11,)),
            pltpu.VMEM((PAIRS, ROWS, LANES), BF),
        ]
        + saved_shapes(pltpu.VMEM)[:5]
        + [pltpu.VMEM((D, 4 * D), BF)],
        compiler_params=params(44),
        name="backward_layer",
    )(lens, own, got_rows, got_grads, *saved[:6], w_proj, w_out, gain_in, gain_attn)


def gradient_terms(own, d_hidden, scaled, mixed, cot, gains):
    half = struct((HALF, LANES), BF)
    return pl.pallas_call(
        terms_kernel,
        out_shape=(half, half),
        in_specs=[SMEM_SPEC] + [HBM_SPEC] * 4 + [VMEM_SPEC],
        out_specs=(VMEM_SPEC, VMEM_SPEC),
        scratch_shapes=[
            pltpu.VMEM((4 * PAIRS, ROWS, LANES), BF),
            pltpu.VMEM((D, ROWS), BF),
            pltpu.VMEM((D, ROWS), BF),
            pltpu.VMEM((ROWS, D), BF),
            pltpu.SemaphoreType.DMA((11,)),
        ],
        compiler_params=params(40),
        cost_estimate=pl.CostEstimate(
            flops=10 * ROWS * D * D, transcendentals=0, bytes_accessed=10 * MIB
        ),
        name="gradient_terms",
    )(own, d_hidden, scaled, mixed, cot, gains)


def in_hbm(array):
    return pltpu.with_memory_space_constraint(array, pltpu.HBM)


def per_device(events, cotangent, lengths, gain_in, w_proj, gain_attn, w_out):
    own = lax.axis_index(("chip", "core")).astype(jnp.int32).reshape(1)
    lens = lengths[0]
    got_rows = lax.all_to_all(send_blocks(lens, own, events), ("chip", "core"), 0, 0, tiled=True)
    got_grads = lax.all_to_all(send_blocks(lens, own, cotangent), ("chip", "core"), 0, 0, tiled=True)
    gain_in = gain_in.reshape(1, D)
    saved = [in_hbm(x) for x in forward_layer(lens, own, got_rows, w_proj, gain_in)]
    send_back, *kept, gains = backward_layer(
        lens, own, got_rows, got_grads, saved, w_proj, w_out, gain_in, gain_attn.reshape(1, D)
    )
    came_back = lax.all_to_all(send_back, ("chip", "core"), 0, 0, tiled=True)
    d_hidden, mixed, cot = (in_hbm(x) for x in kept)
    keep, send = gradient_terms(own, d_hidden, saved[6], mixed, cot, gains)
    send, came_back = lax.optimization_barrier((send, came_back))
    swap = [(0, 1), (1, 0)]
    other = lax.ppermute(send, "core", swap)
    chip_sum = (keep.astype(F32) + other.astype(F32)).astype(BF)
    parts = lax.all_to_all(chip_sum.reshape(64, PART, LANES), ("grp", "chip"), 0, 0, tiled=True)
    total = (jnp.sum(parts.astype(F32), axis=0) * (1.0 / DEVICES)).astype(BF)
    copies = jnp.broadcast_to(total[None], (64, PART, LANES))
    mine = lax.all_to_all(copies, ("grp", "chip"), 0, 0, tiled=True).reshape(HALF, LANES)
    others = lax.ppermute(mine, "core", swap)
    d_rows = pl.pallas_call(
        home_kernel,
        out_shape=struct((LOCAL, BLOCK, D), BF),
        in_specs=[SMEM_SPEC, SMEM_SPEC, VMEM_SPEC],
        out_specs=VMEM_SPEC,
        name="take_home",
    )(lens, own, came_back)
    gain = struct((PAIRS, LANES), F32)
    grad_proj, grad_out, grad_in, grad_attn = pl.pallas_call(
        spread_kernel,
        out_shape=(struct((D, 4 * D), F32), struct((D, D), F32), gain, gain),
        in_specs=[SMEM_SPEC, VMEM_SPEC, VMEM_SPEC],
        out_specs=(ANY_SPEC, ANY_SPEC, VMEM_SPEC, VMEM_SPEC),
        scratch_shapes=[pltpu.VMEM((20, D, LANES), F32), pltpu.SemaphoreType.DMA((20,))],
        compiler_params=params(16),
        name="spread_grads",
    )(own, mine, others)
    return (
        d_rows.reshape(1, LOCAL * BLOCK, D),
        grad_proj,
        grad_out,
        grad_in.reshape(D),
        grad_attn.reshape(D),
    )


def solution(mesh):
    fine = Mesh(mesh.devices.reshape(8, 8, 2), ("grp", "chip", "core"))
    rows = P("grp", ("chip", "core"), None)
    return jax.shard_map(
        per_device,
        mesh=fine,
        in_specs=(rows, rows, P("grp", None), P(), P(), P(), P()),
        out_specs=(rows, P(), P(), P(), P()),
        check_vma=False,
    )
```

```python
import jax
import jax.numpy as jnp
from jax import lax
from jax.experimental import pallas as pl
from jax.experimental.pallas import tpu as pltpu
from jax.sharding import Mesh, PartitionSpec as P

D = 512
HEADS = 8
BLOCK = 64
LEN_BLK = 16
SEQ = 16
PEERS = 16
LOCAL = 8
TILE = 256
TILES = 4
ROWS = 1024
LANES = 128
PAIRS = 4
PART = 88
HALF = 64 * PART
EPS = 1e-06
DEVICES = 128
BF = jnp.bfloat16
F32 = jnp.float32
MIB = 1024 * 1024

SMEM_SPEC = pl.BlockSpec(memory_space=pltpu.SMEM)
ANY_SPEC = pl.BlockSpec(memory_space=pl.ANY)
VMEM_SPEC = pl.BlockSpec(memory_space=pltpu.VMEM)
HBM_SPEC = pl.BlockSpec(memory_space=pltpu.HBM)


def dot(left, right):
    return lax.dot_general(left, right, (((1,), (0,)), ((), ())), preferred_element_type=F32)


def dot_cols(left, right):
    return lax.dot_general(left, right, (((1,), (1,)), ((), ())), preferred_element_type=F32)


def dot_rows(left, right):
    return lax.dot_general(left, right, (((0,), (0,)), ((), ())), preferred_element_type=F32)


def packing(len_ref):
    starts, sizes, ranks = [], [], []
    start = jnp.int32(0)
    rank = jnp.int32(0)
    held = jnp.int32(0)
    for i in range(SEQ):
        size = len_ref[i]
        fresh = held + size > LEN_BLK
        rank = jnp.where(fresh, rank + 1, rank)
        held = jnp.where(fresh, size, held + size)
        starts.append(start)
        sizes.append(size)
        ranks.append(rank)
        start = start + size
    return starts, sizes, ranks


def owners(len_ref, own):
    starts, _, ranks = packing(len_ref)
    found = []
    for k in range(LOCAL):
        block = own + PEERS * k
        owner = ranks[0]
        for i in range(1, SEQ):
            owner = jnp.where(starts[i] <= block, ranks[i], owner)
        found.append(owner)
    return found


def holdings(len_ref, own):
    starts, sizes, ranks = packing(len_ref)
    first = jnp.int32(LEN_BLK * LOCAL)
    count = jnp.int32(0)
    for i in range(SEQ):
        mine = ranks[i] == own
        first = jnp.where(mine, jnp.minimum(first, starts[i]), first)
        count = jnp.where(mine, count + sizes[i], count)
    return starts, sizes, ranks, first, count


def history_starts(hist_ref, own, starts, sizes, ranks, first):
    for j in range(LEN_BLK):
        hist_ref[j] = j
    for i in range(SEQ):

        @pl.when(ranks[i] == own)
        def _(i=i):
            begin = starts[i] - first

            def put(j, carry):
                hist_ref[j] = begin
                return carry

            lax.fori_loop(begin, begin + sizes[i], put, 0)


def send_kernel(len_ref, own_ref, rows_ref, out_ref):
    owner = owners(len_ref, own_ref[0])
    for k in range(LOCAL):
        out_ref[owner[k]] = rows_ref[k]


def home_kernel(len_ref, own_ref, back_ref, out_ref):
    owner = owners(len_ref, own_ref[0])
    for k in range(LOCAL):
        out_ref[k] = back_ref[owner[k]]


def tile_rows(ref, t, first, count):
    slots = [(first + t * 4 + b) & (PEERS - 1) for b in range(4)]
    tile = jnp.concatenate([ref[slot] for slot in slots], axis=0).astype(F32)
    place = lax.broadcasted_iota(jnp.int32, (TILE, D), 0) + t * TILE
    return jnp.where(place < count * BLOCK, tile, 0.0)


def normed_rows(values):
    centred = values - jnp.mean(values, axis=-1, keepdims=True)
    rstd = lax.rsqrt(jnp.mean(centred * centred, axis=-1, keepdims=True) + EPS)
    return centred * rstd, rstd


def head_masks():
    lane = lax.broadcasted_iota(jnp.int32, (1, LANES), 1)
    low = (lane < 64).astype(F32).astype(BF)
    high = (lane >= 64).astype(F32).astype(BF)
    return low, high


GROUP = 4


def rows_at(t):
    return pl.ds(pl.multiple_of(t * TILE, TILE), TILE)


def block_starts(hist_ref, t, shape, dim):
    place = lax.broadcasted_iota(jnp.int32, shape, dim)
    begin = jnp.full(shape, hist_ref[4 * t], jnp.int32)
    for b in range(1, 4):
        begin = jnp.where(place >= b * BLOCK, hist_ref[4 * t + b], begin)
    return begin * BLOCK


def key_tiles(hist_ref, i):
    low = hist_ref[4 * i] // 4
    clear = jnp.minimum((hist_ref[4 * i + 3] + 3) // 4, i)
    return low, jnp.maximum(clear, low)


def forward_kernel(
    len_ref,
    own_ref,
    got_ref,
    w_ref,
    gain_ref,
    attn_ref,
    upper_out,
    values_out,
    query_out,
    keys_out,
    slope_out,
    scaled_out,
    upper_ref,
    values_ref,
    query_ref,
    keys_ref,
    slope_ref,
    scaled_ref,
    acc_ref,
    hist_ref,
    save_sems,
):
    own = own_ref[0]
    starts, sizes, ranks, first, count = holdings(len_ref, own)
    history_starts(hist_ref, own, starts, sizes, ranks, first)
    live = (count + 3) // 4

    def project(t, carry):
        normed, _ = normed_rows(tile_rows(got_ref, t, first, count))
        scaled = (normed * gain_ref[...]).astype(BF)
        rows = rows_at(t)
        scaled_ref[:, rows] = scaled.T
        for quarter in range(4):
            half = 0.5 * dot(scaled, w_ref[:, quarter * D : (quarter + 1) * D])
            swing = jnp.tanh(half)
            active = half + half * swing
            slope = ((0.5 + 0.5 * swing) * (1.0 + (half - half * swing))).astype(BF)
            if quarter == 0:
                upper_ref[rows, :] = active.astype(BF)
            if quarter == 2:
                active = active * 0.0625
            active = active.astype(BF)
            for p in range(PAIRS):
                lanes = slice(p * LANES, (p + 1) * LANES)
                slope_ref[quarter * PAIRS + p, rows, :] = slope[:, lanes]
                if quarter:
                    ref = (None, values_ref, query_ref, keys_ref)[quarter]
                    ref[p, rows, :] = active[:, lanes]
        return carry

    lax.fori_loop(0, live, project, 0)

    def clear(t, carry):
        scaled_ref[:, rows_at(t)] = jnp.zeros((D, TILE), BF)
        return carry

    lax.fori_loop(live, TILES, clear, 0)

    saves = [
        pltpu.make_async_copy(src, dst, save_sems.at[n])
        for n, (src, dst) in enumerate(
            (
                (upper_ref, upper_out),
                (values_ref, values_out),
                (query_ref, query_out),
                (keys_ref, keys_out),
                (slope_ref, slope_out),
                (scaled_ref, scaled_out),
            )
        )
    ]
    for save in saves:
        save.start()

    masks = head_masks()

    def group(g, carry):
        def query_tile(i, carry):
            acc_ref[...] = jnp.zeros((GROUP, TILE, LANES), F32)

            def step(j, masked):
                if masked:
                    shape = (TILE, TILE)
                    col = lax.broadcasted_iota(jnp.int32, shape, 1) + j * TILE
                    row = lax.broadcasted_iota(jnp.int32, shape, 0) + i * TILE
                    allowed = (col <= row) & (col >= block_starts(hist_ref, i, shape, 0))
                for n in range(GROUP):
                    p = g * GROUP + n
                    query = query_ref[p, rows_at(i), :]
                    keys = keys_ref[p, rows_at(j), :]
                    values = values_ref[p, rows_at(j), :]
                    total = acc_ref[n]
                    for mask in masks:
                        half = dot_cols(query, keys * mask)
                        weights = half + half * jnp.tanh(half)
                        if masked:
                            weights = jnp.where(allowed, weights, 0.0)
                        total += dot(weights.astype(BF), values * mask)
                    acc_ref[n] = total

            low, clear_from = key_tiles(hist_ref, i)

            def masked_step(j, carry):
                step(j, True)
                return carry

            def clear_step(j, carry):
                step(j, False)
                return carry

            lax.fori_loop(low, clear_from, masked_step, 0)
            lax.fori_loop(clear_from, i, clear_step, 0)
            step(i, True)
            for n in range(GROUP):
                attn_ref[g * GROUP + n, rows_at(i), :] = acc_ref[n].astype(BF)
            return carry

        return lax.fori_loop(0, live, query_tile, carry)

    lax.fori_loop(0, PAIRS // GROUP, group, 0)
    for save in saves:
        save.wait()


def backward_kernel(
    len_ref,
    own_ref,
    got_ref,
    grads_ref,
    attn_in,
    upper_in,
    values_in,
    query_in,
    keys_in,
    slope_in,
    w_in,
    w_out_in,
    gain_in_ref,
    gain_attn_ref,
    back_ref,
    d_hidden_out,
    mixed_out,
    cot_out,
    gains_ref,
    d_attn_ref,
    d_hidden_ref,
    mixed_ref,
    cot_rows_ref,
    d_query_ref,
    keys_t_ref,
    d_keys_ref,
    d_values_ref,
    hist_ref,
    tile_sems,
    load_sems,
    attn_ref,
    upper_ref,
    values_ref,
    query_ref,
    keys_ref,
    slope_ref,
    w_ref,
    w_out_ref,
):
    own = own_ref[0]
    starts, sizes, ranks, first, count = holdings(len_ref, own)
    live = (count + 3) // 4
    early = pl.ds(0, PAIRS)
    late = pl.ds(PAIRS, 3 * PAIRS)

    def tile_loads(t):
        rows = rows_at(t)
        return [
            pltpu.make_async_copy(
                attn_in.at[:, rows], attn_ref.at[:, rows], tile_sems.at[0, t]
            ),
            pltpu.make_async_copy(upper_in.at[rows], upper_ref.at[rows], tile_sems.at[1, t]),
            pltpu.make_async_copy(
                slope_in.at[early, rows], slope_ref.at[early, rows], tile_sems.at[2, t]
            ),
        ]

    loads = [
        pltpu.make_async_copy(src, dst, load_sems.at[n])
        for n, (src, dst) in enumerate(
            (
                (w_out_in, w_out_ref),
                (keys_in, keys_ref),
                (query_in, query_ref),
                (values_in, values_ref),
                (slope_in.at[late], slope_ref.at[late]),
                (w_in, w_ref),
            )
        )
    ]
    loads[0].start()

    def request(t, carry):
        for load in tile_loads(t):
            load.start()
        return carry

    lax.fori_loop(0, live, request, 0)
    for load in loads[1:]:
        load.start()
    history_starts(hist_ref, own, starts, sizes, ranks, first)
    gains_ref[...] = jnp.zeros((2, D), F32)
    loads[0].wait()

    def middle(t, carry):
        rows = rows_at(t)
        for load in tile_loads(t):
            load.wait()
        attn = jnp.concatenate([attn_ref[p, rows, :] for p in range(PAIRS)], axis=1)
        normed, rstd = normed_rows(attn.astype(F32))
        upper = upper_ref[rows, :].astype(F32)
        cot = tile_rows(grads_ref, t, first, count).astype(BF)
        d_mixed = dot_cols(cot, w_out_ref[...])
        gained = normed * gain_attn_ref[...]
        mixed_ref[:, rows] = (gained * upper).astype(BF).T
        cot_rows_ref[rows, :] = cot
        d_upper = d_mixed * gained
        pull = d_mixed * upper
        gains_ref[1:2, :] += jnp.sum(pull * normed, axis=0, keepdims=True)
        pull = pull * gain_attn_ref[...]
        d_attn = rstd * (
            pull
            - jnp.mean(pull, axis=-1, keepdims=True)
            - normed * jnp.mean(pull * normed, axis=-1, keepdims=True)
        )
        for p in range(PAIRS):
            lanes = slice(p * LANES, (p + 1) * LANES)
            d_attn_ref[p, rows, :] = d_attn[:, lanes].astype(BF)
            slope = slope_ref[p, rows, :].astype(F32)
            d_hidden_ref[p, rows, :] = (d_upper[:, lanes] * slope).astype(BF)
        return carry

    lax.fori_loop(0, live, middle, 0)

    def clear(t, carry):
        d_hidden_ref[:, rows_at(t), :] = jnp.zeros((4 * PAIRS, TILE, LANES), BF)
        mixed_ref[:, rows_at(t)] = jnp.zeros((D, TILE), BF)
        cot_rows_ref[rows_at(t), :] = jnp.zeros((TILE, D), BF)
        return carry

    lax.fori_loop(live, TILES, clear, 0)
    saves = [
        pltpu.make_async_copy(mixed_ref, mixed_out, load_sems.at[7]),
        pltpu.make_async_copy(cot_rows_ref, cot_out, load_sems.at[8]),
    ]
    for save in saves:
        save.start()

    masks = head_masks()
    for load in loads[1:5]:
        load.wait()

    def turn(t, carry):
        for p in range(PAIRS):
            keys_t_ref[p, :, rows_at(t)] = keys_ref[p, rows_at(t), :].T
        return carry

    lax.fori_loop(0, live, turn, 0)

    def group(g, carry):
        d_keys_ref[...] = jnp.zeros((GROUP, ROWS, LANES), F32)
        d_values_ref[...] = jnp.zeros((GROUP, ROWS, LANES), F32)

        def query_tile(i, carry):
            d_query_ref[...] = jnp.zeros((GROUP, LANES, TILE), F32)

            def step(j, masked):
                rows = rows_at(j)
                if masked:
                    shape = (TILE, TILE)
                    key_row = lax.broadcasted_iota(jnp.int32, shape, 0) + j * TILE
                    query_row = lax.broadcasted_iota(jnp.int32, shape, 1) + i * TILE
                    allowed = (key_row <= query_row) & (
                        key_row >= block_starts(hist_ref, i, shape, 1)
                    )
                for n in range(GROUP):
                    p = g * GROUP + n
                    query = query_ref[p, rows_at(i), :]
                    d_attn = d_attn_ref[p, rows_at(i), :]
                    keys = keys_ref[p, rows, :]
                    values = values_ref[p, rows, :]
                    d_keys = d_keys_ref[n, rows, :]
                    d_values = d_values_ref[n, rows, :]
                    for h, mask in enumerate(masks):
                        masked_keys = keys * mask
                        half = dot_cols(masked_keys, query)
                        swing = jnp.tanh(half)
                        bend = half * swing
                        weights = half + bend
                        slope = (1.0 + swing) * ((1.0 + half) - bend)
                        grad = dot_cols(values * mask, d_attn) * slope
                        if masked:
                            weights = jnp.where(allowed, weights, 0.0)
                            grad = jnp.where(allowed, grad, 0.0)
                        grad = grad.astype(BF)
                        d_values += dot(weights.astype(BF), d_attn * mask)
                        d_keys += dot(grad, query * mask)
                        head_rows = slice(h * 64, h * 64 + 64)
                        d_query_ref[n, head_rows, :] += dot(keys_t_ref[p, head_rows, rows], grad)
                    d_keys_ref[n, rows, :] = d_keys
                    d_values_ref[n, rows, :] = d_values

            low, clear_from = key_tiles(hist_ref, i)

            def masked_step(j, carry):
                step(j, True)
                return carry

            def clear_step(j, carry):
                step(j, False)
                return carry

            lax.fori_loop(low, clear_from, masked_step, 0)
            lax.fori_loop(clear_from, i, clear_step, 0)
            step(i, True)
            for n in range(GROUP):
                place = 2 * PAIRS + g * GROUP + n
                slope = slope_ref[place, rows_at(i), :].astype(F32)
                d_hidden_ref[place, rows_at(i), :] = (d_query_ref[n].T * 0.0625 * slope).astype(BF)
            return carry

        lax.fori_loop(0, live, query_tile, 0)

        def finish(t, carry):
            rows = rows_at(t)
            for n in range(GROUP):
                for quarter, ref in ((1, d_values_ref), (3, d_keys_ref)):
                    place = quarter * PAIRS + g * GROUP + n
                    slope = slope_ref[place, rows, :].astype(F32)
                    d_hidden_ref[place, rows, :] = (ref[n, rows, :] * slope).astype(BF)
            return carry

        lax.fori_loop(0, live, finish, 0)
        return carry

    lax.fori_loop(0, PAIRS // GROUP, group, 0)

    saves.append(pltpu.make_async_copy(d_hidden_ref, d_hidden_out, load_sems.at[6]))
    saves[-1].start()
    loads[5].wait()

    def final(t, carry):
        rows = rows_at(t)
        normed, rstd = normed_rows(tile_rows(got_ref, t, first, count))
        d_scaled = jnp.zeros((TILE, D), F32)
        for c in range(8):
            part = jnp.concatenate(
                [d_hidden_ref[2 * c, rows, :], d_hidden_ref[2 * c + 1, rows, :]], axis=1
            )
            d_scaled += dot_cols(part, w_ref[:, c * 256 : (c + 1) * 256])
        gains_ref[0:1, :] += jnp.sum(d_scaled * normed, axis=0, keepdims=True)
        pull = d_scaled * gain_in_ref[...]
        d_rows = rstd * (
            pull
            - jnp.mean(pull, axis=-1, keepdims=True)
            - normed * jnp.mean(pull * normed, axis=-1, keepdims=True)
        )
        d_rows = (d_rows + cot_rows_ref[rows, :].astype(F32)).astype(BF)
        for b in range(4):
            slot = (first + t * 4 + b) & (PEERS - 1)
            back_ref[slot] = d_rows[b * BLOCK : (b + 1) * BLOCK, :]
        return carry

    lax.fori_loop(0, live, final, 0)

    for save in saves:
        save.wait()


def terms_kernel(
    own_ref,
    d_hidden_in,
    scaled_in,
    mixed_in,
    cot_in,
    gains_ref,
    keep_ref,
    send_ref,
    d_hidden_ref,
    scaled_ref,
    mixed_ref,
    cot_ref,
    sems,
):
    core = own_ref[0] & 1
    loads = [
        pltpu.make_async_copy(mixed_in, mixed_ref, sems.at[9]),
        pltpu.make_async_copy(cot_in, cot_ref, sems.at[10]),
        pltpu.make_async_copy(scaled_in, scaled_ref, sems.at[8]),
    ]
    for c in range(8):
        part = pl.ds(2 * c, 2)
        loads.append(
            pltpu.make_async_copy(d_hidden_in.at[part], d_hidden_ref.at[part], sems.at[c])
        )
    for load in loads:
        load.start()

    def put(half, rows, values):
        values = values.astype(BF)

        @pl.when(core == half)
        def _():
            keep_ref[rows, :] = values

        @pl.when(core != half)
        def _():
            send_ref[rows, :] = values

    def put_piece(piece, values):
        half, place = divmod(piece, 10)
        put(half, pl.ds(place * D, D), values)

    for half in range(2):
        tail = jnp.concatenate(
            [gains_ref[half : half + 1, p * LANES : (p + 1) * LANES] for p in range(PAIRS)]
            + [jnp.zeros((HALF - 10 * D - PAIRS, LANES), F32)],
            axis=0,
        )
        put(half, pl.ds(10 * D, HALF - 10 * D), tail)
    loads[0].wait()
    loads[1].wait()
    for c in range(2):
        term = dot(mixed_ref[...], cot_ref[:, c * 256 : (c + 1) * 256])
        put_piece(16 + 2 * c, term[:, :LANES])
        put_piece(17 + 2 * c, term[:, LANES:])
    loads[2].wait()
    for c in range(8):
        loads[3 + c].wait()
        part = jnp.concatenate([d_hidden_ref[2 * c], d_hidden_ref[2 * c + 1]], axis=1)
        term = dot(scaled_ref[...], part)
        put_piece(2 * c, term[:, :LANES])
        put_piece(2 * c + 1, term[:, LANES:])


def spread_kernel(
    own_ref,
    mine_ref,
    other_ref,
    proj_ref,
    out_ref,
    gain_in_ref,
    gain_attn_ref,
    wide_ref,
    sems,
):
    core = own_ref[0] & 1

    def copy(piece):
        if piece < 16:
            target = proj_ref.at[:, pl.ds(piece * LANES, LANES)]
        else:
            target = out_ref.at[:, pl.ds((piece - 16) * LANES, LANES)]
        return pltpu.make_async_copy(wide_ref.at[piece], target, sems.at[piece])

    def write(low_ref, high_ref):
        for piece in range(20):
            half, place = divmod(piece, 10)
            wide_ref[piece] = (low_ref, high_ref)[half][place * D : (place + 1) * D, :].astype(F32)
            copy(piece).start()
        gain_in_ref[...] = low_ref[10 * D : 10 * D + 16, :].astype(F32)[:PAIRS]
        gain_attn_ref[...] = high_ref[10 * D : 10 * D + 16, :].astype(F32)[:PAIRS]

    @pl.when(core == 0)
    def _():
        write(mine_ref, other_ref)

    @pl.when(core == 1)
    def _():
        write(other_ref, mine_ref)

    for piece in range(20):
        copy(piece).wait()


def struct(shape, dtype):
    return jax.ShapeDtypeStruct(shape, dtype)


def params(mebibytes):
    return pltpu.CompilerParams(vmem_limit_bytes=mebibytes * MIB)


def send_blocks(lens, own, rows):
    return pl.pallas_call(
        send_kernel,
        out_shape=struct((PEERS, BLOCK, D), BF),
        in_specs=[SMEM_SPEC, SMEM_SPEC, VMEM_SPEC],
        out_specs=VMEM_SPEC,
        name="send_blocks",
    )(lens, own, rows.reshape(LOCAL, BLOCK, D))


def saved_shapes(make):
    pairs = make((PAIRS, ROWS, LANES), BF)
    wide = make((ROWS, D), BF)
    tall = make((D, ROWS), BF)
    return [wide, pairs, pairs, pairs, make((4 * PAIRS, ROWS, LANES), BF), tall]


def forward_layer(lens, own, got_rows, w_proj, gain_in):
    return pl.pallas_call(
        forward_kernel,
        out_shape=[pltpu.HBM((PAIRS, ROWS, LANES), BF)] + saved_shapes(pltpu.HBM),
        in_specs=[SMEM_SPEC, SMEM_SPEC, VMEM_SPEC, VMEM_SPEC, VMEM_SPEC],
        out_specs=[VMEM_SPEC] + [HBM_SPEC] * 6,
        scratch_shapes=saved_shapes(pltpu.VMEM)
        + [
            pltpu.VMEM((GROUP, TILE, LANES), F32),
            pltpu.SMEM((LEN_BLK,), jnp.int32),
            pltpu.SemaphoreType.DMA((6,)),
        ],
        compiler_params=params(32),
        name="forward_layer",
    )(lens, own, got_rows, w_proj, gain_in)


def backward_layer(lens, own, got_rows, got_grads, saved, w_proj, w_out, gain_in, gain_attn):
    return pl.pallas_call(
        backward_kernel,
        out_shape=(
            pltpu.HBM((PEERS, BLOCK, D), BF),
            pltpu.HBM((4 * PAIRS, ROWS, LANES), BF),
            pltpu.HBM((D, ROWS), BF),
            pltpu.HBM((ROWS, D), BF),
            struct((2, D), F32),
        ),
        in_specs=[SMEM_SPEC] * 2 + [VMEM_SPEC] * 2 + [ANY_SPEC] * 8 + [VMEM_SPEC] * 2,
        out_specs=(VMEM_SPEC, HBM_SPEC, HBM_SPEC, HBM_SPEC, VMEM_SPEC),
        scratch_shapes=[
            pltpu.VMEM((PAIRS, ROWS, LANES), BF),
            pltpu.VMEM((4 * PAIRS, ROWS, LANES), BF),
            pltpu.VMEM((D, ROWS), BF),
            pltpu.VMEM((ROWS, D), BF),
            pltpu.VMEM((GROUP, LANES, TILE), F32),
            pltpu.VMEM((PAIRS, LANES, ROWS), BF),
            pltpu.VMEM((GROUP, ROWS, LANES), F32),
            pltpu.VMEM((GROUP, ROWS, LANES), F32),
            pltpu.SMEM((LEN_BLK,), jnp.int32),
            pltpu.SemaphoreType.DMA((3, TILES)),
            pltpu.SemaphoreType.DMA((9,)),
            pltpu.VMEM((PAIRS, ROWS, LANES), BF),
        ]
        + saved_shapes(pltpu.VMEM)[:5]
        + [pltpu.VMEM((D, 4 * D), BF), pltpu.VMEM((D, D), BF)],
        compiler_params=params(44),
        name="backward_layer",
    )(lens, own, got_rows, got_grads, *saved[:6], w_proj, w_out, gain_in, gain_attn)


def gradient_terms(own, d_hidden, scaled, mixed, cot, gains):
    half = struct((HALF, LANES), BF)
    return pl.pallas_call(
        terms_kernel,
        out_shape=(half, half),
        in_specs=[SMEM_SPEC] + [HBM_SPEC] * 4 + [VMEM_SPEC],
        out_specs=(VMEM_SPEC, VMEM_SPEC),
        scratch_shapes=[
            pltpu.VMEM((4 * PAIRS, ROWS, LANES), BF),
            pltpu.VMEM((D, ROWS), BF),
            pltpu.VMEM((D, ROWS), BF),
            pltpu.VMEM((ROWS, D), BF),
            pltpu.SemaphoreType.DMA((11,)),
        ],
        compiler_params=params(40),
        cost_estimate=pl.CostEstimate(
            flops=10 * ROWS * D * D, transcendentals=0, bytes_accessed=10 * MIB
        ),
        name="gradient_terms",
    )(own, d_hidden, scaled, mixed, cot, gains)


def in_hbm(array):
    return pltpu.with_memory_space_constraint(array, pltpu.HBM)


def per_device(events, cotangent, lengths, gain_in, w_proj, gain_attn, w_out):
    own = lax.axis_index(("chip", "core")).astype(jnp.int32).reshape(1)
    lens = lengths[0]
    got_rows = lax.all_to_all(send_blocks(lens, own, events), ("chip", "core"), 0, 0, tiled=True)
    got_grads = lax.all_to_all(send_blocks(lens, own, cotangent), ("chip", "core"), 0, 0, tiled=True)
    gain_in = gain_in.reshape(1, D)
    saved = [in_hbm(x) for x in forward_layer(lens, own, got_rows, w_proj, gain_in)]
    send_back, *kept, gains = backward_layer(
        lens, own, got_rows, got_grads, saved, w_proj, in_hbm(w_out), gain_in, gain_attn.reshape(1, D)
    )
    came_back = lax.all_to_all(send_back, ("chip", "core"), 0, 0, tiled=True)
    d_hidden, mixed, cot = (in_hbm(x) for x in kept)
    keep, send = gradient_terms(own, d_hidden, saved[6], mixed, cot, gains)
    send, came_back = lax.optimization_barrier((send, came_back))
    swap = [(0, 1), (1, 0)]
    other = lax.ppermute(send, "core", swap)
    chip_sum = (keep.astype(F32) + other.astype(F32)).astype(BF)
    parts = lax.all_to_all(chip_sum.reshape(64, PART, LANES), ("grp", "chip"), 0, 0, tiled=True)
    total = (jnp.sum(parts.astype(F32), axis=0) * (1.0 / DEVICES)).astype(BF)
    copies = jnp.broadcast_to(total[None], (64, PART, LANES))
    mine = lax.all_to_all(copies, ("grp", "chip"), 0, 0, tiled=True).reshape(HALF, LANES)
    others = lax.ppermute(mine, "core", swap)
    d_rows = pl.pallas_call(
        home_kernel,
        out_shape=struct((LOCAL, BLOCK, D), BF),
        in_specs=[SMEM_SPEC, SMEM_SPEC, VMEM_SPEC],
        out_specs=VMEM_SPEC,
        name="take_home",
    )(lens, own, came_back)
    gain = struct((PAIRS, LANES), F32)
    grad_proj, grad_out, grad_in, grad_attn = pl.pallas_call(
        spread_kernel,
        out_shape=(struct((D, 4 * D), F32), struct((D, D), F32), gain, gain),
        in_specs=[SMEM_SPEC, VMEM_SPEC, VMEM_SPEC],
        out_specs=(ANY_SPEC, ANY_SPEC, VMEM_SPEC, VMEM_SPEC),
        scratch_shapes=[pltpu.VMEM((20, D, LANES), F32), pltpu.SemaphoreType.DMA((20,))],
        compiler_params=params(16),
        name="spread_grads",
    )(own, mine, others)
    return (
        d_rows.reshape(1, LOCAL * BLOCK, D),
        grad_proj,
        grad_out,
        grad_in.reshape(D),
        grad_attn.reshape(D),
    )


def solution(mesh):
    fine = Mesh(mesh.devices.reshape(8, 8, 2), ("grp", "chip", "core"))
    rows = P("grp", ("chip", "core"), None)
    return jax.shard_map(
        per_device,
        mesh=fine,
        in_specs=(rows, rows, P("grp", None), P(), P(), P(), P()),
        out_specs=(rows, P(), P(), P(), P()),
        check_vma=False,
    )
```

```python
import jax
import jax.numpy as jnp
from jax import lax
from jax.experimental import pallas as pl
from jax.experimental.pallas import tpu as pltpu
from jax.sharding import Mesh, PartitionSpec as P

D = 512
HEADS = 8
BLOCK = 64
LEN_BLK = 16
SEQ = 16
PEERS = 16
LOCAL = 8
TILE = 256
TILES = 4
ROWS = 1024
LANES = 128
PAIRS = 4
PART = 80
HALF = 64 * PART
EPS = 1e-06
DEVICES = 128
BF = jnp.bfloat16
F32 = jnp.float32
MIB = 1024 * 1024

SMEM_SPEC = pl.BlockSpec(memory_space=pltpu.SMEM)
ANY_SPEC = pl.BlockSpec(memory_space=pl.ANY)
VMEM_SPEC = pl.BlockSpec(memory_space=pltpu.VMEM)
HBM_SPEC = pl.BlockSpec(memory_space=pltpu.HBM)


def dot(left, right):
    return lax.dot_general(left, right, (((1,), (0,)), ((), ())), preferred_element_type=F32)


def dot_cols(left, right):
    return lax.dot_general(left, right, (((1,), (1,)), ((), ())), preferred_element_type=F32)


def dot_rows(left, right):
    return lax.dot_general(left, right, (((0,), (0,)), ((), ())), preferred_element_type=F32)


def packing(len_ref):
    starts, sizes, ranks = [], [], []
    start = jnp.int32(0)
    rank = jnp.int32(0)
    held = jnp.int32(0)
    for i in range(SEQ):
        size = len_ref[i]
        fresh = held + size > LEN_BLK
        rank = jnp.where(fresh, rank + 1, rank)
        held = jnp.where(fresh, size, held + size)
        starts.append(start)
        sizes.append(size)
        ranks.append(rank)
        start = start + size
    return starts, sizes, ranks


def owners(len_ref, own):
    starts, _, ranks = packing(len_ref)
    found = []
    for k in range(LOCAL):
        block = own + PEERS * k
        owner = ranks[0]
        for i in range(1, SEQ):
            owner = jnp.where(starts[i] <= block, ranks[i], owner)
        found.append(owner)
    return found


def holdings(len_ref, own):
    starts, sizes, ranks = packing(len_ref)
    first = jnp.int32(LEN_BLK * LOCAL)
    count = jnp.int32(0)
    for i in range(SEQ):
        mine = ranks[i] == own
        first = jnp.where(mine, jnp.minimum(first, starts[i]), first)
        count = jnp.where(mine, count + sizes[i], count)
    return starts, sizes, ranks, first, count


def history_starts(hist_ref, own, starts, sizes, ranks, first):
    for j in range(LEN_BLK):
        hist_ref[j] = j
    for i in range(SEQ):

        @pl.when(ranks[i] == own)
        def _(i=i):
            begin = starts[i] - first

            def put(j, carry):
                hist_ref[j] = begin
                return carry

            lax.fori_loop(begin, begin + sizes[i], put, 0)


def send_kernel(len_ref, own_ref, rows_ref, out_ref):
    owner = owners(len_ref, own_ref[0])
    for k in range(LOCAL):
        out_ref[owner[k]] = rows_ref[k]


def home_kernel(len_ref, own_ref, back_ref, out_ref):
    owner = owners(len_ref, own_ref[0])
    for k in range(LOCAL):
        out_ref[k] = back_ref[owner[k]]


def tile_rows(ref, t, first, count):
    slots = [(first + t * 4 + b) & (PEERS - 1) for b in range(4)]
    tile = jnp.concatenate([ref[slot] for slot in slots], axis=0).astype(F32)
    place = lax.broadcasted_iota(jnp.int32, (TILE, D), 0) + t * TILE
    return jnp.where(place < count * BLOCK, tile, 0.0)


def normed_rows(values):
    centred = values - jnp.mean(values, axis=-1, keepdims=True)
    rstd = lax.rsqrt(jnp.mean(centred * centred, axis=-1, keepdims=True) + EPS)
    return centred * rstd, rstd


def head_masks():
    lane = lax.broadcasted_iota(jnp.int32, (1, LANES), 1)
    low = (lane < 64).astype(F32).astype(BF)
    high = (lane >= 64).astype(F32).astype(BF)
    return low, high


GROUP = 4


def rows_at(t):
    return pl.ds(pl.multiple_of(t * TILE, TILE), TILE)


def block_starts(hist_ref, t, shape, dim):
    place = lax.broadcasted_iota(jnp.int32, shape, dim)
    begin = jnp.full(shape, hist_ref[4 * t], jnp.int32)
    for b in range(1, 4):
        begin = jnp.where(place >= b * BLOCK, hist_ref[4 * t + b], begin)
    return begin * BLOCK


def key_tiles(hist_ref, i):
    low = hist_ref[4 * i] // 4
    clear = jnp.minimum((hist_ref[4 * i + 3] + 3) // 4, i)
    return low, jnp.maximum(clear, low)


def forward_kernel(
    len_ref,
    own_ref,
    got_ref,
    w_ref,
    gain_ref,
    attn_ref,
    upper_out,
    values_out,
    query_out,
    keys_out,
    slope_out,
    scaled_out,
    upper_ref,
    values_ref,
    query_ref,
    keys_ref,
    slope_ref,
    scaled_ref,
    acc_ref,
    hist_ref,
    save_sems,
):
    own = own_ref[0]
    starts, sizes, ranks, first, count = holdings(len_ref, own)
    history_starts(hist_ref, own, starts, sizes, ranks, first)
    live = (count + 3) // 4

    def project(t, carry):
        normed, _ = normed_rows(tile_rows(got_ref, t, first, count))
        scaled = (normed * gain_ref[...]).astype(BF)
        rows = rows_at(t)
        scaled_ref[:, rows] = scaled.T
        for quarter in range(4):
            half = 0.5 * dot(scaled, w_ref[:, quarter * D : (quarter + 1) * D])
            swing = jnp.tanh(half)
            active = half + half * swing
            slope = ((0.5 + 0.5 * swing) * (1.0 + (half - half * swing))).astype(BF)
            if quarter == 0:
                upper_ref[rows, :] = active.astype(BF)
            if quarter == 2:
                active = active * 0.0625
            active = active.astype(BF)
            for p in range(PAIRS):
                lanes = slice(p * LANES, (p + 1) * LANES)
                slope_ref[quarter * PAIRS + p, rows, :] = slope[:, lanes]
                if quarter:
                    ref = (None, values_ref, query_ref, keys_ref)[quarter]
                    ref[p, rows, :] = active[:, lanes]
        return carry

    lax.fori_loop(0, live, project, 0)

    def clear(t, carry):
        scaled_ref[:, rows_at(t)] = jnp.zeros((D, TILE), BF)
        return carry

    lax.fori_loop(live, TILES, clear, 0)

    saves = [
        pltpu.make_async_copy(src, dst, save_sems.at[n])
        for n, (src, dst) in enumerate(
            (
                (upper_ref, upper_out),
                (values_ref, values_out),
                (query_ref, query_out),
                (keys_ref, keys_out),
                (slope_ref, slope_out),
                (scaled_ref, scaled_out),
            )
        )
    ]
    for save in saves:
        save.start()

    masks = head_masks()

    def group(g, carry):
        def query_tile(i, carry):
            acc_ref[...] = jnp.zeros((GROUP, TILE, LANES), F32)

            def step(j, masked):
                if masked:
                    shape = (TILE, TILE)
                    col = lax.broadcasted_iota(jnp.int32, shape, 1) + j * TILE
                    row = lax.broadcasted_iota(jnp.int32, shape, 0) + i * TILE
                    allowed = (col <= row) & (col >= block_starts(hist_ref, i, shape, 0))
                for n in range(GROUP):
                    p = g * GROUP + n
                    query = query_ref[p, rows_at(i), :]
                    keys = keys_ref[p, rows_at(j), :]
                    values = values_ref[p, rows_at(j), :]
                    total = acc_ref[n]
                    for mask in masks:
                        half = dot_cols(query, keys * mask)
                        weights = half + half * jnp.tanh(half)
                        if masked:
                            weights = jnp.where(allowed, weights, 0.0)
                        total += dot(weights.astype(BF), values * mask)
                    acc_ref[n] = total

            low, clear_from = key_tiles(hist_ref, i)

            def masked_step(j, carry):
                step(j, True)
                return carry

            def clear_step(j, carry):
                step(j, False)
                return carry

            lax.fori_loop(low, clear_from, masked_step, 0)
            lax.fori_loop(clear_from, i, clear_step, 0)
            step(i, True)
            for n in range(GROUP):
                attn_ref[g * GROUP + n, rows_at(i), :] = acc_ref[n].astype(BF)
            return carry

        return lax.fori_loop(0, live, query_tile, carry)

    lax.fori_loop(0, PAIRS // GROUP, group, 0)
    for save in saves:
        save.wait()


def backward_kernel(
    len_ref,
    own_ref,
    got_ref,
    grads_ref,
    attn_in,
    upper_in,
    values_in,
    query_in,
    keys_in,
    slope_in,
    w_in,
    w_out_in,
    gain_in_ref,
    gain_attn_ref,
    back_ref,
    d_hidden_out,
    mixed_out,
    cot_out,
    d_attn_ref,
    d_hidden_ref,
    mixed_ref,
    cot_rows_ref,
    d_query_ref,
    keys_t_ref,
    d_keys_ref,
    d_values_ref,
    hist_ref,
    tile_sems,
    load_sems,
    attn_ref,
    upper_ref,
    values_ref,
    query_ref,
    keys_ref,
    slope_ref,
    w_ref,
    w_out_ref,
):
    own = own_ref[0]
    starts, sizes, ranks, first, count = holdings(len_ref, own)
    live = (count + 3) // 4
    early = pl.ds(0, PAIRS)
    late = pl.ds(PAIRS, 3 * PAIRS)

    def tile_loads(t):
        rows = rows_at(t)
        return [
            pltpu.make_async_copy(
                attn_in.at[:, rows], attn_ref.at[:, rows], tile_sems.at[0, t]
            ),
            pltpu.make_async_copy(upper_in.at[rows], upper_ref.at[rows], tile_sems.at[1, t]),
            pltpu.make_async_copy(
                slope_in.at[early, rows], slope_ref.at[early, rows], tile_sems.at[2, t]
            ),
        ]

    loads = [
        pltpu.make_async_copy(src, dst, load_sems.at[n])
        for n, (src, dst) in enumerate(
            (
                (w_out_in, w_out_ref),
                (keys_in, keys_ref),
                (query_in, query_ref),
                (values_in, values_ref),
                (slope_in.at[late], slope_ref.at[late]),
                (w_in, w_ref),
            )
        )
    ]
    loads[0].start()

    def request(t, carry):
        for load in tile_loads(t):
            load.start()
        return carry

    lax.fori_loop(0, live, request, 0)
    for load in loads[1:]:
        load.start()
    history_starts(hist_ref, own, starts, sizes, ranks, first)
    loads[0].wait()

    def middle(t, carry):
        rows = rows_at(t)
        for load in tile_loads(t):
            load.wait()
        attn = jnp.concatenate([attn_ref[p, rows, :] for p in range(PAIRS)], axis=1)
        normed, rstd = normed_rows(attn.astype(F32))
        upper = upper_ref[rows, :].astype(F32)
        cot = tile_rows(grads_ref, t, first, count).astype(BF)
        d_mixed = dot_cols(cot, w_out_ref[...])
        gained = normed * gain_attn_ref[...]
        mixed_ref[:, rows] = (gained * upper).astype(BF).T
        cot_rows_ref[rows, :] = cot
        d_upper = d_mixed * gained
        pull = d_mixed * upper
        pull = pull * gain_attn_ref[...]
        d_attn = rstd * (
            pull
            - jnp.mean(pull, axis=-1, keepdims=True)
            - normed * jnp.mean(pull * normed, axis=-1, keepdims=True)
        )
        for p in range(PAIRS):
            lanes = slice(p * LANES, (p + 1) * LANES)
            d_attn_ref[p, rows, :] = d_attn[:, lanes].astype(BF)
            slope = slope_ref[p, rows, :].astype(F32)
            d_hidden_ref[p, rows, :] = (d_upper[:, lanes] * slope).astype(BF)
        return carry

    lax.fori_loop(0, live, middle, 0)

    def clear(t, carry):
        d_hidden_ref[:, rows_at(t), :] = jnp.zeros((4 * PAIRS, TILE, LANES), BF)
        mixed_ref[:, rows_at(t)] = jnp.zeros((D, TILE), BF)
        cot_rows_ref[rows_at(t), :] = jnp.zeros((TILE, D), BF)
        return carry

    lax.fori_loop(live, TILES, clear, 0)
    saves = [
        pltpu.make_async_copy(mixed_ref, mixed_out, load_sems.at[7]),
        pltpu.make_async_copy(cot_rows_ref, cot_out, load_sems.at[8]),
    ]
    for save in saves:
        save.start()

    masks = head_masks()
    for load in loads[1:5]:
        load.wait()

    def turn(t, carry):
        for p in range(PAIRS):
            keys_t_ref[p, :, rows_at(t)] = keys_ref[p, rows_at(t), :].T
        return carry

    lax.fori_loop(0, live, turn, 0)

    def group(g, carry):
        d_keys_ref[...] = jnp.zeros((GROUP, ROWS, LANES), F32)
        d_values_ref[...] = jnp.zeros((GROUP, ROWS, LANES), F32)

        def query_tile(i, carry):
            d_query_ref[...] = jnp.zeros((GROUP, LANES, TILE), F32)

            def step(j, masked):
                rows = rows_at(j)
                if masked:
                    shape = (TILE, TILE)
                    key_row = lax.broadcasted_iota(jnp.int32, shape, 0) + j * TILE
                    query_row = lax.broadcasted_iota(jnp.int32, shape, 1) + i * TILE
                    allowed = (key_row <= query_row) & (
                        key_row >= block_starts(hist_ref, i, shape, 1)
                    )
                for n in range(GROUP):
                    p = g * GROUP + n
                    query = query_ref[p, rows_at(i), :]
                    d_attn = d_attn_ref[p, rows_at(i), :]
                    keys = keys_ref[p, rows, :]
                    values = values_ref[p, rows, :]
                    d_keys = d_keys_ref[n, rows, :]
                    d_values = d_values_ref[n, rows, :]
                    for h, mask in enumerate(masks):
                        masked_keys = keys * mask
                        half = dot_cols(masked_keys, query)
                        swing = jnp.tanh(half)
                        bend = half * swing
                        weights = half + bend
                        slope = (1.0 + swing) * ((1.0 + half) - bend)
                        grad = dot_cols(values * mask, d_attn) * slope
                        if masked:
                            weights = jnp.where(allowed, weights, 0.0)
                            grad = jnp.where(allowed, grad, 0.0)
                        grad = grad.astype(BF)
                        d_values += dot(weights.astype(BF), d_attn * mask)
                        d_keys += dot(grad, query * mask)
                        head_rows = slice(h * 64, h * 64 + 64)
                        d_query_ref[n, head_rows, :] += dot(keys_t_ref[p, head_rows, rows], grad)
                    d_keys_ref[n, rows, :] = d_keys
                    d_values_ref[n, rows, :] = d_values

            low, clear_from = key_tiles(hist_ref, i)

            def masked_step(j, carry):
                step(j, True)
                return carry

            def clear_step(j, carry):
                step(j, False)
                return carry

            lax.fori_loop(low, clear_from, masked_step, 0)
            lax.fori_loop(clear_from, i, clear_step, 0)
            step(i, True)
            for n in range(GROUP):
                place = 2 * PAIRS + g * GROUP + n
                slope = slope_ref[place, rows_at(i), :].astype(F32)
                d_hidden_ref[place, rows_at(i), :] = (d_query_ref[n].T * 0.0625 * slope).astype(BF)
            return carry

        lax.fori_loop(0, live, query_tile, 0)

        def finish(t, carry):
            rows = rows_at(t)
            for n in range(GROUP):
                for quarter, ref in ((1, d_values_ref), (3, d_keys_ref)):
                    place = quarter * PAIRS + g * GROUP + n
                    slope = slope_ref[place, rows, :].astype(F32)
                    d_hidden_ref[place, rows, :] = (ref[n, rows, :] * slope).astype(BF)
            return carry

        lax.fori_loop(0, live, finish, 0)
        return carry

    lax.fori_loop(0, PAIRS // GROUP, group, 0)

    saves.append(pltpu.make_async_copy(d_hidden_ref, d_hidden_out, load_sems.at[6]))
    saves[-1].start()
    loads[5].wait()

    def final(t, carry):
        rows = rows_at(t)
        normed, rstd = normed_rows(tile_rows(got_ref, t, first, count))
        d_scaled = jnp.zeros((TILE, D), F32)
        for c in range(8):
            part = jnp.concatenate(
                [d_hidden_ref[2 * c, rows, :], d_hidden_ref[2 * c + 1, rows, :]], axis=1
            )
            d_scaled += dot_cols(part, w_ref[:, c * 256 : (c + 1) * 256])
        pull = d_scaled * gain_in_ref[...]
        d_rows = rstd * (
            pull
            - jnp.mean(pull, axis=-1, keepdims=True)
            - normed * jnp.mean(pull * normed, axis=-1, keepdims=True)
        )
        d_rows = (d_rows + cot_rows_ref[rows, :].astype(F32)).astype(BF)
        for b in range(4):
            slot = (first + t * 4 + b) & (PEERS - 1)
            back_ref[slot] = d_rows[b * BLOCK : (b + 1) * BLOCK, :]
        return carry

    lax.fori_loop(0, live, final, 0)

    for save in saves:
        save.wait()


def terms_kernel(
    own_ref,
    d_hidden_in,
    scaled_in,
    mixed_in,
    cot_in,
    keep_ref,
    send_ref,
    d_hidden_ref,
    scaled_ref,
    mixed_ref,
    cot_ref,
    sems,
):
    core = own_ref[0] & 1
    loads = [
        pltpu.make_async_copy(mixed_in, mixed_ref, sems.at[9]),
        pltpu.make_async_copy(cot_in, cot_ref, sems.at[10]),
        pltpu.make_async_copy(scaled_in, scaled_ref, sems.at[8]),
    ]
    for c in range(8):
        part = pl.ds(2 * c, 2)
        loads.append(
            pltpu.make_async_copy(d_hidden_in.at[part], d_hidden_ref.at[part], sems.at[c])
        )
    for load in loads:
        load.start()

    def put(half, rows, values):
        values = values.astype(BF)

        @pl.when(core == half)
        def _():
            keep_ref[rows, :] = values

        @pl.when(core != half)
        def _():
            send_ref[rows, :] = values

    def put_piece(piece, values):
        half, place = divmod(piece, 10)
        put(half, pl.ds(place * D, D), values)

    loads[0].wait()
    loads[1].wait()
    for c in range(2):
        term = dot(mixed_ref[...], cot_ref[:, c * 256 : (c + 1) * 256])
        put_piece(16 + 2 * c, term[:, :LANES])
        put_piece(17 + 2 * c, term[:, LANES:])
    loads[2].wait()
    for c in range(8):
        loads[3 + c].wait()
        part = jnp.concatenate([d_hidden_ref[2 * c], d_hidden_ref[2 * c + 1]], axis=1)
        term = dot(scaled_ref[...], part)
        put_piece(2 * c, term[:, :LANES])
        put_piece(2 * c + 1, term[:, LANES:])


def spread_half(half, half_ref, w_ref, w_out_ref, proj_ref, out_ref, wide_ref, sums_ref, sems):
    in_sum = jnp.zeros((D, LANES), F32)
    attn_sum = jnp.zeros((D, LANES), F32)
    for place in range(10):
        piece = half * 10 + place
        part = half_ref[place * D : (place + 1) * D, :].astype(F32)
        wide_ref[place] = part
        if piece < 16:
            lanes = pl.ds(piece * LANES, LANES)
            target = proj_ref.at[:, lanes]
            in_sum += part * w_ref[:, lanes].astype(F32)
        else:
            lanes = pl.ds((piece - 16) * LANES, LANES)
            target = out_ref.at[:, lanes]
            attn_sum += part * w_out_ref[:, lanes].astype(F32)
        pltpu.make_async_copy(wide_ref.at[place], target, sems.at[place]).start()
    sums_ref[0] = in_sum
    sums_ref[1] = attn_sum


def spread_wait(proj_ref, wide_ref, sems):
    for place in range(10):
        target = proj_ref.at[:, pl.ds(place * LANES, LANES)]
        pltpu.make_async_copy(wide_ref.at[place], target, sems.at[place]).wait()


def spread_mine(own_ref, mine_ref, w_ref, w_out_ref, proj_ref, out_ref, sums_ref, wide_ref, sems):
    core = own_ref[0] & 1
    for half in range(2):

        @pl.when(core == half)
        def _(half=half):
            spread_half(
                half, mine_ref, w_ref, w_out_ref, proj_ref, out_ref, wide_ref, sums_ref, sems
            )

    spread_wait(proj_ref, wide_ref, sems)


def spread_other(
    own_ref,
    other_ref,
    w_ref,
    w_out_ref,
    gain_in_ref,
    gain_attn_ref,
    mine_sums_ref,
    proj_in,
    out_in,
    proj_ref,
    out_ref,
    grad_in_ref,
    grad_attn_ref,
    wide_ref,
    sums_ref,
    sems,
):
    core = own_ref[0] & 1
    for half in range(2):

        @pl.when(core != half)
        def _(half=half):
            spread_half(
                half, other_ref, w_ref, w_out_ref, proj_ref, out_ref, wide_ref, sums_ref, sems
            )

    for n, (gain_ref, grad_ref) in enumerate(
        ((gain_in_ref, grad_in_ref), (gain_attn_ref, grad_attn_ref))
    ):
        total = (sums_ref[n] + mine_sums_ref[n]).T
        grad_ref[...] = jnp.sum(total, axis=0, keepdims=True) / gain_ref[...]
    spread_wait(proj_ref, wide_ref, sems)


def struct(shape, dtype):
    return jax.ShapeDtypeStruct(shape, dtype)


def params(mebibytes):
    return pltpu.CompilerParams(vmem_limit_bytes=mebibytes * MIB)


def send_blocks(lens, own, rows):
    return pl.pallas_call(
        send_kernel,
        out_shape=struct((PEERS, BLOCK, D), BF),
        in_specs=[SMEM_SPEC, SMEM_SPEC, VMEM_SPEC],
        out_specs=VMEM_SPEC,
        name="send_blocks",
    )(lens, own, rows.reshape(LOCAL, BLOCK, D))


def saved_shapes(make):
    pairs = make((PAIRS, ROWS, LANES), BF)
    wide = make((ROWS, D), BF)
    tall = make((D, ROWS), BF)
    return [wide, pairs, pairs, pairs, make((4 * PAIRS, ROWS, LANES), BF), tall]


def forward_layer(lens, own, got_rows, w_proj, gain_in):
    return pl.pallas_call(
        forward_kernel,
        out_shape=[pltpu.HBM((PAIRS, ROWS, LANES), BF)] + saved_shapes(pltpu.HBM),
        in_specs=[SMEM_SPEC, SMEM_SPEC, VMEM_SPEC, VMEM_SPEC, VMEM_SPEC],
        out_specs=[VMEM_SPEC] + [HBM_SPEC] * 6,
        scratch_shapes=saved_shapes(pltpu.VMEM)
        + [
            pltpu.VMEM((GROUP, TILE, LANES), F32),
            pltpu.SMEM((LEN_BLK,), jnp.int32),
            pltpu.SemaphoreType.DMA((6,)),
        ],
        compiler_params=params(32),
        name="forward_layer",
    )(lens, own, got_rows, w_proj, gain_in)


def backward_layer(lens, own, got_rows, got_grads, saved, w_proj, w_out, gain_in, gain_attn):
    return pl.pallas_call(
        backward_kernel,
        out_shape=(
            pltpu.HBM((PEERS, BLOCK, D), BF),
            pltpu.HBM((4 * PAIRS, ROWS, LANES), BF),
            pltpu.HBM((D, ROWS), BF),
            pltpu.HBM((ROWS, D), BF),
        ),
        in_specs=[SMEM_SPEC] * 2 + [VMEM_SPEC] * 2 + [ANY_SPEC] * 8 + [VMEM_SPEC] * 2,
        out_specs=(VMEM_SPEC, HBM_SPEC, HBM_SPEC, HBM_SPEC),
        scratch_shapes=[
            pltpu.VMEM((PAIRS, ROWS, LANES), BF),
            pltpu.VMEM((4 * PAIRS, ROWS, LANES), BF),
            pltpu.VMEM((D, ROWS), BF),
            pltpu.VMEM((ROWS, D), BF),
            pltpu.VMEM((GROUP, LANES, TILE), F32),
            pltpu.VMEM((PAIRS, LANES, ROWS), BF),
            pltpu.VMEM((GROUP, ROWS, LANES), F32),
            pltpu.VMEM((GROUP, ROWS, LANES), F32),
            pltpu.SMEM((LEN_BLK,), jnp.int32),
            pltpu.SemaphoreType.DMA((3, TILES)),
            pltpu.SemaphoreType.DMA((9,)),
            pltpu.VMEM((PAIRS, ROWS, LANES), BF),
        ]
        + saved_shapes(pltpu.VMEM)[:5]
        + [pltpu.VMEM((D, 4 * D), BF), pltpu.VMEM((D, D), BF)],
        compiler_params=params(44),
        name="backward_layer",
    )(lens, own, got_rows, got_grads, *saved[:6], w_proj, w_out, gain_in, gain_attn)


def gradient_terms(own, d_hidden, scaled, mixed, cot):
    half = struct((HALF, LANES), BF)
    return pl.pallas_call(
        terms_kernel,
        out_shape=(half, half),
        in_specs=[SMEM_SPEC] + [HBM_SPEC] * 4,
        out_specs=(VMEM_SPEC, VMEM_SPEC),
        scratch_shapes=[
            pltpu.VMEM((4 * PAIRS, ROWS, LANES), BF),
            pltpu.VMEM((D, ROWS), BF),
            pltpu.VMEM((D, ROWS), BF),
            pltpu.VMEM((ROWS, D), BF),
            pltpu.SemaphoreType.DMA((11,)),
        ],
        compiler_params=params(40),
        cost_estimate=pl.CostEstimate(
            flops=10 * ROWS * D * D, transcendentals=0, bytes_accessed=10 * MIB
        ),
        name="gradient_terms",
    )(own, d_hidden, scaled, mixed, cot)


def in_hbm(array):
    return pltpu.with_memory_space_constraint(array, pltpu.HBM)


def per_device(events, cotangent, lengths, gain_in, w_proj, gain_attn, w_out):
    own = lax.axis_index(("chip", "core")).astype(jnp.int32).reshape(1)
    lens = lengths[0]
    got_rows = lax.all_to_all(send_blocks(lens, own, events), ("chip", "core"), 0, 0, tiled=True)
    got_grads = lax.all_to_all(send_blocks(lens, own, cotangent), ("chip", "core"), 0, 0, tiled=True)
    gain_in = gain_in.reshape(1, D)
    gain_attn = gain_attn.reshape(1, D)
    saved = [in_hbm(x) for x in forward_layer(lens, own, got_rows, w_proj, gain_in)]
    send_back, *kept = backward_layer(
        lens, own, got_rows, got_grads, saved, w_proj, in_hbm(w_out), gain_in, gain_attn
    )
    came_back = lax.all_to_all(send_back, ("chip", "core"), 0, 0, tiled=True)
    d_hidden, mixed, cot = (in_hbm(x) for x in kept)
    keep, send = gradient_terms(own, d_hidden, saved[6], mixed, cot)
    send, came_back = lax.optimization_barrier((send, came_back))
    swap = [(0, 1), (1, 0)]
    other = lax.ppermute(send, "core", swap)
    chip_sum = (keep.astype(F32) + other.astype(F32)).astype(BF)
    parts = lax.all_to_all(chip_sum.reshape(64, PART, LANES), ("grp", "chip"), 0, 0, tiled=True)
    total = (jnp.sum(parts.astype(F32), axis=0) * (1.0 / DEVICES)).astype(BF)
    copies = jnp.broadcast_to(total[None], (64, PART, LANES))
    mine = lax.all_to_all(copies, ("grp", "chip"), 0, 0, tiled=True).reshape(HALF, LANES)
    d_rows = pl.pallas_call(
        home_kernel,
        out_shape=struct((LOCAL, BLOCK, D), BF),
        in_specs=[SMEM_SPEC, SMEM_SPEC, VMEM_SPEC],
        out_specs=VMEM_SPEC,
        name="take_home",
    )(lens, own, came_back)
    mine, d_rows = lax.optimization_barrier((mine, d_rows))
    others = lax.ppermute(mine, "core", swap)
    grads = (struct((D, 4 * D), F32), struct((D, D), F32))
    scratch = [pltpu.VMEM((10, D, LANES), F32), pltpu.SemaphoreType.DMA((10,))]
    sums = (2, D, LANES)
    grad_proj, grad_out, mine_sums = pl.pallas_call(
        spread_mine,
        out_shape=grads + (struct(sums, F32),),
        in_specs=[SMEM_SPEC, VMEM_SPEC, VMEM_SPEC, VMEM_SPEC],
        out_specs=(ANY_SPEC, ANY_SPEC, VMEM_SPEC),
        scratch_shapes=scratch,
        compiler_params=params(24),
        name="spread_mine",
    )(own, mine, w_proj, w_out)
    gain = struct((1, D), F32)
    grad_proj, grad_out, grad_in, grad_attn = pl.pallas_call(
        spread_other,
        out_shape=grads + (gain, gain),
        in_specs=[SMEM_SPEC] + [VMEM_SPEC] * 6 + [ANY_SPEC] * 2,
        out_specs=(ANY_SPEC, ANY_SPEC, VMEM_SPEC, VMEM_SPEC),
        scratch_shapes=scratch[:1] + [pltpu.VMEM(sums, F32)] + scratch[1:],
        input_output_aliases={7: 0, 8: 1},
        compiler_params=params(24),
        name="spread_other",
    )(own, others, w_proj, w_out, gain_in, gain_attn, mine_sums, grad_proj, grad_out)
    return (
        d_rows.reshape(1, LOCAL * BLOCK, D),
        grad_proj,
        grad_out,
        grad_in.reshape(D),
        grad_attn.reshape(D),
    )


def solution(mesh):
    fine = Mesh(mesh.devices.reshape(8, 8, 2), ("grp", "chip", "core"))
    rows = P("grp", ("chip", "core"), None)
    return jax.shard_map(
        per_device,
        mesh=fine,
        in_specs=(rows, rows, P("grp", None), P(), P(), P(), P()),
        out_specs=(rows, P(), P(), P(), P()),
        check_vma=False,
    )
```

```python
import jax
import jax.numpy as jnp
from jax import lax
from jax.experimental import pallas as pl
from jax.experimental.pallas import tpu as pltpu
from jax.sharding import Mesh, PartitionSpec as P

D = 512
HEADS = 8
BLOCK = 64
LEN_BLK = 16
SEQ = 16
PEERS = 16
LOCAL = 8
TILE = 256
TILES = 4
ROWS = 1024
LANES = 128
PAIRS = 4
PART = 80
HALF = 64 * PART
EPS = 1e-06
DEVICES = 128
BF = jnp.bfloat16
F32 = jnp.float32
MIB = 1024 * 1024

SMEM_SPEC = pl.BlockSpec(memory_space=pltpu.SMEM)
ANY_SPEC = pl.BlockSpec(memory_space=pl.ANY)
VMEM_SPEC = pl.BlockSpec(memory_space=pltpu.VMEM)
HBM_SPEC = pl.BlockSpec(memory_space=pltpu.HBM)


def dot(left, right):
    return lax.dot_general(left, right, (((1,), (0,)), ((), ())), preferred_element_type=F32)


def dot_cols(left, right):
    return lax.dot_general(left, right, (((1,), (1,)), ((), ())), preferred_element_type=F32)


def dot_rows(left, right):
    return lax.dot_general(left, right, (((0,), (0,)), ((), ())), preferred_element_type=F32)


def packing(len_ref):
    starts, sizes, ranks = [], [], []
    start = jnp.int32(0)
    rank = jnp.int32(0)
    held = jnp.int32(0)
    for i in range(SEQ):
        size = len_ref[i]
        fresh = held + size > LEN_BLK
        rank = jnp.where(fresh, rank + 1, rank)
        held = jnp.where(fresh, size, held + size)
        starts.append(start)
        sizes.append(size)
        ranks.append(rank)
        start = start + size
    return starts, sizes, ranks


def owners(len_ref, own):
    starts, _, ranks = packing(len_ref)
    found = []
    for k in range(LOCAL):
        block = own + PEERS * k
        owner = ranks[0]
        for i in range(1, SEQ):
            owner = jnp.where(starts[i] <= block, ranks[i], owner)
        found.append(owner)
    return found


def holdings(len_ref, own):
    starts, sizes, ranks = packing(len_ref)
    first = jnp.int32(LEN_BLK * LOCAL)
    count = jnp.int32(0)
    for i in range(SEQ):
        mine = ranks[i] == own
        first = jnp.where(mine, jnp.minimum(first, starts[i]), first)
        count = jnp.where(mine, count + sizes[i], count)
    return starts, sizes, ranks, first, count


def history_starts(hist_ref, own, starts, sizes, ranks, first):
    for j in range(LEN_BLK):
        hist_ref[j] = j
    for i in range(SEQ):

        @pl.when(ranks[i] == own)
        def _(i=i):
            begin = starts[i] - first

            def put(j, carry):
                hist_ref[j] = begin
                return carry

            lax.fori_loop(begin, begin + sizes[i], put, 0)


def send_kernel(len_ref, own_ref, rows_ref, out_ref):
    owner = owners(len_ref, own_ref[0])
    for k in range(LOCAL):
        out_ref[owner[k]] = rows_ref[k]


def home_kernel(len_ref, own_ref, back_ref, out_ref):
    owner = owners(len_ref, own_ref[0])
    for k in range(LOCAL):
        out_ref[k] = back_ref[owner[k]]


def tile_rows(ref, t, first, count):
    slots = [(first + t * 4 + b) & (PEERS - 1) for b in range(4)]
    tile = jnp.concatenate([ref[slot] for slot in slots], axis=0).astype(F32)
    place = lax.broadcasted_iota(jnp.int32, (TILE, D), 0) + t * TILE
    return jnp.where(place < count * BLOCK, tile, 0.0)


def normed_rows(values):
    centred = values - jnp.mean(values, axis=-1, keepdims=True)
    rstd = lax.rsqrt(jnp.mean(centred * centred, axis=-1, keepdims=True) + EPS)
    return centred * rstd, rstd


def head_masks():
    lane = lax.broadcasted_iota(jnp.int32, (1, LANES), 1)
    low = (lane < 64).astype(F32).astype(BF)
    high = (lane >= 64).astype(F32).astype(BF)
    return low, high


GROUP = 4


def rows_at(t):
    return pl.ds(pl.multiple_of(t * TILE, TILE), TILE)


def block_starts(hist_ref, t, shape, dim):
    place = lax.broadcasted_iota(jnp.int32, shape, dim)
    begin = jnp.full(shape, hist_ref[4 * t], jnp.int32)
    for b in range(1, 4):
        begin = jnp.where(place >= b * BLOCK, hist_ref[4 * t + b], begin)
    return begin * BLOCK


def key_tiles(hist_ref, i):
    low = hist_ref[4 * i] // 4
    clear = jnp.minimum((hist_ref[4 * i + 3] + 3) // 4, i)
    return low, jnp.maximum(clear, low)


def forward_kernel(
    len_ref,
    own_ref,
    got_ref,
    w_ref,
    gain_ref,
    attn_ref,
    upper_out,
    values_out,
    query_out,
    keys_out,
    slope_out,
    scaled_out,
    upper_ref,
    values_ref,
    query_ref,
    keys_ref,
    slope_ref,
    scaled_ref,
    acc_ref,
    hist_ref,
    save_sems,
):
    own = own_ref[0]
    starts, sizes, ranks, first, count = holdings(len_ref, own)
    history_starts(hist_ref, own, starts, sizes, ranks, first)
    live = (count + 3) // 4

    def project(t, carry):
        normed, _ = normed_rows(tile_rows(got_ref, t, first, count))
        scaled = (normed * gain_ref[...]).astype(BF)
        rows = rows_at(t)
        scaled_ref[rows, :] = scaled
        for quarter in range(4):
            half = 0.5 * dot(scaled, w_ref[:, quarter * D : (quarter + 1) * D])
            swing = jnp.tanh(half)
            active = half + half * swing
            slope = ((0.5 + 0.5 * swing) * (1.0 + (half - half * swing))).astype(BF)
            if quarter == 0:
                upper_ref[rows, :] = active.astype(BF)
            if quarter == 2:
                active = active * 0.0625
            active = active.astype(BF)
            for p in range(PAIRS):
                lanes = slice(p * LANES, (p + 1) * LANES)
                slope_ref[quarter * PAIRS + p, rows, :] = slope[:, lanes]
                if quarter:
                    ref = (None, values_ref, query_ref, keys_ref)[quarter]
                    ref[p, rows, :] = active[:, lanes]
        return carry

    lax.fori_loop(0, live, project, 0)

    def clear(t, carry):
        scaled_ref[rows_at(t), :] = jnp.zeros((TILE, D), BF)
        return carry

    lax.fori_loop(live, TILES, clear, 0)

    saves = [
        pltpu.make_async_copy(src, dst, save_sems.at[n])
        for n, (src, dst) in enumerate(
            (
                (upper_ref, upper_out),
                (values_ref, values_out),
                (query_ref, query_out),
                (keys_ref, keys_out),
                (slope_ref, slope_out),
                (scaled_ref, scaled_out),
            )
        )
    ]
    for save in saves:
        save.start()

    masks = head_masks()

    def group(g, carry):
        def query_tile(i, carry):
            acc_ref[...] = jnp.zeros((GROUP, TILE, LANES), F32)

            def step(j, masked):
                if masked:
                    shape = (TILE, TILE)
                    col = lax.broadcasted_iota(jnp.int32, shape, 1) + j * TILE
                    row = lax.broadcasted_iota(jnp.int32, shape, 0) + i * TILE
                    allowed = (col <= row) & (col >= block_starts(hist_ref, i, shape, 0))
                for n in range(GROUP):
                    p = g * GROUP + n
                    query = query_ref[p, rows_at(i), :]
                    keys = keys_ref[p, rows_at(j), :]
                    values = values_ref[p, rows_at(j), :]
                    total = acc_ref[n]
                    for mask in masks:
                        half = dot_cols(query, keys * mask)
                        weights = half + half * jnp.tanh(half)
                        if masked:
                            weights = jnp.where(allowed, weights, 0.0)
                        total += dot(weights.astype(BF), values * mask)
                    acc_ref[n] = total

            low, clear_from = key_tiles(hist_ref, i)

            def masked_step(j, carry):
                step(j, True)
                return carry

            def clear_step(j, carry):
                step(j, False)
                return carry

            lax.fori_loop(low, clear_from, masked_step, 0)
            lax.fori_loop(clear_from, i, clear_step, 0)
            step(i, True)
            for n in range(GROUP):
                attn_ref[g * GROUP + n, rows_at(i), :] = acc_ref[n].astype(BF)
            return carry

        return lax.fori_loop(0, live, query_tile, carry)

    lax.fori_loop(0, PAIRS // GROUP, group, 0)
    for save in saves:
        save.wait()


def backward_kernel(
    len_ref,
    own_ref,
    got_ref,
    grads_ref,
    attn_in,
    upper_in,
    values_in,
    query_in,
    keys_in,
    slope_in,
    w_in,
    w_out_in,
    gain_in_ref,
    gain_attn_ref,
    back_ref,
    d_hidden_out,
    mixed_out,
    cot_out,
    d_attn_ref,
    d_hidden_ref,
    mixed_ref,
    cot_rows_ref,
    d_query_ref,
    keys_t_ref,
    d_keys_ref,
    d_values_ref,
    hist_ref,
    tile_sems,
    load_sems,
    attn_ref,
    upper_ref,
    values_ref,
    query_ref,
    keys_ref,
    slope_ref,
    w_ref,
    w_out_ref,
):
    own = own_ref[0]
    starts, sizes, ranks, first, count = holdings(len_ref, own)
    live = (count + 3) // 4
    early = pl.ds(0, PAIRS)
    late = pl.ds(PAIRS, 3 * PAIRS)

    def tile_loads(t):
        rows = rows_at(t)
        return [
            pltpu.make_async_copy(
                attn_in.at[:, rows], attn_ref.at[:, rows], tile_sems.at[0, t]
            ),
            pltpu.make_async_copy(upper_in.at[rows], upper_ref.at[rows], tile_sems.at[1, t]),
            pltpu.make_async_copy(
                slope_in.at[early, rows], slope_ref.at[early, rows], tile_sems.at[2, t]
            ),
        ]

    loads = [
        pltpu.make_async_copy(src, dst, load_sems.at[n])
        for n, (src, dst) in enumerate(
            (
                (w_out_in, w_out_ref),
                (keys_in, keys_ref),
                (query_in, query_ref),
                (values_in, values_ref),
                (slope_in.at[late], slope_ref.at[late]),
                (w_in, w_ref),
            )
        )
    ]
    loads[0].start()

    def request(t, carry):
        for load in tile_loads(t):
            load.start()
        return carry

    lax.fori_loop(0, live, request, 0)
    for load in loads[1:]:
        load.start()
    history_starts(hist_ref, own, starts, sizes, ranks, first)
    loads[0].wait()

    def middle(t, carry):
        rows = rows_at(t)
        for load in tile_loads(t):
            load.wait()
        attn = jnp.concatenate([attn_ref[p, rows, :] for p in range(PAIRS)], axis=1)
        normed, rstd = normed_rows(attn.astype(F32))
        upper = upper_ref[rows, :].astype(F32)
        cot = tile_rows(grads_ref, t, first, count).astype(BF)
        d_mixed = dot_cols(cot, w_out_ref[...])
        gained = normed * gain_attn_ref[...]
        mixed_ref[rows, :] = (gained * upper).astype(BF)
        cot_rows_ref[rows, :] = cot
        d_upper = d_mixed * gained
        pull = d_mixed * upper
        pull = pull * gain_attn_ref[...]
        d_attn = rstd * (
            pull
            - jnp.mean(pull, axis=-1, keepdims=True)
            - normed * jnp.mean(pull * normed, axis=-1, keepdims=True)
        )
        for p in range(PAIRS):
            lanes = slice(p * LANES, (p + 1) * LANES)
            d_attn_ref[p, rows, :] = d_attn[:, lanes].astype(BF)
            slope = slope_ref[p, rows, :].astype(F32)
            d_hidden_ref[p, rows, :] = (d_upper[:, lanes] * slope).astype(BF)
        return carry

    lax.fori_loop(0, live, middle, 0)

    def clear(t, carry):
        d_hidden_ref[:, rows_at(t), :] = jnp.zeros((4 * PAIRS, TILE, LANES), BF)
        mixed_ref[rows_at(t), :] = jnp.zeros((TILE, D), BF)
        cot_rows_ref[rows_at(t), :] = jnp.zeros((TILE, D), BF)
        return carry

    lax.fori_loop(live, TILES, clear, 0)
    saves = [
        pltpu.make_async_copy(mixed_ref, mixed_out, load_sems.at[7]),
        pltpu.make_async_copy(cot_rows_ref, cot_out, load_sems.at[8]),
    ]
    for save in saves:
        save.start()

    masks = head_masks()
    for load in loads[1:5]:
        load.wait()

    def turn(t, carry):
        for p in range(PAIRS):
            keys_t_ref[p, :, rows_at(t)] = keys_ref[p, rows_at(t), :].T
        return carry

    lax.fori_loop(0, live, turn, 0)

    def group(g, carry):
        d_keys_ref[...] = jnp.zeros((GROUP, ROWS, LANES), F32)
        d_values_ref[...] = jnp.zeros((GROUP, ROWS, LANES), F32)

        def query_tile(i, carry):
            d_query_ref[...] = jnp.zeros((GROUP, LANES, TILE), F32)

            def step(j, masked):
                rows = rows_at(j)
                if masked:
                    shape = (TILE, TILE)
                    key_row = lax.broadcasted_iota(jnp.int32, shape, 0) + j * TILE
                    query_row = lax.broadcasted_iota(jnp.int32, shape, 1) + i * TILE
                    allowed = (key_row <= query_row) & (
                        key_row >= block_starts(hist_ref, i, shape, 1)
                    )
                for n in range(GROUP):
                    p = g * GROUP + n
                    query = query_ref[p, rows_at(i), :]
                    d_attn = d_attn_ref[p, rows_at(i), :]
                    keys = keys_ref[p, rows, :]
                    values = values_ref[p, rows, :]
                    d_keys = d_keys_ref[n, rows, :]
                    d_values = d_values_ref[n, rows, :]
                    for h, mask in enumerate(masks):
                        masked_keys = keys * mask
                        half = dot_cols(masked_keys, query)
                        swing = jnp.tanh(half)
                        bend = half * swing
                        weights = half + bend
                        slope = (1.0 + swing) * ((1.0 + half) - bend)
                        grad = dot_cols(values * mask, d_attn) * slope
                        if masked:
                            weights = jnp.where(allowed, weights, 0.0)
                            grad = jnp.where(allowed, grad, 0.0)
                        grad = grad.astype(BF)
                        d_values += dot(weights.astype(BF), d_attn * mask)
                        d_keys += dot(grad, query * mask)
                        head_rows = slice(h * 64, h * 64 + 64)
                        d_query_ref[n, head_rows, :] += dot(keys_t_ref[p, head_rows, rows], grad)
                    d_keys_ref[n, rows, :] = d_keys
                    d_values_ref[n, rows, :] = d_values

            low, clear_from = key_tiles(hist_ref, i)

            def masked_step(j, carry):
                step(j, True)
                return carry

            def clear_step(j, carry):
                step(j, False)
                return carry

            lax.fori_loop(low, clear_from, masked_step, 0)
            lax.fori_loop(clear_from, i, clear_step, 0)
            step(i, True)
            for n in range(GROUP):
                place = 2 * PAIRS + g * GROUP + n
                slope = slope_ref[place, rows_at(i), :].astype(F32)
                d_hidden_ref[place, rows_at(i), :] = (d_query_ref[n].T * 0.0625 * slope).astype(BF)
            return carry

        lax.fori_loop(0, live, query_tile, 0)

        def finish(t, carry):
            rows = rows_at(t)
            for n in range(GROUP):
                for quarter, ref in ((1, d_values_ref), (3, d_keys_ref)):
                    place = quarter * PAIRS + g * GROUP + n
                    slope = slope_ref[place, rows, :].astype(F32)
                    d_hidden_ref[place, rows, :] = (ref[n, rows, :] * slope).astype(BF)
            return carry

        lax.fori_loop(0, live, finish, 0)
        return carry

    lax.fori_loop(0, PAIRS // GROUP, group, 0)

    saves.append(pltpu.make_async_copy(d_hidden_ref, d_hidden_out, load_sems.at[6]))
    saves[-1].start()
    loads[5].wait()

    def final(t, carry):
        rows = rows_at(t)
        normed, rstd = normed_rows(tile_rows(got_ref, t, first, count))
        d_scaled = jnp.zeros((TILE, D), F32)
        for c in range(8):
            part = jnp.concatenate(
                [d_hidden_ref[2 * c, rows, :], d_hidden_ref[2 * c + 1, rows, :]], axis=1
            )
            d_scaled += dot_cols(part, w_ref[:, c * 256 : (c + 1) * 256])
        pull = d_scaled * gain_in_ref[...]
        d_rows = rstd * (
            pull
            - jnp.mean(pull, axis=-1, keepdims=True)
            - normed * jnp.mean(pull * normed, axis=-1, keepdims=True)
        )
        d_rows = (d_rows + cot_rows_ref[rows, :].astype(F32)).astype(BF)
        for b in range(4):
            slot = (first + t * 4 + b) & (PEERS - 1)
            back_ref[slot] = d_rows[b * BLOCK : (b + 1) * BLOCK, :]
        return carry

    lax.fori_loop(0, live, final, 0)

    for save in saves:
        save.wait()


def terms_kernel(
    own_ref,
    d_hidden_in,
    scaled_in,
    mixed_in,
    cot_in,
    keep_ref,
    send_low_ref,
    send_high_ref,
    d_hidden_ref,
    scaled_ref,
    mixed_ref,
    cot_ref,
    turned_ref,
    sems,
):
    core = own_ref[0] & 1
    loads = [
        pltpu.make_async_copy(mixed_in, mixed_ref, sems.at[9]),
        pltpu.make_async_copy(cot_in, cot_ref, sems.at[10]),
        pltpu.make_async_copy(scaled_in, scaled_ref, sems.at[8]),
    ]
    for c in range(8):
        part = pl.ds(2 * c, 2)
        loads.append(
            pltpu.make_async_copy(d_hidden_in.at[part], d_hidden_ref.at[part], sems.at[c])
        )
    for load in loads:
        load.start()

    def put_piece(piece, values):
        half, place = divmod(piece, 10)
        values = values.astype(BF)

        @pl.when(core == half)
        def _():
            keep_ref[place * D : (place + 1) * D, :] = values

        @pl.when(core != half)
        def _():
            send_ref = (send_low_ref, send_high_ref)[place // 5]
            send_ref[place % 5 * D : (place % 5 + 1) * D, :] = values

    loads[0].wait()
    turned_ref[...] = mixed_ref[...].T
    loads[1].wait()
    for c in range(2):
        term = dot(turned_ref[...], cot_ref[:, c * 256 : (c + 1) * 256])
        put_piece(16 + 2 * c, term[:, :LANES])
        put_piece(17 + 2 * c, term[:, LANES:])
    loads[2].wait()
    turned_ref[...] = scaled_ref[...].T
    for c in range(8):
        loads[3 + c].wait()
        part = jnp.concatenate([d_hidden_ref[2 * c], d_hidden_ref[2 * c + 1]], axis=1)
        term = dot(turned_ref[...], part)
        put_piece(2 * c, term[:, :LANES])
        put_piece(2 * c + 1, term[:, LANES:])


def spread_half(half, half_ref, w_ref, w_out_ref, proj_ref, out_ref, wide_ref, sums_ref, sems):
    in_sum = jnp.zeros((D, LANES), F32)
    attn_sum = jnp.zeros((D, LANES), F32)
    for place in range(10):
        piece = half * 10 + place
        part = half_ref[place * D : (place + 1) * D, :].astype(F32)
        wide_ref[place] = part
        if piece < 16:
            lanes = pl.ds(piece * LANES, LANES)
            target = proj_ref.at[:, lanes]
            in_sum += part * w_ref[:, lanes].astype(F32)
        else:
            lanes = pl.ds((piece - 16) * LANES, LANES)
            target = out_ref.at[:, lanes]
            attn_sum += part * w_out_ref[:, lanes].astype(F32)
        pltpu.make_async_copy(wide_ref.at[place], target, sems.at[place]).start()
    sums_ref[0] = in_sum
    sums_ref[1] = attn_sum


def spread_wait(proj_ref, wide_ref, sems):
    for place in range(10):
        target = proj_ref.at[:, pl.ds(place * LANES, LANES)]
        pltpu.make_async_copy(wide_ref.at[place], target, sems.at[place]).wait()


def spread_mine(own_ref, mine_ref, w_ref, w_out_ref, proj_ref, out_ref, sums_ref, wide_ref, sems):
    core = own_ref[0] & 1
    for half in range(2):

        @pl.when(core == half)
        def _(half=half):
            spread_half(
                half, mine_ref, w_ref, w_out_ref, proj_ref, out_ref, wide_ref, sums_ref, sems
            )

    spread_wait(proj_ref, wide_ref, sems)


def spread_other(
    own_ref,
    other_ref,
    w_ref,
    w_out_ref,
    gain_in_ref,
    gain_attn_ref,
    mine_sums_ref,
    proj_in,
    out_in,
    proj_ref,
    out_ref,
    grad_in_ref,
    grad_attn_ref,
    wide_ref,
    sums_ref,
    sems,
):
    core = own_ref[0] & 1
    for half in range(2):

        @pl.when(core != half)
        def _(half=half):
            spread_half(
                half, other_ref, w_ref, w_out_ref, proj_ref, out_ref, wide_ref, sums_ref, sems
            )

    for n, (gain_ref, grad_ref) in enumerate(
        ((gain_in_ref, grad_in_ref), (gain_attn_ref, grad_attn_ref))
    ):
        total = (sums_ref[n] + mine_sums_ref[n]).T
        grad_ref[...] = jnp.sum(total, axis=0, keepdims=True) / gain_ref[...]
    spread_wait(proj_ref, wide_ref, sems)


def struct(shape, dtype):
    return jax.ShapeDtypeStruct(shape, dtype)


def params(mebibytes):
    return pltpu.CompilerParams(vmem_limit_bytes=mebibytes * MIB)


def send_blocks(lens, own, rows):
    return pl.pallas_call(
        send_kernel,
        out_shape=struct((PEERS, BLOCK, D), BF),
        in_specs=[SMEM_SPEC, SMEM_SPEC, VMEM_SPEC],
        out_specs=VMEM_SPEC,
        name="send_blocks",
    )(lens, own, rows.reshape(LOCAL, BLOCK, D))


def saved_shapes(make):
    pairs = make((PAIRS, ROWS, LANES), BF)
    wide = make((ROWS, D), BF)
    return [wide, pairs, pairs, pairs, make((4 * PAIRS, ROWS, LANES), BF), wide]


def forward_layer(lens, own, got_rows, w_proj, gain_in):
    return pl.pallas_call(
        forward_kernel,
        out_shape=[pltpu.HBM((PAIRS, ROWS, LANES), BF)] + saved_shapes(pltpu.HBM),
        in_specs=[SMEM_SPEC, SMEM_SPEC, VMEM_SPEC, VMEM_SPEC, VMEM_SPEC],
        out_specs=[VMEM_SPEC] + [HBM_SPEC] * 6,
        scratch_shapes=saved_shapes(pltpu.VMEM)
        + [
            pltpu.VMEM((GROUP, TILE, LANES), F32),
            pltpu.SMEM((LEN_BLK,), jnp.int32),
            pltpu.SemaphoreType.DMA((6,)),
        ],
        compiler_params=params(32),
        name="forward_layer",
    )(lens, own, got_rows, w_proj, gain_in)


def backward_layer(lens, own, got_rows, got_grads, saved, w_proj, w_out, gain_in, gain_attn):
    return pl.pallas_call(
        backward_kernel,
        out_shape=(
            pltpu.HBM((PEERS, BLOCK, D), BF),
            pltpu.HBM((4 * PAIRS, ROWS, LANES), BF),
            pltpu.HBM((ROWS, D), BF),
            pltpu.HBM((ROWS, D), BF),
        ),
        in_specs=[SMEM_SPEC] * 2 + [VMEM_SPEC] * 2 + [ANY_SPEC] * 8 + [VMEM_SPEC] * 2,
        out_specs=(VMEM_SPEC, HBM_SPEC, HBM_SPEC, HBM_SPEC),
        scratch_shapes=[
            pltpu.VMEM((PAIRS, ROWS, LANES), BF),
            pltpu.VMEM((4 * PAIRS, ROWS, LANES), BF),
            pltpu.VMEM((ROWS, D), BF),
            pltpu.VMEM((ROWS, D), BF),
            pltpu.VMEM((GROUP, LANES, TILE), F32),
            pltpu.VMEM((PAIRS, LANES, ROWS), BF),
            pltpu.VMEM((GROUP, ROWS, LANES), F32),
            pltpu.VMEM((GROUP, ROWS, LANES), F32),
            pltpu.SMEM((LEN_BLK,), jnp.int32),
            pltpu.SemaphoreType.DMA((3, TILES)),
            pltpu.SemaphoreType.DMA((9,)),
            pltpu.VMEM((PAIRS, ROWS, LANES), BF),
        ]
        + saved_shapes(pltpu.VMEM)[:5]
        + [pltpu.VMEM((D, 4 * D), BF), pltpu.VMEM((D, D), BF)],
        compiler_params=params(44),
        name="backward_layer",
    )(lens, own, got_rows, got_grads, *saved[:6], w_proj, w_out, gain_in, gain_attn)


def gradient_terms(own, d_hidden, scaled, mixed, cot):
    half = struct((HALF, LANES), BF)
    quarter = pltpu.HBM((HALF // 2, LANES), BF)
    return pl.pallas_call(
        terms_kernel,
        out_shape=(half, quarter, quarter),
        in_specs=[SMEM_SPEC] + [HBM_SPEC] * 4,
        out_specs=(VMEM_SPEC,) * 3,
        scratch_shapes=[
            pltpu.VMEM((4 * PAIRS, ROWS, LANES), BF),
            pltpu.VMEM((ROWS, D), BF),
            pltpu.VMEM((ROWS, D), BF),
            pltpu.VMEM((ROWS, D), BF),
            pltpu.VMEM((D, ROWS), BF),
            pltpu.SemaphoreType.DMA((11,)),
        ],
        compiler_params=params(40),
        cost_estimate=pl.CostEstimate(
            flops=10 * ROWS * D * D, transcendentals=0, bytes_accessed=10 * MIB
        ),
        name="gradient_terms",
    )(own, d_hidden, scaled, mixed, cot)


def in_hbm(array):
    return pltpu.with_memory_space_constraint(array, pltpu.HBM)


def per_device(events, cotangent, lengths, gain_in, w_proj, gain_attn, w_out):
    own = lax.axis_index(("chip", "core")).astype(jnp.int32).reshape(1)
    lens = lengths[0]
    got_rows = lax.all_to_all(send_blocks(lens, own, events), ("chip", "core"), 0, 0, tiled=True)
    got_grads = lax.all_to_all(send_blocks(lens, own, cotangent), ("chip", "core"), 0, 0, tiled=True)
    gain_in = gain_in.reshape(1, D)
    gain_attn = gain_attn.reshape(1, D)
    saved = [in_hbm(x) for x in forward_layer(lens, own, got_rows, w_proj, gain_in)]
    send_back, *kept = backward_layer(
        lens, own, got_rows, got_grads, saved, w_proj, in_hbm(w_out), gain_in, gain_attn
    )
    came_back = lax.all_to_all(send_back, ("chip", "core"), 0, 0, tiled=True)
    d_hidden, mixed, cot = (in_hbm(x) for x in kept)
    keep, *send = gradient_terms(own, d_hidden, saved[6], mixed, cot)
    swap = [(0, 1), (1, 0)]
    send[0], came_back = lax.optimization_barrier((send[0], came_back))
    other = jnp.concatenate([lax.ppermute(part, "core", swap) for part in send])
    chip_sum = (keep.astype(F32) + other.astype(F32)).astype(BF)
    parts = lax.all_to_all(chip_sum.reshape(64, PART, LANES), ("grp", "chip"), 0, 0, tiled=True)
    total = (jnp.sum(parts.astype(F32), axis=0) * (1.0 / DEVICES)).astype(BF)
    copies = jnp.broadcast_to(total[None], (64, PART, LANES))
    mine = lax.all_to_all(copies, ("grp", "chip"), 0, 0, tiled=True).reshape(HALF, LANES)
    d_rows = pl.pallas_call(
        home_kernel,
        out_shape=struct((LOCAL, BLOCK, D), BF),
        in_specs=[SMEM_SPEC, SMEM_SPEC, VMEM_SPEC],
        out_specs=VMEM_SPEC,
        name="take_home",
    )(lens, own, came_back)
    mine, d_rows = lax.optimization_barrier((mine, d_rows))
    others = lax.ppermute(mine, "core", swap)
    grads = (struct((D, 4 * D), F32), struct((D, D), F32))
    scratch = [pltpu.VMEM((10, D, LANES), F32), pltpu.SemaphoreType.DMA((10,))]
    sums = (2, D, LANES)
    grad_proj, grad_out, mine_sums = pl.pallas_call(
        spread_mine,
        out_shape=grads + (struct(sums, F32),),
        in_specs=[SMEM_SPEC, VMEM_SPEC, VMEM_SPEC, VMEM_SPEC],
        out_specs=(ANY_SPEC, ANY_SPEC, VMEM_SPEC),
        scratch_shapes=scratch,
        compiler_params=params(24),
        name="spread_mine",
    )(own, mine, w_proj, w_out)
    gain = struct((1, D), F32)
    grad_proj, grad_out, grad_in, grad_attn = pl.pallas_call(
        spread_other,
        out_shape=grads + (gain, gain),
        in_specs=[SMEM_SPEC] + [VMEM_SPEC] * 6 + [ANY_SPEC] * 2,
        out_specs=(ANY_SPEC, ANY_SPEC, VMEM_SPEC, VMEM_SPEC),
        scratch_shapes=scratch[:1] + [pltpu.VMEM(sums, F32)] + scratch[1:],
        input_output_aliases={7: 0, 8: 1},
        compiler_params=params(24),
        name="spread_other",
    )(own, others, w_proj, w_out, gain_in, gain_attn, mine_sums, grad_proj, grad_out)
    return (
        d_rows.reshape(1, LOCAL * BLOCK, D),
        grad_proj,
        grad_out,
        grad_in.reshape(D),
        grad_attn.reshape(D),
    )


def solution(mesh):
    fine = Mesh(mesh.devices.reshape(8, 8, 2), ("grp", "chip", "core"))
    rows = P("grp", ("chip", "core"), None)
    return jax.shard_map(
        per_device,
        mesh=fine,
        in_specs=(rows, rows, P("grp", None), P(), P(), P(), P()),
        out_specs=(rows, P(), P(), P(), P()),
        check_vma=False,
    )
```

```python
import jax
import jax.numpy as jnp
from jax import lax
from jax.experimental import pallas as pl
from jax.experimental.pallas import tpu as pltpu
from jax.sharding import Mesh, PartitionSpec as P

D = 512
HEADS = 8
BLOCK = 64
LEN_BLK = 16
SEQ = 16
PEERS = 16
LOCAL = 8
TILE = 256
TILES = 4
ROWS = 1024
LANES = 128
PAIRS = 4
PART = 80
HALF = 64 * PART
EPS = 1e-06
DEVICES = 128
BF = jnp.bfloat16
F32 = jnp.float32
MIB = 1024 * 1024

SMEM_SPEC = pl.BlockSpec(memory_space=pltpu.SMEM)
ANY_SPEC = pl.BlockSpec(memory_space=pl.ANY)
VMEM_SPEC = pl.BlockSpec(memory_space=pltpu.VMEM)
HBM_SPEC = pl.BlockSpec(memory_space=pltpu.HBM)


def dot(left, right):
    return lax.dot_general(left, right, (((1,), (0,)), ((), ())), preferred_element_type=F32)


def dot_cols(left, right):
    return lax.dot_general(left, right, (((1,), (1,)), ((), ())), preferred_element_type=F32)


def dot_rows(left, right):
    return lax.dot_general(left, right, (((0,), (0,)), ((), ())), preferred_element_type=F32)


def packing(len_ref):
    starts, sizes, ranks = [], [], []
    start = jnp.int32(0)
    rank = jnp.int32(0)
    held = jnp.int32(0)
    for i in range(SEQ):
        size = len_ref[i]
        fresh = held + size > LEN_BLK
        rank = jnp.where(fresh, rank + 1, rank)
        held = jnp.where(fresh, size, held + size)
        starts.append(start)
        sizes.append(size)
        ranks.append(rank)
        start = start + size
    return starts, sizes, ranks


def owners(len_ref, own):
    starts, _, ranks = packing(len_ref)
    found = []
    for k in range(LOCAL):
        block = own + PEERS * k
        owner = ranks[0]
        for i in range(1, SEQ):
            owner = jnp.where(starts[i] <= block, ranks[i], owner)
        found.append(owner)
    return found


def holdings(len_ref, own):
    starts, sizes, ranks = packing(len_ref)
    first = jnp.int32(LEN_BLK * LOCAL)
    count = jnp.int32(0)
    for i in range(SEQ):
        mine = ranks[i] == own
        first = jnp.where(mine, jnp.minimum(first, starts[i]), first)
        count = jnp.where(mine, count + sizes[i], count)
    return starts, sizes, ranks, first, count


def history_starts(hist_ref, own, starts, sizes, ranks, first):
    for j in range(LEN_BLK):
        hist_ref[j] = j
    for i in range(SEQ):

        @pl.when(ranks[i] == own)
        def _(i=i):
            begin = starts[i] - first

            def put(j, carry):
                hist_ref[j] = begin
                return carry

            lax.fori_loop(begin, begin + sizes[i], put, 0)


def send_kernel(len_ref, own_ref, rows_ref, out_ref):
    owner = owners(len_ref, own_ref[0])
    for k in range(LOCAL):
        out_ref[owner[k]] = rows_ref[k]


def home_kernel(len_ref, own_ref, back_ref, out_ref):
    owner = owners(len_ref, own_ref[0])
    for k in range(LOCAL):
        out_ref[k] = back_ref[owner[k]]


def tile_rows(ref, t, first, count):
    slots = [(first + t * 4 + b) & (PEERS - 1) for b in range(4)]
    tile = jnp.concatenate([ref[slot] for slot in slots], axis=0).astype(F32)
    place = lax.broadcasted_iota(jnp.int32, (TILE, D), 0) + t * TILE
    return jnp.where(place < count * BLOCK, tile, 0.0)


def normed_rows(values):
    centred = values - jnp.mean(values, axis=-1, keepdims=True)
    rstd = lax.rsqrt(jnp.mean(centred * centred, axis=-1, keepdims=True) + EPS)
    return centred * rstd, rstd


def head_masks():
    lane = lax.broadcasted_iota(jnp.int32, (1, LANES), 1)
    low = (lane < 64).astype(F32).astype(BF)
    high = (lane >= 64).astype(F32).astype(BF)
    return low, high


GROUP = 4


def rows_at(t):
    return pl.ds(pl.multiple_of(t * TILE, TILE), TILE)


def block_starts(hist_ref, t, shape, dim):
    place = lax.broadcasted_iota(jnp.int32, shape, dim)
    begin = jnp.full(shape, hist_ref[4 * t], jnp.int32)
    for b in range(1, 4):
        begin = jnp.where(place >= b * BLOCK, hist_ref[4 * t + b], begin)
    return begin * BLOCK


def key_tiles(hist_ref, i):
    low = hist_ref[4 * i] // 4
    clear = jnp.minimum((hist_ref[4 * i + 3] + 3) // 4, i)
    return low, jnp.maximum(clear, low)


def forward_kernel(
    len_ref,
    own_ref,
    got_ref,
    w_ref,
    gain_ref,
    attn_ref,
    upper_out,
    values_out,
    query_out,
    keys_out,
    slope_out,
    scaled_out,
    upper_ref,
    values_ref,
    query_ref,
    keys_ref,
    slope_ref,
    scaled_ref,
    acc_ref,
    hist_ref,
    save_sems,
):
    own = own_ref[0]
    starts, sizes, ranks, first, count = holdings(len_ref, own)
    history_starts(hist_ref, own, starts, sizes, ranks, first)
    live = (count + 3) // 4

    def project(t, carry):
        normed, _ = normed_rows(tile_rows(got_ref, t, first, count))
        scaled = (normed * gain_ref[...]).astype(BF)
        rows = rows_at(t)
        scaled_ref[rows, :] = scaled
        for quarter in range(4):
            half = 0.5 * dot(scaled, w_ref[:, quarter * D : (quarter + 1) * D])
            swing = jnp.tanh(half)
            active = half + half * swing
            slope = ((0.5 + 0.5 * swing) * (1.0 + (half - half * swing))).astype(BF)
            if quarter == 0:
                upper_ref[rows, :] = active.astype(BF)
            if quarter == 2:
                active = active * 0.0625
            active = active.astype(BF)
            for p in range(PAIRS):
                lanes = slice(p * LANES, (p + 1) * LANES)
                slope_ref[quarter * PAIRS + p, rows, :] = slope[:, lanes]
                if quarter:
                    ref = (None, values_ref, query_ref, keys_ref)[quarter]
                    ref[p, rows, :] = active[:, lanes]
        return carry

    lax.fori_loop(0, live, project, 0)

    def clear(t, carry):
        scaled_ref[rows_at(t), :] = jnp.zeros((TILE, D), BF)
        return carry

    lax.fori_loop(live, TILES, clear, 0)

    saves = [
        pltpu.make_async_copy(src, dst, save_sems.at[n])
        for n, (src, dst) in enumerate(
            (
                (upper_ref, upper_out),
                (values_ref, values_out),
                (query_ref, query_out),
                (keys_ref, keys_out),
                (slope_ref, slope_out),
                (scaled_ref, scaled_out),
            )
        )
    ]
    for save in saves:
        save.start()

    masks = head_masks()

    def group(g, carry):
        def query_tile(i, carry):
            acc_ref[...] = jnp.zeros((GROUP, TILE, LANES), F32)

            def step(j, masked):
                if masked:
                    shape = (TILE, TILE)
                    col = lax.broadcasted_iota(jnp.int32, shape, 1) + j * TILE
                    row = lax.broadcasted_iota(jnp.int32, shape, 0) + i * TILE
                    allowed = (col <= row) & (col >= block_starts(hist_ref, i, shape, 0))
                for n in range(GROUP):
                    p = g * GROUP + n
                    query = query_ref[p, rows_at(i), :]
                    keys = keys_ref[p, rows_at(j), :]
                    values = values_ref[p, rows_at(j), :]
                    total = acc_ref[n]
                    for mask in masks:
                        half = dot_cols(query, keys * mask)
                        weights = half + half * jnp.tanh(half)
                        if masked:
                            weights = jnp.where(allowed, weights, 0.0)
                        total += dot(weights.astype(BF), values * mask)
                    acc_ref[n] = total

            low, clear_from = key_tiles(hist_ref, i)

            def masked_step(j, carry):
                step(j, True)
                return carry

            def clear_step(j, carry):
                step(j, False)
                return carry

            lax.fori_loop(low, clear_from, masked_step, 0)
            lax.fori_loop(clear_from, i, clear_step, 0)
            step(i, True)
            for n in range(GROUP):
                attn_ref[g * GROUP + n, rows_at(i), :] = acc_ref[n].astype(BF)
            return carry

        return lax.fori_loop(0, live, query_tile, carry)

    lax.fori_loop(0, PAIRS // GROUP, group, 0)
    for save in saves:
        save.wait()


def backward_kernel(
    len_ref,
    own_ref,
    got_in,
    grads_in,
    attn_in,
    upper_in,
    values_in,
    query_in,
    keys_in,
    slope_in,
    w_in,
    w_out_in,
    gain_in_ref,
    gain_attn_ref,
    back_ref,
    d_hidden_out,
    mixed_out,
    cot_out,
    d_attn_ref,
    d_hidden_ref,
    mixed_ref,
    cot_rows_ref,
    d_query_ref,
    keys_t_ref,
    d_keys_ref,
    d_values_ref,
    hist_ref,
    tile_sems,
    load_sems,
    attn_ref,
    upper_ref,
    values_ref,
    query_ref,
    keys_ref,
    slope_ref,
    w_ref,
    w_out_ref,
    got_ref,
    grads_ref,
):
    own = own_ref[0]
    load_grads = pltpu.make_async_copy(grads_in, grads_ref, load_sems.at[9])
    load_grads.start()
    load_got = pltpu.make_async_copy(got_in, got_ref, load_sems.at[10])
    starts, sizes, ranks, first, count = holdings(len_ref, own)
    live = (count + 3) // 4
    early = pl.ds(0, PAIRS)
    late = pl.ds(PAIRS, 3 * PAIRS)

    def tile_loads(t):
        rows = rows_at(t)
        return [
            pltpu.make_async_copy(
                attn_in.at[:, rows], attn_ref.at[:, rows], tile_sems.at[0, t]
            ),
            pltpu.make_async_copy(upper_in.at[rows], upper_ref.at[rows], tile_sems.at[1, t]),
            pltpu.make_async_copy(
                slope_in.at[early, rows], slope_ref.at[early, rows], tile_sems.at[2, t]
            ),
        ]

    loads = [
        pltpu.make_async_copy(src, dst, load_sems.at[n])
        for n, (src, dst) in enumerate(
            (
                (w_out_in, w_out_ref),
                (keys_in, keys_ref),
                (query_in, query_ref),
                (values_in, values_ref),
                (slope_in.at[late], slope_ref.at[late]),
                (w_in, w_ref),
            )
        )
    ]
    loads[0].start()

    def request(t, carry):
        for load in tile_loads(t):
            load.start()
        return carry

    lax.fori_loop(0, live, request, 0)
    for load in loads[1:]:
        load.start()
    load_got.start()
    history_starts(hist_ref, own, starts, sizes, ranks, first)
    loads[0].wait()
    load_grads.wait()

    def middle(t, carry):
        rows = rows_at(t)
        for load in tile_loads(t):
            load.wait()
        attn = jnp.concatenate([attn_ref[p, rows, :] for p in range(PAIRS)], axis=1)
        normed, rstd = normed_rows(attn.astype(F32))
        upper = upper_ref[rows, :].astype(F32)
        cot = tile_rows(grads_ref, t, first, count).astype(BF)
        d_mixed = dot_cols(cot, w_out_ref[...])
        gained = normed * gain_attn_ref[...]
        mixed_ref[rows, :] = (gained * upper).astype(BF)
        cot_rows_ref[rows, :] = cot
        d_upper = d_mixed * gained
        pull = d_mixed * upper
        pull = pull * gain_attn_ref[...]
        d_attn = rstd * (
            pull
            - jnp.mean(pull, axis=-1, keepdims=True)
            - normed * jnp.mean(pull * normed, axis=-1, keepdims=True)
        )
        for p in range(PAIRS):
            lanes = slice(p * LANES, (p + 1) * LANES)
            d_attn_ref[p, rows, :] = d_attn[:, lanes].astype(BF)
            slope = slope_ref[p, rows, :].astype(F32)
            d_hidden_ref[p, rows, :] = (d_upper[:, lanes] * slope).astype(BF)
        return carry

    lax.fori_loop(0, live, middle, 0)

    def clear(t, carry):
        d_hidden_ref[:, rows_at(t), :] = jnp.zeros((4 * PAIRS, TILE, LANES), BF)
        mixed_ref[rows_at(t), :] = jnp.zeros((TILE, D), BF)
        cot_rows_ref[rows_at(t), :] = jnp.zeros((TILE, D), BF)
        return carry

    lax.fori_loop(live, TILES, clear, 0)
    saves = [
        pltpu.make_async_copy(mixed_ref, mixed_out, load_sems.at[7]),
        pltpu.make_async_copy(cot_rows_ref, cot_out, load_sems.at[8]),
    ]
    for save in saves:
        save.start()

    masks = head_masks()
    for load in loads[1:5]:
        load.wait()

    def turn(t, carry):
        for p in range(PAIRS):
            keys_t_ref[p, :, rows_at(t)] = keys_ref[p, rows_at(t), :].T
        return carry

    lax.fori_loop(0, live, turn, 0)

    def group(g, carry):
        d_keys_ref[...] = jnp.zeros((GROUP, ROWS, LANES), F32)
        d_values_ref[...] = jnp.zeros((GROUP, ROWS, LANES), F32)

        def query_tile(i, carry):
            d_query_ref[...] = jnp.zeros((GROUP, LANES, TILE), F32)

            def step(j, masked):
                rows = rows_at(j)
                if masked:
                    shape = (TILE, TILE)
                    key_row = lax.broadcasted_iota(jnp.int32, shape, 0) + j * TILE
                    query_row = lax.broadcasted_iota(jnp.int32, shape, 1) + i * TILE
                    allowed = (key_row <= query_row) & (
                        key_row >= block_starts(hist_ref, i, shape, 1)
                    )
                for n in range(GROUP):
                    p = g * GROUP + n
                    query = query_ref[p, rows_at(i), :]
                    d_attn = d_attn_ref[p, rows_at(i), :]
                    keys = keys_ref[p, rows, :]
                    values = values_ref[p, rows, :]
                    d_keys = d_keys_ref[n, rows, :]
                    d_values = d_values_ref[n, rows, :]
                    for h, mask in enumerate(masks):
                        masked_keys = keys * mask
                        half = dot_cols(masked_keys, query)
                        swing = jnp.tanh(half)
                        bend = half * swing
                        weights = half + bend
                        slope = (1.0 + swing) * ((1.0 + half) - bend)
                        grad = dot_cols(values * mask, d_attn) * slope
                        if masked:
                            weights = jnp.where(allowed, weights, 0.0)
                            grad = jnp.where(allowed, grad, 0.0)
                        grad = grad.astype(BF)
                        d_values += dot(weights.astype(BF), d_attn * mask)
                        d_keys += dot(grad, query * mask)
                        head_rows = slice(h * 64, h * 64 + 64)
                        d_query_ref[n, head_rows, :] += dot(keys_t_ref[p, head_rows, rows], grad)
                    d_keys_ref[n, rows, :] = d_keys
                    d_values_ref[n, rows, :] = d_values

            low, clear_from = key_tiles(hist_ref, i)

            def masked_step(j, carry):
                step(j, True)
                return carry

            def clear_step(j, carry):
                step(j, False)
                return carry

            lax.fori_loop(low, clear_from, masked_step, 0)
            lax.fori_loop(clear_from, i, clear_step, 0)
            step(i, True)
            for n in range(GROUP):
                place = 2 * PAIRS + g * GROUP + n
                slope = slope_ref[place, rows_at(i), :].astype(F32)
                d_hidden_ref[place, rows_at(i), :] = (d_query_ref[n].T * 0.0625 * slope).astype(BF)
            return carry

        lax.fori_loop(0, live, query_tile, 0)

        def finish(t, carry):
            rows = rows_at(t)
            for n in range(GROUP):
                for quarter, ref in ((1, d_values_ref), (3, d_keys_ref)):
                    place = quarter * PAIRS + g * GROUP + n
                    slope = slope_ref[place, rows, :].astype(F32)
                    d_hidden_ref[place, rows, :] = (ref[n, rows, :] * slope).astype(BF)
            return carry

        lax.fori_loop(0, live, finish, 0)
        return carry

    lax.fori_loop(0, PAIRS // GROUP, group, 0)

    saves.append(pltpu.make_async_copy(d_hidden_ref, d_hidden_out, load_sems.at[6]))
    saves[-1].start()
    loads[5].wait()
    load_got.wait()

    def final(t, carry):
        rows = rows_at(t)
        normed, rstd = normed_rows(tile_rows(got_ref, t, first, count))
        d_scaled = jnp.zeros((TILE, D), F32)
        for c in range(8):
            part = jnp.concatenate(
                [d_hidden_ref[2 * c, rows, :], d_hidden_ref[2 * c + 1, rows, :]], axis=1
            )
            d_scaled += dot_cols(part, w_ref[:, c * 256 : (c + 1) * 256])
        pull = d_scaled * gain_in_ref[...]
        d_rows = rstd * (
            pull
            - jnp.mean(pull, axis=-1, keepdims=True)
            - normed * jnp.mean(pull * normed, axis=-1, keepdims=True)
        )
        d_rows = (d_rows + cot_rows_ref[rows, :].astype(F32)).astype(BF)
        for b in range(4):
            slot = (first + t * 4 + b) & (PEERS - 1)
            back_ref[slot] = d_rows[b * BLOCK : (b + 1) * BLOCK, :]
        return carry

    lax.fori_loop(0, live, final, 0)

    for save in saves:
        save.wait()


def terms_kernel(
    own_ref,
    d_hidden_in,
    scaled_in,
    mixed_in,
    cot_in,
    keep_ref,
    send_low_ref,
    send_high_ref,
    d_hidden_ref,
    scaled_ref,
    mixed_ref,
    cot_ref,
    turned_ref,
    sems,
):
    core = own_ref[0] & 1
    loads = [
        pltpu.make_async_copy(mixed_in, mixed_ref, sems.at[9]),
        pltpu.make_async_copy(cot_in, cot_ref, sems.at[10]),
        pltpu.make_async_copy(scaled_in, scaled_ref, sems.at[8]),
    ]
    for c in range(8):
        part = pl.ds(2 * c, 2)
        loads.append(
            pltpu.make_async_copy(d_hidden_in.at[part], d_hidden_ref.at[part], sems.at[c])
        )
    for load in loads:
        load.start()

    def put_piece(piece, values):
        half, place = divmod(piece, 10)
        values = values.astype(BF)

        @pl.when(core == half)
        def _():
            keep_ref[place * D : (place + 1) * D, :] = values

        @pl.when(core != half)
        def _():
            send_ref = (send_low_ref, send_high_ref)[place // 5]
            send_ref[place % 5 * D : (place % 5 + 1) * D, :] = values

    loads[0].wait()
    turned_ref[...] = mixed_ref[...].T
    loads[1].wait()
    for c in range(2):
        term = dot(turned_ref[...], cot_ref[:, c * 256 : (c + 1) * 256])
        put_piece(16 + 2 * c, term[:, :LANES])
        put_piece(17 + 2 * c, term[:, LANES:])
    loads[2].wait()
    turned_ref[...] = scaled_ref[...].T
    for c in range(8):
        loads[3 + c].wait()
        part = jnp.concatenate([d_hidden_ref[2 * c], d_hidden_ref[2 * c + 1]], axis=1)
        term = dot(turned_ref[...], part)
        put_piece(2 * c, term[:, :LANES])
        put_piece(2 * c + 1, term[:, LANES:])


def spread_half(half, half_ref, w_ref, w_out_ref, proj_ref, out_ref, wide_ref, sums_ref, sems):
    in_sum = jnp.zeros((D, LANES), F32)
    attn_sum = jnp.zeros((D, LANES), F32)
    for place in range(10):
        piece = half * 10 + place
        part = half_ref[place * D : (place + 1) * D, :].astype(F32)
        wide_ref[place] = part
        if piece < 16:
            lanes = pl.ds(piece * LANES, LANES)
            target = proj_ref.at[:, lanes]
            in_sum += part * w_ref[:, lanes].astype(F32)
        else:
            lanes = pl.ds((piece - 16) * LANES, LANES)
            target = out_ref.at[:, lanes]
            attn_sum += part * w_out_ref[:, lanes].astype(F32)
        pltpu.make_async_copy(wide_ref.at[place], target, sems.at[place]).start()
    sums_ref[0] = in_sum
    sums_ref[1] = attn_sum


def spread_wait(proj_ref, wide_ref, sems):
    for place in range(10):
        target = proj_ref.at[:, pl.ds(place * LANES, LANES)]
        pltpu.make_async_copy(wide_ref.at[place], target, sems.at[place]).wait()


def spread_mine(own_ref, mine_ref, w_ref, w_out_ref, proj_ref, out_ref, sums_ref, wide_ref, sems):
    core = own_ref[0] & 1
    for half in range(2):

        @pl.when(core == half)
        def _(half=half):
            spread_half(
                half, mine_ref, w_ref, w_out_ref, proj_ref, out_ref, wide_ref, sums_ref, sems
            )

    spread_wait(proj_ref, wide_ref, sems)


def spread_other(
    own_ref,
    other_ref,
    w_ref,
    w_out_ref,
    gain_in_ref,
    gain_attn_ref,
    mine_sums_ref,
    proj_in,
    out_in,
    proj_ref,
    out_ref,
    grad_in_ref,
    grad_attn_ref,
    wide_ref,
    sums_ref,
    sems,
):
    core = own_ref[0] & 1
    for half in range(2):

        @pl.when(core != half)
        def _(half=half):
            spread_half(
                half, other_ref, w_ref, w_out_ref, proj_ref, out_ref, wide_ref, sums_ref, sems
            )

    for n, (gain_ref, grad_ref) in enumerate(
        ((gain_in_ref, grad_in_ref), (gain_attn_ref, grad_attn_ref))
    ):
        total = (sums_ref[n] + mine_sums_ref[n]).T
        grad_ref[...] = jnp.sum(total, axis=0, keepdims=True) / gain_ref[...]
    spread_wait(proj_ref, wide_ref, sems)


def struct(shape, dtype):
    return jax.ShapeDtypeStruct(shape, dtype)


def params(mebibytes):
    return pltpu.CompilerParams(vmem_limit_bytes=mebibytes * MIB)


def send_blocks(lens, own, rows):
    return pl.pallas_call(
        send_kernel,
        out_shape=struct((PEERS, BLOCK, D), BF),
        in_specs=[SMEM_SPEC, SMEM_SPEC, VMEM_SPEC],
        out_specs=VMEM_SPEC,
        name="send_blocks",
    )(lens, own, rows.reshape(LOCAL, BLOCK, D))


def saved_shapes(make):
    pairs = make((PAIRS, ROWS, LANES), BF)
    wide = make((ROWS, D), BF)
    return [wide, pairs, pairs, pairs, make((4 * PAIRS, ROWS, LANES), BF), wide]


def forward_layer(lens, own, got_rows, w_proj, gain_in):
    return pl.pallas_call(
        forward_kernel,
        out_shape=[pltpu.HBM((PAIRS, ROWS, LANES), BF)] + saved_shapes(pltpu.HBM),
        in_specs=[SMEM_SPEC, SMEM_SPEC, VMEM_SPEC, VMEM_SPEC, VMEM_SPEC],
        out_specs=[VMEM_SPEC] + [HBM_SPEC] * 6,
        scratch_shapes=saved_shapes(pltpu.VMEM)
        + [
            pltpu.VMEM((GROUP, TILE, LANES), F32),
            pltpu.SMEM((LEN_BLK,), jnp.int32),
            pltpu.SemaphoreType.DMA((6,)),
        ],
        compiler_params=params(32),
        name="forward_layer",
    )(lens, own, got_rows, w_proj, gain_in)


def backward_layer(lens, own, got_rows, got_grads, saved, w_proj, w_out, gain_in, gain_attn):
    return pl.pallas_call(
        backward_kernel,
        out_shape=(
            pltpu.HBM((PEERS, BLOCK, D), BF),
            pltpu.HBM((4 * PAIRS, ROWS, LANES), BF),
            pltpu.HBM((ROWS, D), BF),
            pltpu.HBM((ROWS, D), BF),
        ),
        in_specs=[SMEM_SPEC] * 2 + [ANY_SPEC] * 10 + [VMEM_SPEC] * 2,
        out_specs=(VMEM_SPEC, HBM_SPEC, HBM_SPEC, HBM_SPEC),
        scratch_shapes=[
            pltpu.VMEM((PAIRS, ROWS, LANES), BF),
            pltpu.VMEM((4 * PAIRS, ROWS, LANES), BF),
            pltpu.VMEM((ROWS, D), BF),
            pltpu.VMEM((ROWS, D), BF),
            pltpu.VMEM((GROUP, LANES, TILE), F32),
            pltpu.VMEM((PAIRS, LANES, ROWS), BF),
            pltpu.VMEM((GROUP, ROWS, LANES), F32),
            pltpu.VMEM((GROUP, ROWS, LANES), F32),
            pltpu.SMEM((LEN_BLK,), jnp.int32),
            pltpu.SemaphoreType.DMA((3, TILES)),
            pltpu.SemaphoreType.DMA((11,)),
            pltpu.VMEM((PAIRS, ROWS, LANES), BF),
        ]
        + saved_shapes(pltpu.VMEM)[:5]
        + [pltpu.VMEM((D, 4 * D), BF), pltpu.VMEM((D, D), BF)]
        + [pltpu.VMEM((PEERS, BLOCK, D), BF)] * 2,
        compiler_params=params(44),
        name="backward_layer",
    )(lens, own, got_rows, got_grads, *saved[:6], w_proj, w_out, gain_in, gain_attn)


def gradient_terms(own, d_hidden, scaled, mixed, cot):
    half = struct((HALF, LANES), BF)
    quarter = pltpu.HBM((HALF // 2, LANES), BF)
    return pl.pallas_call(
        terms_kernel,
        out_shape=(half, quarter, quarter),
        in_specs=[SMEM_SPEC] + [HBM_SPEC] * 4,
        out_specs=(VMEM_SPEC,) * 3,
        scratch_shapes=[
            pltpu.VMEM((4 * PAIRS, ROWS, LANES), BF),
            pltpu.VMEM((ROWS, D), BF),
            pltpu.VMEM((ROWS, D), BF),
            pltpu.VMEM((ROWS, D), BF),
            pltpu.VMEM((D, ROWS), BF),
            pltpu.SemaphoreType.DMA((11,)),
        ],
        compiler_params=params(40),
        cost_estimate=pl.CostEstimate(
            flops=10 * ROWS * D * D, transcendentals=0, bytes_accessed=10 * MIB
        ),
        name="gradient_terms",
    )(own, d_hidden, scaled, mixed, cot)


def in_hbm(array):
    return pltpu.with_memory_space_constraint(array, pltpu.HBM)


def per_device(events, cotangent, lengths, gain_in, w_proj, gain_attn, w_out):
    own = lax.axis_index(("chip", "core")).astype(jnp.int32).reshape(1)
    lens = lengths[0]
    got_rows = lax.all_to_all(send_blocks(lens, own, events), ("chip", "core"), 0, 0, tiled=True)
    got_grads = lax.all_to_all(send_blocks(lens, own, cotangent), ("chip", "core"), 0, 0, tiled=True)
    gain_in = gain_in.reshape(1, D)
    gain_attn = gain_attn.reshape(1, D)
    saved = [in_hbm(x) for x in forward_layer(lens, own, got_rows, w_proj, gain_in)]
    send_back, *kept = backward_layer(
        lens, own, got_rows, got_grads, saved, w_proj, in_hbm(w_out), gain_in, gain_attn
    )
    came_back = lax.all_to_all(send_back, ("chip", "core"), 0, 0, tiled=True)
    d_hidden, mixed, cot = (in_hbm(x) for x in kept)
    keep, *send = gradient_terms(own, d_hidden, saved[6], mixed, cot)
    swap = [(0, 1), (1, 0)]
    send[0], came_back = lax.optimization_barrier((send[0], came_back))
    other = jnp.concatenate([lax.ppermute(part, "core", swap) for part in send])
    chip_sum = (keep.astype(F32) + other.astype(F32)).astype(BF)
    parts = lax.all_to_all(chip_sum.reshape(64, PART, LANES), ("grp", "chip"), 0, 0, tiled=True)
    total = (jnp.sum(parts.astype(F32), axis=0) * (1.0 / DEVICES)).astype(BF)
    copies = jnp.broadcast_to(total[None], (64, PART, LANES))
    mine = lax.all_to_all(copies, ("grp", "chip"), 0, 0, tiled=True).reshape(HALF, LANES)
    d_rows = pl.pallas_call(
        home_kernel,
        out_shape=struct((LOCAL, BLOCK, D), BF),
        in_specs=[SMEM_SPEC, SMEM_SPEC, VMEM_SPEC],
        out_specs=VMEM_SPEC,
        name="take_home",
    )(lens, own, came_back)
    mine, d_rows = lax.optimization_barrier((mine, d_rows))
    others = lax.ppermute(mine, "core", swap)
    grads = (struct((D, 4 * D), F32), struct((D, D), F32))
    scratch = [pltpu.VMEM((10, D, LANES), F32), pltpu.SemaphoreType.DMA((10,))]
    sums = (2, D, LANES)
    grad_proj, grad_out, mine_sums = pl.pallas_call(
        spread_mine,
        out_shape=grads + (struct(sums, F32),),
        in_specs=[SMEM_SPEC, VMEM_SPEC, VMEM_SPEC, VMEM_SPEC],
        out_specs=(ANY_SPEC, ANY_SPEC, VMEM_SPEC),
        scratch_shapes=scratch,
        compiler_params=params(24),
        name="spread_mine",
    )(own, mine, w_proj, w_out)
    gain = struct((1, D), F32)
    grad_proj, grad_out, grad_in, grad_attn = pl.pallas_call(
        spread_other,
        out_shape=grads + (gain, gain),
        in_specs=[SMEM_SPEC] + [VMEM_SPEC] * 6 + [ANY_SPEC] * 2,
        out_specs=(ANY_SPEC, ANY_SPEC, VMEM_SPEC, VMEM_SPEC),
        scratch_shapes=scratch[:1] + [pltpu.VMEM(sums, F32)] + scratch[1:],
        input_output_aliases={7: 0, 8: 1},
        compiler_params=params(24),
        name="spread_other",
    )(own, others, w_proj, w_out, gain_in, gain_attn, mine_sums, grad_proj, grad_out)
    return (
        d_rows.reshape(1, LOCAL * BLOCK, D),
        grad_proj,
        grad_out,
        grad_in.reshape(D),
        grad_attn.reshape(D),
    )


def solution(mesh):
    fine = Mesh(mesh.devices.reshape(8, 8, 2), ("grp", "chip", "core"))
    rows = P("grp", ("chip", "core"), None)
    return jax.shard_map(
        per_device,
        mesh=fine,
        in_specs=(rows, rows, P("grp", None), P(), P(), P(), P()),
        out_specs=(rows, P(), P(), P(), P()),
        check_vma=False,
    )
```

```python
import jax
import jax.numpy as jnp
from jax import lax
from jax.experimental import pallas as pl
from jax.experimental.pallas import tpu as pltpu
from jax.sharding import Mesh, PartitionSpec as P

D = 512
HEADS = 8
BLOCK = 64
LEN_BLK = 16
SEQ = 16
PEERS = 16
LOCAL = 8
TILE = 256
TILES = 4
ROWS = 1024
LANES = 128
PAIRS = 4
PART = 80
HALF = 64 * PART
EPS = 1e-06
DEVICES = 128
BF = jnp.bfloat16
F32 = jnp.float32
MIB = 1024 * 1024

SMEM_SPEC = pl.BlockSpec(memory_space=pltpu.SMEM)
ANY_SPEC = pl.BlockSpec(memory_space=pl.ANY)
VMEM_SPEC = pl.BlockSpec(memory_space=pltpu.VMEM)
HBM_SPEC = pl.BlockSpec(memory_space=pltpu.HBM)


def dot(left, right):
    return lax.dot_general(left, right, (((1,), (0,)), ((), ())), preferred_element_type=F32)


def dot_cols(left, right):
    return lax.dot_general(left, right, (((1,), (1,)), ((), ())), preferred_element_type=F32)


def dot_rows(left, right):
    return lax.dot_general(left, right, (((0,), (0,)), ((), ())), preferred_element_type=F32)


def packing(len_ref):
    starts, sizes, ranks = [], [], []
    start = jnp.int32(0)
    rank = jnp.int32(0)
    held = jnp.int32(0)
    for i in range(SEQ):
        size = len_ref[i]
        fresh = held + size > LEN_BLK
        rank = jnp.where(fresh, rank + 1, rank)
        held = jnp.where(fresh, size, held + size)
        starts.append(start)
        sizes.append(size)
        ranks.append(rank)
        start = start + size
    return starts, sizes, ranks


def owners(len_ref, own):
    starts, _, ranks = packing(len_ref)
    found = []
    for k in range(LOCAL):
        block = own + PEERS * k
        owner = ranks[0]
        for i in range(1, SEQ):
            owner = jnp.where(starts[i] <= block, ranks[i], owner)
        found.append(owner)
    return found


def holdings(len_ref, own):
    starts, sizes, ranks = packing(len_ref)
    first = jnp.int32(LEN_BLK * LOCAL)
    count = jnp.int32(0)
    for i in range(SEQ):
        mine = ranks[i] == own
        first = jnp.where(mine, jnp.minimum(first, starts[i]), first)
        count = jnp.where(mine, count + sizes[i], count)
    return starts, sizes, ranks, first, count


def history_starts(hist_ref, own, starts, sizes, ranks, first):
    for j in range(LEN_BLK):
        hist_ref[j] = j
    for i in range(SEQ):

        @pl.when(ranks[i] == own)
        def _(i=i):
            begin = starts[i] - first

            def put(j, carry):
                hist_ref[j] = begin
                return carry

            lax.fori_loop(begin, begin + sizes[i], put, 0)


def send_kernel(len_ref, own_ref, rows_ref, out_ref):
    owner = owners(len_ref, own_ref[0])
    for k in range(LOCAL):
        out_ref[owner[k]] = rows_ref[k]


def home_kernel(len_ref, own_ref, back_ref, out_ref):
    owner = owners(len_ref, own_ref[0])
    for k in range(LOCAL):
        out_ref[k] = back_ref[owner[k]]


def tile_rows(ref, t, first, count):
    slots = [(first + t * 4 + b) & (PEERS - 1) for b in range(4)]
    tile = jnp.concatenate([ref[slot] for slot in slots], axis=0).astype(F32)
    place = lax.broadcasted_iota(jnp.int32, (TILE, D), 0) + t * TILE
    return jnp.where(place < count * BLOCK, tile, 0.0)


def normed_rows(values):
    centred = values - jnp.mean(values, axis=-1, keepdims=True)
    rstd = lax.rsqrt(jnp.mean(centred * centred, axis=-1, keepdims=True) + EPS)
    return centred * rstd, rstd


def head_masks():
    lane = lax.broadcasted_iota(jnp.int32, (1, LANES), 1)
    low = (lane < 64).astype(F32).astype(BF)
    high = (lane >= 64).astype(F32).astype(BF)
    return low, high


GROUP = 4


def rows_at(t):
    return pl.ds(pl.multiple_of(t * TILE, TILE), TILE)


def block_starts(hist_ref, t, shape, dim):
    place = lax.broadcasted_iota(jnp.int32, shape, dim)
    begin = jnp.full(shape, hist_ref[4 * t], jnp.int32)
    for b in range(1, 4):
        begin = jnp.where(place >= b * BLOCK, hist_ref[4 * t + b], begin)
    return begin * BLOCK


def key_tiles(hist_ref, i):
    low = hist_ref[4 * i] // 4
    clear = jnp.minimum((hist_ref[4 * i + 3] + 3) // 4, i)
    return low, jnp.maximum(clear, low)


def forward_kernel(
    len_ref,
    own_ref,
    got_ref,
    w_ref,
    gain_ref,
    attn_ref,
    upper_out,
    values_out,
    query_out,
    keys_out,
    slope_out,
    scaled_out,
    upper_ref,
    values_ref,
    query_ref,
    keys_ref,
    slope_ref,
    scaled_ref,
    acc_ref,
    hist_ref,
    save_sems,
):
    own = own_ref[0]
    starts, sizes, ranks, first, count = holdings(len_ref, own)
    history_starts(hist_ref, own, starts, sizes, ranks, first)
    live = (count + 3) // 4

    def project(t, carry):
        normed, _ = normed_rows(tile_rows(got_ref, t, first, count))
        scaled = (normed * gain_ref[...]).astype(BF)
        rows = rows_at(t)
        scaled_ref[rows, :] = scaled
        for quarter in range(4):
            half = 0.5 * dot(scaled, w_ref[:, quarter * D : (quarter + 1) * D])
            swing = jnp.tanh(half)
            active = half + half * swing
            slope = ((0.5 + 0.5 * swing) * (1.0 + (half - half * swing))).astype(BF)
            if quarter == 0:
                upper_ref[rows, :] = active.astype(BF)
            if quarter == 2:
                active = active * 0.0625
            active = active.astype(BF)
            for p in range(PAIRS):
                lanes = slice(p * LANES, (p + 1) * LANES)
                slope_ref[quarter * PAIRS + p, rows, :] = slope[:, lanes]
                if quarter:
                    ref = (None, values_ref, query_ref, keys_ref)[quarter]
                    ref[p, rows, :] = active[:, lanes]
        return carry

    lax.fori_loop(0, live, project, 0)

    def clear(t, carry):
        scaled_ref[rows_at(t), :] = jnp.zeros((TILE, D), BF)
        return carry

    lax.fori_loop(live, TILES, clear, 0)

    saves = [
        pltpu.make_async_copy(src, dst, save_sems.at[n])
        for n, (src, dst) in enumerate(
            (
                (upper_ref, upper_out),
                (values_ref, values_out),
                (query_ref, query_out),
                (keys_ref, keys_out),
                (slope_ref, slope_out),
                (scaled_ref, scaled_out),
            )
        )
    ]
    for save in saves:
        save.start()

    masks = head_masks()

    def group(g, carry):
        def query_tile(i, carry):
            acc_ref[...] = jnp.zeros((GROUP, TILE, LANES), F32)

            def step(j, masked):
                if masked:
                    shape = (TILE, TILE)
                    col = lax.broadcasted_iota(jnp.int32, shape, 1) + j * TILE
                    row = lax.broadcasted_iota(jnp.int32, shape, 0) + i * TILE
                    allowed = (col <= row) & (col >= block_starts(hist_ref, i, shape, 0))
                for n in range(GROUP):
                    p = g * GROUP + n
                    query = query_ref[p, rows_at(i), :]
                    keys = keys_ref[p, rows_at(j), :]
                    values = values_ref[p, rows_at(j), :]
                    total = acc_ref[n]
                    for mask in masks:
                        half = dot_cols(query, keys * mask)
                        weights = half + half * jnp.tanh(half)
                        if masked:
                            weights = jnp.where(allowed, weights, 0.0)
                        total += dot(weights.astype(BF), values * mask)
                    acc_ref[n] = total

            low, clear_from = key_tiles(hist_ref, i)

            def masked_step(j, carry):
                step(j, True)
                return carry

            def clear_step(j, carry):
                step(j, False)
                return carry

            lax.fori_loop(low, clear_from, masked_step, 0)
            lax.fori_loop(clear_from, i, clear_step, 0)
            step(i, True)
            for n in range(GROUP):
                attn_ref[g * GROUP + n, rows_at(i), :] = acc_ref[n].astype(BF)
            return carry

        return lax.fori_loop(0, live, query_tile, carry)

    lax.fori_loop(0, PAIRS // GROUP, group, 0)
    for save in saves:
        save.wait()


def backward_kernel(
    len_ref,
    own_ref,
    got_in,
    grads_in,
    attn_in,
    upper_in,
    values_in,
    query_in,
    keys_in,
    slope_in,
    w_in,
    w_out_in,
    gain_in_ref,
    gain_attn_ref,
    back_ref,
    d_hidden_out,
    mixed_out,
    cot_out,
    d_attn_ref,
    d_hidden_ref,
    mixed_ref,
    cot_rows_ref,
    d_query_ref,
    keys_t_ref,
    d_keys_ref,
    d_values_ref,
    hist_ref,
    tile_sems,
    load_sems,
    attn_ref,
    upper_ref,
    values_ref,
    query_ref,
    keys_ref,
    slope_ref,
    w_ref,
    w_out_ref,
    got_ref,
    grads_ref,
):
    own = own_ref[0]
    load_grads = pltpu.make_async_copy(grads_in, grads_ref, load_sems.at[9])
    load_grads.start()
    load_got = pltpu.make_async_copy(got_in, got_ref, load_sems.at[10])
    starts, sizes, ranks, first, count = holdings(len_ref, own)
    live = (count + 3) // 4
    early = pl.ds(0, PAIRS)
    late = pl.ds(PAIRS, 3 * PAIRS)

    def tile_loads(t):
        rows = rows_at(t)
        return [
            pltpu.make_async_copy(
                attn_in.at[:, rows], attn_ref.at[:, rows], tile_sems.at[0, t]
            ),
            pltpu.make_async_copy(upper_in.at[rows], upper_ref.at[rows], tile_sems.at[1, t]),
            pltpu.make_async_copy(
                slope_in.at[early, rows], slope_ref.at[early, rows], tile_sems.at[2, t]
            ),
        ]

    loads = [
        pltpu.make_async_copy(src, dst, load_sems.at[n])
        for n, (src, dst) in enumerate(
            (
                (w_out_in, w_out_ref),
                (keys_in, keys_ref),
                (query_in, query_ref),
                (values_in, values_ref),
                (slope_in.at[late], slope_ref.at[late]),
                (w_in, w_ref),
            )
        )
    ]
    loads[0].start()

    def request(t, carry):
        for load in tile_loads(t):
            load.start()
        return carry

    lax.fori_loop(0, live, request, 0)
    for load in loads[1:]:
        load.start()
    load_got.start()
    history_starts(hist_ref, own, starts, sizes, ranks, first)
    loads[0].wait()
    load_grads.wait()

    def middle(t, carry):
        rows = rows_at(t)
        for load in tile_loads(t):
            load.wait()
        attn = jnp.concatenate([attn_ref[p, rows, :] for p in range(PAIRS)], axis=1)
        normed, rstd = normed_rows(attn.astype(F32))
        upper = upper_ref[rows, :].astype(F32)
        cot = tile_rows(grads_ref, t, first, count).astype(BF)
        d_mixed = dot_cols(cot, w_out_ref[...])
        gained = normed * gain_attn_ref[...]
        mixed_ref[rows, :] = (gained * upper).astype(BF)
        cot_rows_ref[rows, :] = cot
        d_upper = d_mixed * gained
        pull = d_mixed * upper
        pull = pull * gain_attn_ref[...]
        d_attn = rstd * (
            pull
            - jnp.mean(pull, axis=-1, keepdims=True)
            - normed * jnp.mean(pull * normed, axis=-1, keepdims=True)
        )
        for p in range(PAIRS):
            lanes = slice(p * LANES, (p + 1) * LANES)
            d_attn_ref[p, rows, :] = d_attn[:, lanes].astype(BF)
            slope = slope_ref[p, rows, :].astype(F32)
            d_hidden_ref[p, rows, :] = (d_upper[:, lanes] * slope).astype(BF)
        return carry

    lax.fori_loop(0, live, middle, 0)

    def clear(t, carry):
        d_hidden_ref[:, rows_at(t), :] = jnp.zeros((4 * PAIRS, TILE, LANES), BF)
        mixed_ref[rows_at(t), :] = jnp.zeros((TILE, D), BF)
        cot_rows_ref[rows_at(t), :] = jnp.zeros((TILE, D), BF)
        return carry

    lax.fori_loop(live, TILES, clear, 0)
    saves = [
        pltpu.make_async_copy(mixed_ref, mixed_out, load_sems.at[7]),
        pltpu.make_async_copy(cot_rows_ref, cot_out, load_sems.at[8]),
    ]
    for save in saves:
        save.start()

    masks = head_masks()
    for load in loads[1:5]:
        load.wait()

    def turn(t, carry):
        for p in range(PAIRS):
            keys_t_ref[p, :, rows_at(t)] = keys_ref[p, rows_at(t), :].T
        return carry

    lax.fori_loop(0, live, turn, 0)

    def group(g, carry):
        d_keys_ref[...] = jnp.zeros((GROUP, ROWS, LANES), F32)
        d_values_ref[...] = jnp.zeros((GROUP, ROWS, LANES), F32)

        def query_tile(i, carry):
            d_query_ref[...] = jnp.zeros((GROUP, LANES, TILE), F32)

            def step(j, masked):
                rows = rows_at(j)
                if masked:
                    shape = (TILE, TILE)
                    key_row = lax.broadcasted_iota(jnp.int32, shape, 0) + j * TILE
                    query_row = lax.broadcasted_iota(jnp.int32, shape, 1) + i * TILE
                    allowed = (key_row <= query_row) & (
                        key_row >= block_starts(hist_ref, i, shape, 1)
                    )
                for n in range(GROUP):
                    p = g * GROUP + n
                    query = query_ref[p, rows_at(i), :]
                    d_attn = d_attn_ref[p, rows_at(i), :]
                    keys = keys_ref[p, rows, :]
                    values = values_ref[p, rows, :]
                    d_keys = d_keys_ref[n, rows, :]
                    d_values = d_values_ref[n, rows, :]
                    for h, mask in enumerate(masks):
                        masked_keys = keys * mask
                        half = dot_cols(masked_keys, query)
                        swing = jnp.tanh(half)
                        bend = half * swing
                        weights = half + bend
                        slope = (1.0 + swing) * ((1.0 + half) - bend)
                        grad = dot_cols(values * mask, d_attn) * slope
                        if masked:
                            weights = jnp.where(allowed, weights, 0.0)
                            grad = jnp.where(allowed, grad, 0.0)
                        grad = grad.astype(BF)
                        d_values += dot(weights.astype(BF), d_attn * mask)
                        d_keys += dot(grad, query * mask)
                        head_rows = slice(h * 64, h * 64 + 64)
                        d_query_ref[n, head_rows, :] += dot(keys_t_ref[p, head_rows, rows], grad)
                    d_keys_ref[n, rows, :] = d_keys
                    d_values_ref[n, rows, :] = d_values

            low, clear_from = key_tiles(hist_ref, i)

            def masked_step(j, carry):
                step(j, True)
                return carry

            def clear_step(j, carry):
                step(j, False)
                return carry

            lax.fori_loop(low, clear_from, masked_step, 0)
            lax.fori_loop(clear_from, i, clear_step, 0)
            step(i, True)
            for n in range(GROUP):
                place = 2 * PAIRS + g * GROUP + n
                slope = slope_ref[place, rows_at(i), :].astype(F32)
                d_hidden_ref[place, rows_at(i), :] = (d_query_ref[n].T * 0.0625 * slope).astype(BF)
            return carry

        lax.fori_loop(0, live, query_tile, 0)

        def finish(t, carry):
            rows = rows_at(t)
            for n in range(GROUP):
                for quarter, ref in ((1, d_values_ref), (3, d_keys_ref)):
                    place = quarter * PAIRS + g * GROUP + n
                    slope = slope_ref[place, rows, :].astype(F32)
                    d_hidden_ref[place, rows, :] = (ref[n, rows, :] * slope).astype(BF)
            return carry

        lax.fori_loop(0, live, finish, 0)
        return carry

    lax.fori_loop(0, PAIRS // GROUP, group, 0)

    saves.append(pltpu.make_async_copy(d_hidden_ref, d_hidden_out, load_sems.at[6]))
    saves[-1].start()
    loads[5].wait()
    load_got.wait()

    def final(t, carry):
        rows = rows_at(t)
        normed, rstd = normed_rows(tile_rows(got_ref, t, first, count))
        d_scaled = jnp.zeros((TILE, D), F32)
        for c in range(8):
            part = jnp.concatenate(
                [d_hidden_ref[2 * c, rows, :], d_hidden_ref[2 * c + 1, rows, :]], axis=1
            )
            d_scaled += dot_cols(part, w_ref[:, c * 256 : (c + 1) * 256])
        pull = d_scaled * gain_in_ref[...]
        d_rows = rstd * (
            pull
            - jnp.mean(pull, axis=-1, keepdims=True)
            - normed * jnp.mean(pull * normed, axis=-1, keepdims=True)
        )
        d_rows = (d_rows + cot_rows_ref[rows, :].astype(F32)).astype(BF)
        for b in range(4):
            slot = (first + t * 4 + b) & (PEERS - 1)
            back_ref[slot] = d_rows[b * BLOCK : (b + 1) * BLOCK, :]
        return carry

    lax.fori_loop(0, live, final, 0)

    for save in saves:
        save.wait()


def terms_kernel(
    own_ref,
    d_hidden_in,
    scaled_in,
    mixed_in,
    cot_in,
    keep_ref,
    send_low_ref,
    send_high_ref,
    d_hidden_ref,
    scaled_ref,
    mixed_ref,
    cot_ref,
    turned_ref,
    sems,
):
    core = own_ref[0] & 1
    loads = [
        pltpu.make_async_copy(mixed_in, mixed_ref, sems.at[9]),
        pltpu.make_async_copy(cot_in, cot_ref, sems.at[10]),
        pltpu.make_async_copy(scaled_in, scaled_ref, sems.at[8]),
    ]
    for c in range(8):
        part = pl.ds(2 * c, 2)
        loads.append(
            pltpu.make_async_copy(d_hidden_in.at[part], d_hidden_ref.at[part], sems.at[c])
        )
    for load in loads:
        load.start()

    def put_piece(piece, values):
        half, place = divmod(piece, 10)
        values = values.astype(BF)

        @pl.when(core == half)
        def _():
            keep_ref[place * D : (place + 1) * D, :] = values

        @pl.when(core != half)
        def _():
            send_ref = (send_low_ref, send_high_ref)[place // 5]
            send_ref[place % 5 * D : (place % 5 + 1) * D, :] = values

    loads[0].wait()
    turned_ref[...] = mixed_ref[...].T
    loads[1].wait()
    for c in range(2):
        term = dot(turned_ref[...], cot_ref[:, c * 256 : (c + 1) * 256])
        put_piece(16 + 2 * c, term[:, :LANES])
        put_piece(17 + 2 * c, term[:, LANES:])
    loads[2].wait()
    turned_ref[...] = scaled_ref[...].T
    for c in range(8):
        loads[3 + c].wait()
        part = jnp.concatenate([d_hidden_ref[2 * c], d_hidden_ref[2 * c + 1]], axis=1)
        term = dot(turned_ref[...], part)
        put_piece(2 * c, term[:, :LANES])
        put_piece(2 * c + 1, term[:, LANES:])


def spread_half(half, half_ref, w_ref, w_out_ref, proj_ref, out_ref, wide_ref, sums_ref, sems):
    in_sum = jnp.zeros((D, LANES), F32)
    attn_sum = jnp.zeros((D, LANES), F32)
    for place in range(10):
        piece = half * 10 + place
        part = half_ref[place * D : (place + 1) * D, :].astype(F32)
        wide_ref[place] = part
        if piece < 16:
            lanes = pl.ds(piece * LANES, LANES)
            target = proj_ref.at[:, lanes]
            in_sum += part * w_ref[:, lanes].astype(F32)
        else:
            lanes = pl.ds((piece - 16) * LANES, LANES)
            target = out_ref.at[:, lanes]
            attn_sum += part * w_out_ref[:, lanes].astype(F32)
        pltpu.make_async_copy(wide_ref.at[place], target, sems.at[place]).start()
    sums_ref[0] = in_sum
    sums_ref[1] = attn_sum


def spread_wait(proj_ref, wide_ref, sems):
    for place in range(10):
        target = proj_ref.at[:, pl.ds(place * LANES, LANES)]
        pltpu.make_async_copy(wide_ref.at[place], target, sems.at[place]).wait()


def spread_mine(own_ref, mine_ref, w_ref, w_out_ref, proj_ref, out_ref, sums_ref, wide_ref, sems):
    core = own_ref[0] & 1
    for half in range(2):

        @pl.when(core == half)
        def _(half=half):
            spread_half(
                half, mine_ref, w_ref, w_out_ref, proj_ref, out_ref, wide_ref, sums_ref, sems
            )

    spread_wait(proj_ref, wide_ref, sems)


def spread_other(
    own_ref,
    other_ref,
    w_ref,
    w_out_ref,
    gain_in_ref,
    gain_attn_ref,
    mine_sums_ref,
    proj_in,
    out_in,
    proj_ref,
    out_ref,
    grad_in_ref,
    grad_attn_ref,
    wide_ref,
    sums_ref,
    sems,
):
    core = own_ref[0] & 1
    for half in range(2):

        @pl.when(core != half)
        def _(half=half):
            spread_half(
                half, other_ref, w_ref, w_out_ref, proj_ref, out_ref, wide_ref, sums_ref, sems
            )

    for n, (gain_ref, grad_ref) in enumerate(
        ((gain_in_ref, grad_in_ref), (gain_attn_ref, grad_attn_ref))
    ):
        total = (sums_ref[n] + mine_sums_ref[n]).T
        grad_ref[...] = jnp.sum(total, axis=0, keepdims=True) / gain_ref[...]
    spread_wait(proj_ref, wide_ref, sems)


def struct(shape, dtype):
    return jax.ShapeDtypeStruct(shape, dtype)


def params(mebibytes):
    return pltpu.CompilerParams(vmem_limit_bytes=mebibytes * MIB)


def send_blocks(lens, own, rows):
    return pl.pallas_call(
        send_kernel,
        out_shape=struct((PEERS, BLOCK, D), BF),
        in_specs=[SMEM_SPEC, SMEM_SPEC, VMEM_SPEC],
        out_specs=VMEM_SPEC,
        name="send_blocks",
    )(lens, own, rows.reshape(LOCAL, BLOCK, D))


def saved_shapes(make):
    pairs = make((PAIRS, ROWS, LANES), BF)
    wide = make((ROWS, D), BF)
    return [wide, pairs, pairs, pairs, make((4 * PAIRS, ROWS, LANES), BF), wide]


def forward_layer(lens, own, got_rows, w_proj, gain_in):
    return pl.pallas_call(
        forward_kernel,
        out_shape=[pltpu.HBM((PAIRS, ROWS, LANES), BF)] + saved_shapes(pltpu.HBM),
        in_specs=[SMEM_SPEC, SMEM_SPEC, VMEM_SPEC, VMEM_SPEC, VMEM_SPEC],
        out_specs=[VMEM_SPEC] + [HBM_SPEC] * 6,
        scratch_shapes=saved_shapes(pltpu.VMEM)
        + [
            pltpu.VMEM((GROUP, TILE, LANES), F32),
            pltpu.SMEM((LEN_BLK,), jnp.int32),
            pltpu.SemaphoreType.DMA((6,)),
        ],
        compiler_params=params(32),
        name="forward_layer",
    )(lens, own, got_rows, w_proj, gain_in)


def backward_layer(lens, own, got_rows, got_grads, saved, w_proj, w_out, gain_in, gain_attn):
    return pl.pallas_call(
        backward_kernel,
        out_shape=(
            pltpu.HBM((PEERS, BLOCK, D), BF),
            pltpu.HBM((4 * PAIRS, ROWS, LANES), BF),
            pltpu.HBM((ROWS, D), BF),
            pltpu.HBM((ROWS, D), BF),
        ),
        in_specs=[SMEM_SPEC] * 2 + [ANY_SPEC] * 10 + [VMEM_SPEC] * 2,
        out_specs=(VMEM_SPEC, HBM_SPEC, HBM_SPEC, HBM_SPEC),
        scratch_shapes=[
            pltpu.VMEM((PAIRS, ROWS, LANES), BF),
            pltpu.VMEM((4 * PAIRS, ROWS, LANES), BF),
            pltpu.VMEM((ROWS, D), BF),
            pltpu.VMEM((ROWS, D), BF),
            pltpu.VMEM((GROUP, LANES, TILE), F32),
            pltpu.VMEM((PAIRS, LANES, ROWS), BF),
            pltpu.VMEM((GROUP, ROWS, LANES), F32),
            pltpu.VMEM((GROUP, ROWS, LANES), F32),
            pltpu.SMEM((LEN_BLK,), jnp.int32),
            pltpu.SemaphoreType.DMA((3, TILES)),
            pltpu.SemaphoreType.DMA((11,)),
            pltpu.VMEM((PAIRS, ROWS, LANES), BF),
        ]
        + saved_shapes(pltpu.VMEM)[:5]
        + [pltpu.VMEM((D, 4 * D), BF), pltpu.VMEM((D, D), BF)]
        + [pltpu.VMEM((PEERS, BLOCK, D), BF)] * 2,
        compiler_params=params(44),
        name="backward_layer",
    )(lens, own, got_rows, got_grads, *saved[:6], w_proj, w_out, gain_in, gain_attn)


def gradient_terms(own, d_hidden, scaled, mixed, cot):
    half = struct((HALF, LANES), BF)
    quarter = pltpu.HBM((HALF // 2, LANES), BF)
    return pl.pallas_call(
        terms_kernel,
        out_shape=(half, quarter, quarter),
        in_specs=[SMEM_SPEC] + [HBM_SPEC] * 4,
        out_specs=(VMEM_SPEC,) * 3,
        scratch_shapes=[
            pltpu.VMEM((4 * PAIRS, ROWS, LANES), BF),
            pltpu.VMEM((ROWS, D), BF),
            pltpu.VMEM((ROWS, D), BF),
            pltpu.VMEM((ROWS, D), BF),
            pltpu.VMEM((D, ROWS), BF),
            pltpu.SemaphoreType.DMA((11,)),
        ],
        compiler_params=params(40),
        cost_estimate=pl.CostEstimate(
            flops=10 * ROWS * D * D, transcendentals=0, bytes_accessed=10 * MIB
        ),
        name="gradient_terms",
    )(own, d_hidden, scaled, mixed, cot)


def in_hbm(array):
    return pltpu.with_memory_space_constraint(array, pltpu.HBM)


def per_device(events, cotangent, lengths, gain_in, w_proj, gain_attn, w_out):
    own = lax.axis_index(("chip", "core")).astype(jnp.int32).reshape(1)
    lens = lengths[0]
    got_rows = lax.all_to_all(send_blocks(lens, own, events), ("chip", "core"), 0, 0, tiled=True)
    got_grads = lax.all_to_all(send_blocks(lens, own, cotangent), ("chip", "core"), 0, 0, tiled=True)
    gain_in = gain_in.reshape(1, D)
    gain_attn = gain_attn.reshape(1, D)
    saved = [in_hbm(x) for x in forward_layer(lens, own, got_rows, w_proj, gain_in)]
    send_back, *kept = backward_layer(
        lens, own, got_rows, got_grads, saved, w_proj, in_hbm(w_out), gain_in, gain_attn
    )
    came_back = lax.all_to_all(send_back, ("chip", "core"), 0, 0, tiled=True)
    d_hidden, mixed, cot = (in_hbm(x) for x in kept)
    keep, *send = gradient_terms(own, d_hidden, saved[6], mixed, cot)
    swap = [(0, 1), (1, 0)]
    send[0], came_back = lax.optimization_barrier((send[0], came_back))
    chip_sum = keep
    for n in (1, 0):
        other = lax.ppermute(send[n], "core", swap)
        rows = slice(n * HALF // 2, (n + 1) * HALF // 2)
        pair_sum = (keep[rows].astype(F32) + other.astype(F32)).astype(BF)
        chip_sum = lax.dynamic_update_slice(chip_sum, pair_sum, (n * HALF // 2, 0))
    parts = lax.all_to_all(chip_sum.reshape(64, PART, LANES), ("grp", "chip"), 0, 0, tiled=True)
    total = (jnp.sum(parts.astype(F32), axis=0) * (1.0 / DEVICES)).astype(BF)
    copies = jnp.broadcast_to(total[None], (64, PART, LANES))
    mine = lax.all_to_all(copies, ("grp", "chip"), 0, 0, tiled=True).reshape(HALF, LANES)
    d_rows = pl.pallas_call(
        home_kernel,
        out_shape=struct((LOCAL, BLOCK, D), BF),
        in_specs=[SMEM_SPEC, SMEM_SPEC, VMEM_SPEC],
        out_specs=VMEM_SPEC,
        name="take_home",
    )(lens, own, came_back)
    mine, d_rows = lax.optimization_barrier((mine, d_rows))
    others = lax.ppermute(mine, "core", swap)
    grads = (struct((D, 4 * D), F32), struct((D, D), F32))
    scratch = [pltpu.VMEM((10, D, LANES), F32), pltpu.SemaphoreType.DMA((10,))]
    sums = (2, D, LANES)
    grad_proj, grad_out, mine_sums = pl.pallas_call(
        spread_mine,
        out_shape=grads + (struct(sums, F32),),
        in_specs=[SMEM_SPEC, VMEM_SPEC, VMEM_SPEC, VMEM_SPEC],
        out_specs=(ANY_SPEC, ANY_SPEC, VMEM_SPEC),
        scratch_shapes=scratch,
        compiler_params=params(24),
        name="spread_mine",
    )(own, mine, w_proj, w_out)
    gain = struct((1, D), F32)
    grad_proj, grad_out, grad_in, grad_attn = pl.pallas_call(
        spread_other,
        out_shape=grads + (gain, gain),
        in_specs=[SMEM_SPEC] + [VMEM_SPEC] * 6 + [ANY_SPEC] * 2,
        out_specs=(ANY_SPEC, ANY_SPEC, VMEM_SPEC, VMEM_SPEC),
        scratch_shapes=scratch[:1] + [pltpu.VMEM(sums, F32)] + scratch[1:],
        input_output_aliases={7: 0, 8: 1},
        compiler_params=params(24),
        name="spread_other",
    )(own, others, w_proj, w_out, gain_in, gain_attn, mine_sums, grad_proj, grad_out)
    return (
        d_rows.reshape(1, LOCAL * BLOCK, D),
        grad_proj,
        grad_out,
        grad_in.reshape(D),
        grad_attn.reshape(D),
    )


def solution(mesh):
    fine = Mesh(mesh.devices.reshape(8, 8, 2), ("grp", "chip", "core"))
    rows = P("grp", ("chip", "core"), None)
    return jax.shard_map(
        per_device,
        mesh=fine,
        in_specs=(rows, rows, P("grp", None), P(), P(), P(), P()),
        out_specs=(rows, P(), P(), P(), P()),
        check_vma=False,
    )
```
